32 devices in a mesh: gx: 4 (over z), gy: 4 (over x, core), gz: 2 (over y).
Axes of the slice: x: 2, y: 2, z: 4, core: 2. Of those that a mesh axis runs over, the one named last changes fastest.
Arguments:
- pressure: float32 [128, 128, 256], P('gx', 'gy', 'gz'), may hold values from -2.5 to 2.5
- source: float32 [128, 128, 256], P('gx', 'gy', 'gz'), may hold values from -40 to 40
- saturation: float32 [128, 128, 256], P('gx', 'gy', 'gz'), may hold values from 0.1 to 0.9
- permeability: float32 [128, 128, 256], P('gx', 'gy', 'gz'), may hold values from 0.1 to 10
- compress: float32 [128, 128, 256], P('gx', 'gy', 'gz'), may hold values from 0.1 to 1
- porosity: float32 [128, 128, 256], P('gx', 'gy', 'gz'), may hold values from 0.1 to 0.3
- rock_type: int32 [128, 128, 256], P('gx', 'gy', 'gz'), may hold values from 0 to 7
- well_mask: int32 [128, 128, 256], P('gx', 'gy', 'gz'), may hold values 0 or 1
- oil_factor: float32 [8], replicated, may hold values from 0.3 to 3
Outputs:
- pressure_new: float32 [128, 128, 256], P('gx', 'gy', 'gz')
- residual_new: float32 [128, 128, 256], P('gx', 'gy', 'gz')
- saturation_new: float32 [128, 128, 256], P('gx', 'gy', 'gz')
The draws below stay inside these ranges and needn't reach their ends.
All inputs are finite; a program needn't handle non-finite values. No bound on the sum of `well_mask` on one device may be relied on, other than what follows from the above.
Results may differ from the reference program's by a relative error of at most 0.0003.
Values sent between devices are 32-bit elements; how exact they have to be, the bound alone decides.
No kernel may reach another device: no remote copies, remote signals or barrier semaphores. Data moves between devices by JAX's collectives and lax.ppermute only.
A program may use at most 64 MiB of HBM per device.

```python
import math
import jax
import jax.numpy as jnp
from jax import lax

CX = 32
CY = 32
CZ = 128
INTERSECTION = 8
NEWTON = 3
ROCKS = 8
NX = 128
NY = 128
NZ = 256
N_GX = 4
N_GY = 4
N_GZ = 2


def draw_source(key, part):
    key_base, key_x, key_y = jax.random.split(jax.random.fold_in(key, 11), 3)
    scale_x = 0.1 * jnp.exp(jax.random.uniform(key_x, (NX,), jnp.float32, 0.0, math.log(10.0)))
    scale_y = 0.1 * jnp.exp(jax.random.uniform(key_y, (NY,), jnp.float32, 0.0, math.log(10.0)))
    base_vals = jnp.clip(jax.random.normal(key_base, (NX, NY, NZ), jnp.float32), -4.0, 4.0)
    return base_vals * (scale_x[:, None, None] * 10.0) * scale_y[None, :, None]


def touch_ends(values, stream_key, low, top_value):
    shape = values.shape
    place = [jax.random.randint(jax.random.fold_in(stream_key, axis), (), 0, shape[axis]) for axis in range(len(shape))]
    values = values.at[tuple(place)].set(low)
    longest = shape.index(max(shape))
    place[longest] = (place[longest] + 1) % shape[longest]
    return values.at[tuple(place)].set(top_value)


def steps_of(rng, dims, cuts, low, high):
    gain = 1.0
    for axis_at, blocks in cuts:
        steps = jax.random.uniform(jax.random.fold_in(jax.random.fold_in(rng, 6), axis_at), (blocks,), jnp.float32, low / len(cuts), high / len(cuts))
        gain = gain * jnp.repeat(jnp.exp(steps), dims[axis_at] // blocks).reshape((-1,) + (1,) * (len(dims) - 1 - axis_at))
    return gain


def normal_values(rng, extent, deviation, limit, shards=(), kind=jnp.bfloat16):
    values = jax.random.normal(rng, extent, jnp.float32) * deviation
    if len(shards) > 0:
        values = steps_of(rng, extent, shards, -0.22, 0.18) * values
    return jnp.clip(values, min=-limit, max=limit).astype(kind)


def setup_inputs(seed: int = 0) -> dict:
    keys = jax.random.split(jax.random.key(seed), 10)
    pressure = normal_values(keys[0], (NX, NY, NZ), 0.3, 2.5, ((0, 4), (1, 4), (2, 2)), jnp.float32)
    source = draw_source(jax.random.fold_in(keys[9], 71), 0)
    saturation = jnp.clip(0.1 + 0.79999997 * jax.random.uniform(keys[2], (NX, NY, NZ), jnp.float32) ** steps_of(keys[2], (NX, NY, NZ), ((0, 4), (1, 4), (2, 2)), -0.2, 0.2), 0.1, 0.9)
    permeability = jnp.clip(jnp.exp(math.log(10.0) - 4.6051702 * jax.random.uniform(keys[3], (NX, NY, NZ), jnp.float32) ** steps_of(keys[3], (NX, NY, NZ), ((0, 4), (1, 4), (2, 2)), -0.2, 0.2)), 0.1, 10.0)
    compress = jnp.clip(jnp.exp(math.log(1.0) - 2.3025851 * jax.random.uniform(keys[4], (NX, NY, NZ), jnp.float32) ** steps_of(keys[4], (NX, NY, NZ), ((0, 4), (1, 4), (2, 2)), -0.2, 0.2)), 0.1, 1.0)
    porosity = jnp.clip(0.1 + 0.20000001043081284 * jax.random.uniform(keys[5], (NX, NY, NZ), jnp.float32) ** steps_of(keys[5], (NX, NY, NZ), ((0, 4), (1, 4), (2, 2)), -0.2, 0.2), 0.1, 0.3)
    rock_type = touch_ends(jax.random.randint(keys[6], (NX, NY, NZ), 0, ROCKS), jax.random.fold_in(keys[6], 1), 0, ROCKS - 1).astype(jnp.int32)
    well_mask = touch_ends((jax.random.randint(keys[7], (NX, NY, NZ), 0, 32) < 1).astype(jnp.int32), jax.random.fold_in(keys[7], 1), 0, 1)
    oil_factor = jnp.clip(jnp.exp(jax.random.uniform(keys[8], (ROCKS,), jnp.float32, math.log(0.3), math.log(3.0))), 0.3, 3.0)
    return dict(pressure=pressure, source=source, saturation=saturation, permeability=permeability, compress=compress, porosity=porosity, rock_type=rock_type, well_mask=well_mask, oil_factor=oil_factor)


WELL_INDEX = 4.0
INJECT_RATE = 2.0
TIME_STEP = 0.05

def sine_basis(length):
    points = jnp.arange(length, dtype=jnp.int32) + 1
    product = points[:, None] * points[None, :] % (2 * (length + 1))
    angles = product.astype(jnp.float32) * (math.pi / (length + 1))
    sine_table = math.sqrt(2.0 / (length + 1)) * jnp.sin(angles)
    eigen_vals = 2.0 - 2.0 * jnp.cos(points.astype(jnp.float32) * (math.pi / (length + 1)))
    return (sine_table, eigen_vals)

def solve_box(box_field):
    basis_x, eigen_x = sine_basis(box_field.shape[0])
    basis_y, eigen_y = sine_basis(box_field.shape[1])
    basis_z, eigen_z = sine_basis(box_field.shape[2])
    precise = lax.Precision.HIGHEST
    spectral = jnp.einsum('ai,ijk->ajk', basis_x, box_field, precision=precise)
    spectral = jnp.einsum('bj,ajk->abk', basis_y, spectral, precision=precise)
    spectral = jnp.einsum('ck,abk->abc', basis_z, spectral, precision=precise)
    spectral = spectral / (eigen_x[:, None, None] + eigen_y[None, :, None] + eigen_z[None, None, :])
    spectral = jnp.einsum('ai,ijk->ajk', basis_x, spectral, precision=precise)
    spectral = jnp.einsum('bj,ajk->abk', basis_y, spectral, precision=precise)
    spectral = jnp.einsum('ck,abk->abc', basis_z, spectral, precision=precise)
    return spectral

def fractional(sat_vals, oil_coef):
    water_mob = sat_vals * sat_vals
    divisor = water_mob + oil_coef * (1.0 - sat_vals) * (1.0 - sat_vals)
    return (water_mob / divisor, 2.0 * oil_coef * sat_vals * (1.0 - sat_vals) / (divisor * divisor))

def neighbour(field_vals, along, offset):
    if along < 2:
        return jnp.roll(field_vals, -offset, along)
    zero_plane = jnp.zeros_like(field_vals[:, :, :1])
    if offset == 1:
        return jnp.concatenate([field_vals[:, :, 1:], zero_plane], axis=2)
    return jnp.concatenate([zero_plane, field_vals[:, :, :-1]], axis=2)

def harmonic(lower_mob, upper_mob):
    return 2.0 * lower_mob * upper_mob / (lower_mob + upper_mob)

def transmissibility(mobility):
    trans_x = harmonic(mobility, neighbour(mobility, 0, 1))
    trans_y = harmonic(mobility, neighbour(mobility, 1, 1))
    inner_z = harmonic(mobility[:, :, :-1], mobility[:, :, 1:])
    trans_z = jnp.concatenate([inner_z, jnp.zeros_like(mobility[:, :, :1])], axis=2)
    return (trans_x, trans_y, trans_z)

def face_of(face_arr, along, offset):
    if offset == 1:
        return face_arr
    return neighbour(face_arr, along, -1)

def operate(field_vals, trans_all, diag_coef):
    result = diag_coef * field_vals
    for along in range(3):
        for offset in (1, -1):
            result = result + face_of(trans_all[along], along, offset) * (field_vals - neighbour(field_vals, along, offset))
    return result

def precondition(residual, mobility):
    padded = jnp.pad(residual, ((INTERSECTION, INTERSECTION), (INTERSECTION, INTERSECTION), (0, 0)), mode='wrap')
    padded = jnp.pad(padded, ((0, 0), (0, 0), (INTERSECTION, INTERSECTION)))
    brick_count = N_GX * N_GY * N_GZ

    def one_brick(brick_id):
        index_x = brick_id // (N_GY * N_GZ)
        index_y = brick_id // N_GZ % N_GY
        index_z = brick_id % N_GZ
        starts = (index_x * CX, index_y * CY, index_z * CZ)
        box_field = lax.dynamic_slice(padded, starts, (CX + 2 * INTERSECTION, CY + 2 * INTERSECTION, CZ + 2 * INTERSECTION))
        local_mob = lax.dynamic_slice(mobility, starts, (CX, CY, CZ))
        solved = solve_box(box_field)
        return solved[INTERSECTION:INTERSECTION + CX, INTERSECTION:INTERSECTION + CY, INTERSECTION:INTERSECTION + CZ] / jnp.mean(local_mob)
    blocks = lax.map(one_brick, jnp.arange(brick_count, dtype=jnp.int32))
    blocks = blocks.reshape(N_GX, N_GY, N_GZ, CX, CY, CZ).transpose(0, 3, 1, 4, 2, 5)
    return blocks.reshape(NX, NY, NZ)

def reference(pressure, source, saturation, permeability, compress, porosity, rock_type, well_mask, oil_factor):
    oil_coef = oil_factor[rock_type]
    mobility = permeability * (saturation * saturation + oil_coef * (1.0 - saturation) * (1.0 - saturation))
    well_flag = well_mask.astype(jnp.float32)
    trans_all = transmissibility(mobility)
    diag_coef = compress + WELL_INDEX * well_flag * mobility
    residual = source - operate(pressure, trans_all, diag_coef)
    direction = precondition(residual, mobility)
    image_vec = operate(direction, trans_all, diag_coef)
    step_len = jnp.sum(residual * direction) / jnp.sum(direction * image_vec)
    pressure_new = pressure + step_len * direction
    residual_new = residual - step_len * image_vec
    storage_rate = porosity / TIME_STEP
    inject = INJECT_RATE * well_flag
    current = saturation
    for sweep_index in range(NEWTON):
        flow_frac, slope_val = fractional(current, oil_coef)
        balance = storage_rate * (current - saturation) - inject
        outflow = jnp.zeros_like(current)
        for along in range(3):
            for offset in (1, -1):
                face_flux = face_of(trans_all[along], along, offset) * (pressure_new - neighbour(pressure_new, along, offset))
                balance = balance + jnp.maximum(face_flux, 0.0) * flow_frac + jnp.minimum(face_flux, 0.0) * neighbour(flow_frac, along, offset)
                outflow = outflow + jnp.maximum(face_flux, 0.0)
        current = current - balance / (storage_rate + outflow * jnp.abs(slope_val))
    return (pressure_new, residual_new, current)
```

```python
import functools
import math

import jax
import jax.numpy as jnp
import numpy as np
from jax import lax
from jax.experimental import pallas as pl
from jax.experimental.pallas import tpu as pltpu
from jax.sharding import PartitionSpec as P

INTERSECTION = 8
NEWTON = 3

WELL_INDEX = 4.0
INJECT_RATE = 2.0
TIME_STEP = 0.05

AXES = ("gx", "gy", "gz")
F32 = jnp.float32
HIGH = lax.Precision.HIGHEST
MSG_ROWS = 16


def sine_basis(length):
    points = np.arange(length) + 1
    angles = np.outer(points, points) % (2 * (length + 1)) * (math.pi / (length + 1))
    table = math.sqrt(2.0 / (length + 1)) * np.sin(angles)
    eigen = 2.0 - 2.0 * np.cos(points * (math.pi / (length + 1)))
    return table, eigen


def sweep_factors(count, eigen_y, eigen_z):
    shift = 2.0 + eigen_y[:, None] + eigen_z[None, :]
    factors = []
    last = np.zeros_like(shift)
    for _ in range(count):
        last = 1.0 / (shift - last)
        factors.append(last)
    return np.stack(factors), 1.0 / (1.0 - last * last)


def pairs(count, periodic, parity):
    if periodic and count % 2:
        step = 1 if parity == 0 else -1
        return [(i, (i + step) % count) for i in range(count)]
    out = []
    for i in range(parity, count, 2):
        j = i + 1
        if periodic:
            j = j % count
        if j < count:
            out += [(i, j), (j, i)]
    return out


def harmonic(one, two):
    return 2.0 * one * two / (one + two)


def dot(one, two, dims=((1,), (0,))):
    return lax.dot_general(
        one, two, (dims, ((), ())), precision=HIGH, preferred_element_type=F32
    )


def rows_of(shape):
    return lax.broadcasted_iota(jnp.int32, shape, 0)


def lanes_of(shape):
    return lax.broadcasted_iota(jnp.int32, shape, 1)


def back(value, axis):
    return pltpu.roll(value, value.shape[axis] - 1, axis)


def ahead(value, axis):
    return pltpu.roll(value, 1, axis)


class Plan:
    def __init__(self, nx, ny, nz, counts):
        self.nx, self.ny, self.nz = nx, ny, nz
        self.counts = counts
        self.z_msgs = [q for q in (0, 1) if pairs(counts["gz"], False, q)]

    def perm(self, axis, which):
        return pairs(self.counts[axis], axis != "gz", which)

    def high(self, axis, which):
        if axis != "gz" and self.counts[axis] % 2:
            return (which == 0, which == 1)
        up = (lax.axis_index(axis) % 2) == which
        return (up, up)


def call(kernel, outs, args, scratch=(), aliases=None, smem=(), limit=28):
    vmem = pl.BlockSpec(memory_space=pltpu.VMEM)
    return pl.pallas_call(
        kernel,
        out_shape=[jax.ShapeDtypeStruct(s, F32) for s in outs],
        in_specs=[
            pl.BlockSpec(memory_space=pltpu.SMEM) if k in smem else vmem
            for k in range(len(args))
        ],
        out_specs=[vmem] * len(outs),
        scratch_shapes=[pltpu.VMEM(s, F32) for s in scratch],
        input_output_aliases=aliases or {},
        compiler_params=pltpu.CompilerParams(vmem_limit_bytes=limit << 20),
    )(*args)


def side(plan, axis, ref_a, ref_b, high):
    a_high = plan.high(axis, 0)[1]
    if high:
        return jnp.where(a_high, ref_a, ref_b)
    return jnp.where(a_high, ref_b, ref_a)


def pack_x(plan, ref, out_a, out_b):
    last = plan.nx - 1
    for which, out in ((0, out_a), (1, out_b)):
        out[...] = ref[jnp.where(plan.high("gx", which)[0], last, 0)]


def pack_y(plan, ref, out_a, out_b):
    low, top = ref[:, 0, :], ref[:, plan.ny - 1, :]
    for which, out in ((0, out_a), (1, out_b)):
        out[...] = jnp.where(plan.high("gy", which)[0], top, low)


def pack_z(plan, flat, outs):
    for q, out in zip(plan.z_msgs, outs):
        face = jnp.where(plan.high("gz", q)[0], plan.nz - 1, 0)
        pick = (rows_of((8, plan.nz)) == 0) & (lanes_of((8, plan.nz)) == face)
        out[...] = dot(pick.astype(F32), flat, ((1,), (1,)))


def columns(rows):
    eye = (rows_of((8, 128)) == lanes_of((8, 128))).astype(F32)
    return dot(rows, eye, ((0,), (0,)))


def stack_rows(parts):
    cells = parts[0].shape[1]
    row = rows_of((8, cells))
    out = jnp.zeros((8, cells), F32)
    for k, part in enumerate(parts):
        out = jnp.where(row == k, jnp.broadcast_to(part, (8, cells)), out)
    return out


def z_sides(plan, vals):
    low, top = jnp.zeros_like(vals[0]), jnp.zeros_like(vals[0])
    for q, val in zip(plan.z_msgs, vals):
        up = plan.high("gz", q)[1]
        low = low + jnp.where(up, 0.0, val)
        top = top + jnp.where(up, val, 0.0)
    return low, top


def mobility_kernel(
    plan, press, sat, perm, rock, oil, mob, coef, frac, xa, xb, ya, yb, total
):
    kinds = oil.shape[0]

    def layer(i, acc):
        s, kind = sat[i], rock[i]
        c = jnp.full(s.shape, oil[0], F32)
        for k in range(1, kinds):
            c = jnp.where(kind == k, oil[k], c)
        water, rest = s * s, 1.0 - s
        den = water + c * rest * rest
        m = perm[i] * den
        coef[i] = c
        mob[i] = m
        frac[i] = water / den
        return acc + m

    total[...] = lax.fori_loop(
        0, plan.nx, layer, jnp.zeros((plan.ny, plan.nz), F32), unroll=2
    )
    for k, ref in enumerate((press, mob, frac)):
        pack_x(plan, ref, xa.at[k], xb.at[k])
        pack_y(plan, ref, ya.at[k], yb.at[k])


def inner_kernel(plan, press, mob, source, compress, well, res, tx, ty, tz, diag):
    shape = (plan.ny, plan.nz)
    row, lane = rows_of(shape), lanes_of(shape)

    def layer(i, carry):
        p_last, m_last, r_last = carry
        p, m = press[i], mob[i]
        t = harmonic(m_last, m)
        tx[i] = t
        flux_x = t * (p_last - p)
        t = harmonic(jnp.where(row == 0, 0.0, ahead(m, 0)), m)
        ty[i] = t
        flux_y = t * (ahead(p, 0) - p)
        t = harmonic(jnp.where(lane == 0, 0.0, ahead(m, 1)), m)
        tz[i] = t
        flux_z = t * (ahead(p, 1) - p)
        d = compress[i] + WELL_INDEX * well[i].astype(F32) * m
        diag[i] = d
        r = source[i] - d * p + flux_x + (flux_y - back(flux_y, 0)) + (flux_z - back(flux_z, 1))
        res[jnp.maximum(i - 1, 0)] = r_last - flux_x
        return p, m, r

    zero = jnp.zeros(shape, F32)
    res[plan.nx - 1] = lax.fori_loop(0, plan.nx, layer, (zero, zero, zero), unroll=2)[2]


def rim_kernel(plan, res_in, press, mob, frac, xa, xb, ya, yb, res, *rest):
    z_outs, comp = rest[:-1], rest[-1]
    nx, ny, nz = plan.nx, plan.ny, plan.nz
    last = nx - 1
    for high, k in ((False, 0), (True, last)):
        p, m = (side(plan, "gx", xa[f], xb[f], high) for f in (0, 1))
        res[k] = res[k] + harmonic(mob[k], m) * (p - press[k])
    for high, k in ((False, 0), (True, ny - 1)):
        p, m = (side(plan, "gy", ya[f], yb[f], high) for f in (0, 1))
        res[:, k, :] = res[:, k, :] + harmonic(mob[:, k, :], m) * (p - press[:, k, :])
    lane = lanes_of((ny, nz))
    pick = (rows_of((MSG_ROWS, nz)) == lanes_of((MSG_ROWS, nz))).astype(F32)
    wide = INTERSECTION
    for q, out in zip(plan.z_msgs, z_outs):
        up = plan.high("gz", q)[0]

        def layer(i, carry):
            acc = jnp.where(
                lane < wide, jnp.where(up, pltpu.roll(res[i], wide, 1), res[i]), 0.0
            )
            for k, ref in enumerate((press, mob, frac)):
                moved = jnp.where(
                    up,
                    pltpu.roll(ref[i], wide + k + 1, 1),
                    pltpu.roll(ref[i], wide + k, 1),
                )
                acc = jnp.where(lane == wide + k, moved, acc)
            comp[pl.ds(i * ny, ny), :] = acc
            return carry

        lax.fori_loop(0, nx, layer, 0, unroll=2)
        out[...] = dot(pick, comp[...], ((1,), (1,)))


def z_flux(plan, sent, got):
    wide = INTERSECTION
    out = []
    for own, other in zip(sent, got):
        t = harmonic(own[wide + 1 : wide + 2, :], other[wide + 1 : wide + 2, :])
        q = t * (other[wide : wide + 1, :] - own[wide : wide + 1, :])
        out.append((other[wide : wide + 1, :], other[wide + 2 : wide + 3, :], t, q))
    return out


def z_kernel(plan, n_msg, res, basis, rim_low, rim_top, *rest):
    sent, got = rest[:n_msg], rest[n_msg : 2 * n_msg]
    spec, ya, yb = rest[2 * n_msg :]
    nx, ny, nz = plan.nx, plan.ny, plan.nz
    wide = INTERSECTION
    out = dot(res[...].reshape(nx * ny, nz), basis[...])
    for q, other, (_, _, _, flux) in zip(plan.z_msgs, got, z_flux(plan, sent, got)):
        up = plan.high("gz", q)[1]
        row = rows_of(other.shape)
        near = jnp.where(up, 0, wide - 1)
        flux = jnp.broadcast_to(flux, other.shape)
        mix = jnp.where(row < wide, other[...], 0.0)
        mix = jnp.where(row == near, mix - flux, mix)
        mix = jnp.where(row == wide, flux, mix)
        rim = jnp.where(up, rim_top[...], rim_low[...])
        out = out + dot(mix, rim, ((0,), (0,)))
    spec[...] = out.reshape(nx, ny, out.shape[1])
    low, top = spec[:, :wide, :], spec[:, ny - wide :, :]
    for which, ref in ((0, ya), (1, yb)):
        ref[...] = jnp.where(plan.high("gy", which)[0], top, low)


def faces_kernel(plan, n_msg, res, mob, tx_in, ty_in, tz_in, xa, xb, ya, yb, *rest):
    sent, got = rest[:n_msg], rest[n_msg : 2 * n_msg]
    full, tx, ty_low, ty_top, tz_low, tz_top, hx, hy, hz, ty_rim = rest[2 * n_msg :]
    nx, ny, nz = plan.nx, plan.ny, plan.nz
    parts = z_flux(plan, sent, got)
    split = [z_sides(plan, [part[k] for part in parts]) for k in range(4)]
    hz[...] = columns(stack_rows([v for pair in split for v in pair]))
    for k, high in ((0, False), (1, True)):
        for f, field in ((0, 0), (1, 2)):
            hx[k, f] = side(plan, "gx", xa[field], xb[field], high)
            hy[k, f] = side(plan, "gy", ya[field], yb[field], high)
    tx[0] = harmonic(mob[0], side(plan, "gx", xa[1], xb[1], False))
    tx[nx] = harmonic(mob[nx - 1], side(plan, "gx", xa[1], xb[1], True))
    ty_rim[0] = harmonic(mob[:, 0, :], side(plan, "gy", ya[1], yb[1], False))
    ty_rim[1] = harmonic(mob[:, ny - 1, :], side(plan, "gy", ya[1], yb[1], True))
    row, lane = rows_of((ny, nz)), lanes_of((ny, nz))

    def layer(i, carry):
        @pl.when(i > 0)
        def _():
            tx[i] = tx_in[i]

        ty = ty_in[i]
        ty_low[i] = jnp.where(row == 0, ty_rim[0, pl.ds(i, 1), :], ty)
        ty_top[i] = jnp.where(row == ny - 1, ty_rim[1, pl.ds(i, 1), :], back(ty, 0))
        tz = tz_in[i]
        col = hz[pl.ds(i * ny, ny), :]
        tz_low[i] = jnp.where(lane == 0, col[:, 4:5], tz)
        tz_top[i] = jnp.where(lane == nz - 1, col[:, 5:6], back(tz, 1))
        flux = jnp.where(lane == 0, col[:, 6:7], 0.0) + jnp.where(
            lane == nz - 1, col[:, 7:8], 0.0
        )
        full[i] = res[i] + flux
        return carry

    lax.fori_loop(0, nx, layer, 0, unroll=2)


def y_kernel(plan, spec, ya, yb, basis, factors, modes, xa, xb):
    nx = plan.nx
    wide = INTERSECTION

    def layer(i, carry):
        low = side(plan, "gy", ya[i], yb[i], False)
        top = side(plan, "gy", ya[i], yb[i], True)
        modes[i] = dot(basis[...], jnp.concatenate([low, spec[i], top], axis=0))
        return carry

    lax.fori_loop(0, nx, layer, 0, unroll=2)
    low = jnp.zeros(modes.shape[1:], F32)
    top = low
    for k in range(wide):
        low = (modes[wide - 1 - k] + low) * factors[k]
        top = (modes[nx - wide + k] + top) * factors[k]
    for which, out in ((0, xa), (1, xb)):
        out[...] = jnp.where(plan.high("gx", which)[0], top, low)


def solve_kernel(
    plan, modes, xa, xb, factors, middle, basis_y, basis_z, total, direction, *rest
):
    (dxa, dxb, dya, dyb), z_outs, work = rest[:4], rest[4:-1], rest[-1]
    nx, ny, nz = plan.nx, plan.ny, plan.nz
    wide = INTERSECTION
    half = nx // 2
    low = side(plan, "gx", xa[...], xb[...], False)
    top = side(plan, "gx", xa[...], xb[...], True)

    def inward(k, carry):
        low, top = carry
        c = factors[wide + k]
        low = (modes[k] + low) * c
        top = (modes[nx - 1 - k] + top) * c
        modes[k] = low
        modes[nx - 1 - k] = top
        return low, top

    low, top = lax.fori_loop(0, half, inward, (low, top), unroll=2)
    c, mid = factors[wide + half - 1], middle[...]
    low, top = (low + c * top) * mid, (top + c * low) * mid

    def put(i, value):
        work[pl.ds(i * ny, ny), :] = dot(basis_y[...], value)

    put(half - 1, low)
    put(half, top)

    def outward(k, carry):
        low, top = carry
        i = half - 2 - k
        c = factors[wide + i]
        low = modes[i] + c * low
        top = modes[nx - 1 - i] + c * top
        put(i, low)
        put(nx - 1 - i, top)
        return low, top

    lax.fori_loop(0, half - 1, outward, (low, top), unroll=2)
    mean = jnp.sum(jnp.sum(total[...], axis=0, keepdims=True), axis=1, keepdims=True) / (
        nx * ny * nz
    )
    flat = dot(work[...], basis_z[...]) / mean
    direction[...] = flat.reshape(nx, ny, nz)
    pack_x(plan, direction, dxa, dxb)
    pack_y(plan, direction, dya, dyb)
    pack_z(plan, flat, z_outs)


def image_kernel(
    plan, n_dev, direction, diag, full, tx, ty_low, ty_top, tz_low, tz_top, xa, xb, ya, yb, *rest
):
    n_msg = len(plan.z_msgs)
    got = rest[:n_msg]
    image, sums, hz, hy = rest[n_msg:]
    nx, ny, nz = plan.nx, plan.ny, plan.nz
    hz[...] = columns(stack_rows(z_sides(plan, [ref[0:1, :] for ref in got])))
    hy[0] = side(plan, "gy", ya[...], yb[...], False)
    hy[1] = side(plan, "gy", ya[...], yb[...], True)
    row, lane = rows_of((ny, nz)), lanes_of((ny, nz))

    def layer(i, carry):
        d_last, im_last, rd, da = carry
        d = direction[i]
        flux = tx[i] * (d_last - d)
        col = hz[pl.ds(i * ny, ny), :]
        y_last = jnp.where(row == 0, hy[0, pl.ds(i, 1), :], ahead(d, 0))
        y_next = jnp.where(row == ny - 1, hy[1, pl.ds(i, 1), :], back(d, 0))
        z_last = jnp.where(lane == 0, col[:, 0:1], ahead(d, 1))
        z_next = jnp.where(lane == nz - 1, col[:, 1:2], back(d, 1))
        im = (
            diag[i] * d
            - flux
            + (ty_low[i] * (d - y_last) + ty_top[i] * (d - y_next))
            + (tz_low[i] * (d - z_last) + tz_top[i] * (d - z_next))
        )
        im_last = im_last + flux
        image[jnp.maximum(i - 1, 0)] = im_last
        rd = rd + full[i] * d
        da = da + jnp.where(i > 0, d_last, 0.0) * im_last
        return d, im, rd, da

    zero = jnp.zeros((ny, nz), F32)
    low = side(plan, "gx", xa[...], xb[...], False)
    top = side(plan, "gx", xa[...], xb[...], True)
    d, im, rd, da = lax.fori_loop(0, nx, layer, (low, zero, zero, zero), unroll=2)
    im = im + tx[nx] * (d - top)
    image[nx - 1] = im
    da = da + d * im
    lane = lanes_of((n_dev, 128))
    sums[...] = jnp.where(lane < 64, jnp.sum(rd), jnp.sum(da))


def sweep(plan, first, last_sweep, refs):
    nx, ny, nz = plan.nx, plan.ny, plan.nz
    (start, now, frac, coef, poro, well, gx, gy_low, gy_top, gz_low, gz_top, outflow) = refs[:12]
    x_low, x_top, hy, col_at, new, new_frac = refs[12:]
    row, lane = rows_of((ny, nz)), lanes_of((ny, nz))

    def upwind(g, low, high):
        return g * jnp.where(g > 0.0, low, high)

    def layer(i, carry):
        f, flow = carry
        is_end = i == nx - 1
        f_next = jnp.where(is_end, x_top, frac[jnp.minimum(i + 1, nx - 1)])
        s, c = now[i], coef[i]
        flow_next = upwind(gx[i + 1], f, f_next)
        y_last = jnp.where(row == 0, hy[0, pl.ds(i, 1), :], ahead(f, 0))
        y_next = jnp.where(row == ny - 1, hy[1, pl.ds(i, 1), :], back(f, 0))
        z_low, z_top = col_at(i)
        z_last = jnp.where(lane == 0, z_low, ahead(f, 1))
        z_next = jnp.where(lane == nz - 1, z_top, back(f, 1))
        rate = poro[i] * (1.0 / TIME_STEP)
        bal = (
            (flow_next - flow)
            + (upwind(gy_top[i], f, y_next) - upwind(gy_low[i], y_last, f))
            + (upwind(gz_top[i], f, z_next) - upwind(gz_low[i], z_last, f))
            - INJECT_RATE * well[i].astype(F32)
        )
        if not first:
            bal = bal + rate * (s - start[i])
        rest = 1.0 - s
        den = s * s + c * rest * rest
        slope = 2.0 * c * s * rest / (den * den)
        s = s - bal / (rate + outflow[i] * jnp.abs(slope))
        new[i] = s
        if not last_sweep:
            water, rest = s * s, 1.0 - s
            new_frac[i] = water / (water + c * rest * rest)
        return f_next, flow_next

    f0 = frac[0]
    lax.fori_loop(0, nx, layer, (f0, upwind(gx[0], x_low, f0)), unroll=2)


def pack_all(plan, ref, outs):
    xa, xb, ya, yb = outs[:4]
    pack_x(plan, ref, xa, xb)
    pack_y(plan, ref, ya, yb)
    pack_z(plan, ref[...].reshape(plan.nx * plan.ny, plan.nz), outs[4:])


def step_kernel(plan, *refs):
    n_msg = len(plan.z_msgs)
    (sums, press, direction, full, image, tx, ty_low, ty_top, tz_low, tz_top) = refs[:10]
    (hx, hy, hz, dxa, dxb, dya, dyb, dhz, sat, frac, coef, poro, well) = refs[10:23]
    (p_new, r_new, s_new, f_new, gx, gy_low, gy_top, gz_low, gz_top, outflow) = refs[23:33]
    packs = refs[33 : 37 + n_msg]
    ph, fh = refs[37 + n_msg :]
    nx, ny, nz = plan.nx, plan.ny, plan.nz
    all_sums = jnp.sum(sums[...], axis=0, keepdims=True)
    step = all_sums[:, 0:1] / all_sums[:, 64:65]
    x_low = hx[0, 0] + step * side(plan, "gx", dxa[...], dxb[...], False)
    x_top = hx[1, 0] + step * side(plan, "gx", dxa[...], dxb[...], True)
    ph[0] = hy[0, 0] + step * side(plan, "gy", dya[...], dyb[...], False)
    ph[1] = hy[1, 0] + step * side(plan, "gy", dya[...], dyb[...], True)
    fh[0] = hy[0, 1]
    fh[1] = hy[1, 1]
    row, lane = rows_of((ny, nz)), lanes_of((ny, nz))

    def layer(i, carry):
        p, g = carry
        p_new[i] = p
        r_new[i] = full[i] - step * image[i]
        k = jnp.minimum(i + 1, nx - 1)
        p_next = jnp.where(i == nx - 1, x_top, press[k] + step * direction[k])
        g_next = tx[i + 1] * (p - p_next)
        gx[i + 1] = g_next
        cells = pl.ds(i * ny, ny)
        zc = hz[cells, 0:2] + step * dhz[cells, 0:2]
        y_last = jnp.where(row == 0, ph[0, pl.ds(i, 1), :], ahead(p, 0))
        y_next = jnp.where(row == ny - 1, ph[1, pl.ds(i, 1), :], back(p, 0))
        z_last = jnp.where(lane == 0, zc[:, 0:1], ahead(p, 1))
        z_next = jnp.where(lane == nz - 1, zc[:, 1:2], back(p, 1))
        parts = (
            (gy_low, ty_low[i] * (y_last - p), -1.0),
            (gy_top, ty_top[i] * (p - y_next), 1.0),
            (gz_low, tz_low[i] * (z_last - p), -1.0),
            (gz_top, tz_top[i] * (p - z_next), 1.0),
        )
        total = jnp.maximum(-g, 0.0) + jnp.maximum(g_next, 0.0)
        for ref, value, sign in parts:
            ref[i] = value
            total = total + jnp.maximum(value * sign, 0.0)
        outflow[i] = total
        return p_next, g_next

    p0 = press[0] + step * direction[0]
    g0 = tx[0] * (x_low - p0)
    gx[0] = g0
    lax.fori_loop(0, nx, layer, (p0, g0), unroll=2)

    def col_at(i):
        cells = pl.ds(i * ny, ny)
        return hz[cells, 2:3], hz[cells, 3:4]

    sweep(
        plan, True, False,
        (sat, sat, frac, coef, poro, well, gx, gy_low, gy_top, gz_low, gz_top, outflow,
         hx[0, 1], hx[1, 1], fh, col_at, s_new, f_new),
    )
    pack_all(plan, f_new, packs)


def later_kernel(plan, last_sweep, *refs):
    n_msg = len(plan.z_msgs)
    fields = refs[:12]
    xa, xb, ya, yb = refs[12:16]
    got = refs[16 : 16 + n_msg]
    rest = refs[16 + n_msg :]
    if last_sweep:
        new, fh, hz = rest
        new_frac, packs = None, ()
    else:
        new, new_frac = rest[:2]
        packs = rest[2 : 6 + n_msg]
        fh, hz = rest[6 + n_msg :]
    ny = plan.ny
    hz[...] = columns(stack_rows(z_sides(plan, [ref[0:1, :] for ref in got])))
    fh[0] = side(plan, "gy", ya[...], yb[...], False)
    fh[1] = side(plan, "gy", ya[...], yb[...], True)

    def col_at(i):
        cells = pl.ds(i * ny, ny)
        return hz[cells, 0:1], hz[cells, 1:2]

    sweep(
        plan, False, last_sweep,
        fields + (side(plan, "gx", xa[...], xb[...], False), side(plan, "gx", xa[...], xb[...], True),
                  fh, col_at, new, new_frac),
    )
    if not last_sweep:
        pack_all(plan, new_frac, packs)


def per_device(
    counts, pressure, source, saturation, permeability, compress, porosity, rock_type, well_mask, oil_factor
):
    nx, ny, nz = pressure.shape
    wide = INTERSECTION
    plan = Plan(nx, ny, nz, counts)
    n_msg = len(plan.z_msgs)
    n_dev = counts["gx"] * counts["gy"] * counts["gz"]
    cells = nx * ny
    my, mz = ny + 2 * wide, nz + 2 * wide
    table_y, eigen_y = sine_basis(my)
    table_z, eigen_z = sine_basis(mz)
    factors, middle = sweep_factors(wide + nx // 2, eigen_y, eigen_z)
    const = lambda v: jnp.asarray(v, F32)
    factors, middle = const(factors), const(middle)
    rim = np.zeros((2, MSG_ROWS, mz))
    rim[0, :wide] = table_z[:wide]
    rim[0, wide] = table_z[wide]
    rim[1, :wide] = table_z[mz - wide :]
    rim[1, wide] = table_z[mz - wide - 1]

    def swap(axis, a, b):
        return (
            lax.ppermute(a, axis, plan.perm(axis, 0)),
            lax.ppermute(b, axis, plan.perm(axis, 1)),
        )

    def swap_z(msgs):
        return [lax.ppermute(v, "gz", plan.perm("gz", q)) for q, v in zip(plan.z_msgs, msgs)]

    full_shape = (nx, ny, nz)
    x_face, y_face, z_face = (ny, nz), (nx, nz), (8, cells)
    face_shapes = [x_face, x_face, y_face, y_face] + [z_face] * n_msg

    def exchange(packs):
        z = swap_z(packs[4:])
        y = swap("gy", packs[2], packs[3])
        x = swap("gx", packs[0], packs[1])
        return [*x, *y, *z]

    mob, coef, frac, xa, xb, ya, yb, total = call(
        functools.partial(mobility_kernel, plan),
        [full_shape] * 3 + [(3,) + x_face] * 2 + [(3,) + y_face] * 2 + [x_face],
        (pressure, saturation, permeability, rock_type, oil_factor),
        smem=(4,),
    )
    ya, yb = swap("gy", ya, yb)
    xa, xb = swap("gx", xa, xb)
    res, tx, ty, tz, diag = call(
        functools.partial(inner_kernel, plan),
        [full_shape] * 5,
        (pressure, mob, source, compress, well_mask),
    )
    res, *sent = call(
        functools.partial(rim_kernel, plan),
        [full_shape] + [(MSG_ROWS, cells)] * n_msg,
        (res, pressure, mob, frac, xa, xb, ya, yb),
        scratch=[(cells, nz)],
        aliases={0: 0},
    )
    got = swap_z(sent)
    spec, sa, sb = call(
        functools.partial(z_kernel, plan, n_msg),
        [(nx, ny, mz)] + [(nx, wide, mz)] * 2,
        (res, const(table_z[wide : wide + nz]), const(rim[0]), const(rim[1]), *sent, *got),
    )
    sa, sb = swap("gy", sa, sb)
    full, tx, ty_low, ty_top, tz_low, tz_top, hx, hy, hz = call(
        functools.partial(faces_kernel, plan, n_msg),
        [full_shape, (nx + 1, ny, nz)] + [full_shape] * 4
        + [(2, 2) + x_face, (2, 2) + y_face, (cells, 128)],
        (res, mob, tx, ty, tz, xa, xb, ya, yb, *sent, *got),
        scratch=[(2,) + y_face],
    )
    modes, ma, mb = call(
        functools.partial(y_kernel, plan),
        [(nx, my, mz), (my, mz), (my, mz)],
        (spec, sa, sb, const(table_y), factors),
    )
    ma, mb = swap("gx", ma, mb)
    direction, *packs = call(
        functools.partial(solve_kernel, plan),
        [full_shape] + face_shapes,
        (modes, ma, mb, factors, middle, const(table_y[wide : wide + ny]),
         const(table_z[:, wide : wide + nz]), total),
        scratch=[(cells, mz)],
    )
    dhalo = exchange(packs)
    image, sums, dhz = call(
        functools.partial(image_kernel, plan, n_dev),
        [full_shape, (n_dev, 128), (cells, 128)],
        (direction, diag, full, tx, ty_low, ty_top, tz_low, tz_top, *dhalo),
        scratch=[(2,) + y_face],
    )
    sums = lax.all_to_all(sums, AXES, 0, 0, tiled=True)
    outs = call(
        functools.partial(step_kernel, plan),
        [full_shape] * 4 + [(nx + 1, ny, nz)] + [full_shape] * 5 + face_shapes,
        (sums, pressure, direction, full, image, tx, ty_low, ty_top, tz_low, tz_top,
         hx, hy, hz, *dhalo[:4], dhz, saturation, frac, coef, porosity, well_mask),
        scratch=[(2,) + y_face] * 2,
        limit=40,
    )
    p_new, r_new, current, frac, *flows = outs[:10]
    packs = outs[10:]
    for sweep_index in range(1, NEWTON):
        halo = exchange(packs)
        last_sweep = sweep_index == NEWTON - 1
        outs = call(
            functools.partial(later_kernel, plan, last_sweep),
            [full_shape] if last_sweep else [full_shape] * 2 + face_shapes,
            (saturation, current, frac, coef, porosity, well_mask, *flows, *halo),
            scratch=[(2,) + y_face, (cells, 128)],
        )
        current = outs[0]
        if not last_sweep:
            frac, packs = outs[1], outs[2:]
    return p_new, r_new, current


def solution(mesh):
    spec = P(*AXES)
    return jax.shard_map(
        functools.partial(per_device, dict(mesh.shape)),
        mesh=mesh,
        in_specs=(spec,) * 8 + (P(),),
        out_specs=(spec,) * 3,
        check_vma=False,
    )
```

```python
import functools
import math

import jax
import jax.numpy as jnp
import numpy as np
from jax import lax
from jax.experimental import pallas as pl
from jax.experimental.pallas import tpu as pltpu
from jax.sharding import PartitionSpec as P

INTERSECTION = 8
NEWTON = 3

WELL_INDEX = 4.0
INJECT_RATE = 2.0
TIME_STEP = 0.05

AXES = ("gx", "gy", "gz")
F32 = jnp.float32
HIGH = lax.Precision.HIGHEST
MSG_ROWS = 16
CHUNKS = 4


def sine_basis(length):
    points = np.arange(length) + 1
    angles = np.outer(points, points) % (2 * (length + 1)) * (math.pi / (length + 1))
    table = math.sqrt(2.0 / (length + 1)) * np.sin(angles)
    eigen = 2.0 - 2.0 * np.cos(points * (math.pi / (length + 1)))
    return table, eigen


def sweep_factors(count, eigen_y, eigen_z):
    shift = 2.0 + eigen_y[:, None] + eigen_z[None, :]
    factors = []
    last = np.zeros_like(shift)
    for _ in range(count):
        last = 1.0 / (shift - last)
        factors.append(last)
    return np.stack(factors), 1.0 / (1.0 - last * last)


def pairs(count, periodic, parity):
    if periodic and count % 2:
        step = 1 if parity == 0 else -1
        return [(i, (i + step) % count) for i in range(count)]
    out = []
    for i in range(parity, count, 2):
        j = i + 1
        if periodic:
            j = j % count
        if j < count:
            out += [(i, j), (j, i)]
    return out


def harmonic(one, two):
    return 2.0 * one * two / (one + two)


def dot(one, two, dims=((1,), (0,))):
    return lax.dot_general(
        one, two, (dims, ((), ())), precision=HIGH, preferred_element_type=F32
    )


def rows_of(shape):
    return lax.broadcasted_iota(jnp.int32, shape, 0)


def lanes_of(shape):
    return lax.broadcasted_iota(jnp.int32, shape, 1)


def back(value, axis):
    return pltpu.roll(value, value.shape[axis] - 1, axis)


def ahead(value, axis):
    return pltpu.roll(value, 1, axis)


class Plan:
    def __init__(self, nx, ny, nz, counts):
        self.nx, self.ny, self.nz = nx, ny, nz
        self.counts = counts
        self.z_msgs = [q for q in (0, 1) if pairs(counts["gz"], False, q)]

    def perm(self, axis, which):
        return pairs(self.counts[axis], axis != "gz", which)

    def high(self, axis, which):
        if axis != "gz" and self.counts[axis] % 2:
            return (which == 0, which == 1)
        up = (lax.axis_index(axis) % 2) == which
        return (up, up)


def call(kernel, outs, args, scratch=(), aliases=None, hbm=(), hbm_out=(), limit=28):
    def spec(k, remote):
        return pl.BlockSpec(memory_space=pltpu.HBM if k in remote else pltpu.VMEM)

    args = [
        pltpu.with_memory_space_constraint(v, pltpu.HBM) if k in hbm else v
        for k, v in enumerate(args)
    ]
    return pl.pallas_call(
        kernel,
        out_shape=[jax.ShapeDtypeStruct(s, F32) for s in outs],
        in_specs=[spec(k, hbm) for k in range(len(args))],
        out_specs=[spec(k, hbm_out) for k in range(len(outs))],
        scratch_shapes=[pltpu.VMEM(v, F32) if isinstance(v, tuple) else v for v in scratch],
        input_output_aliases=aliases or {},
        compiler_params=pltpu.CompilerParams(vmem_limit_bytes=limit << 20),
    )(*args)


def halves(value):
    top = value.astype(jnp.bfloat16)
    return top, (value - top.astype(F32)).astype(jnp.bfloat16)


def mxu(one, two, dims=((1,), (0,))):
    return lax.dot_general(one, two, (dims, ((), ())), preferred_element_type=F32)


def side(plan, axis, ref_a, ref_b, high):
    a_high = plan.high(axis, 0)[1]
    if high:
        return jnp.where(a_high, ref_a, ref_b)
    return jnp.where(a_high, ref_b, ref_a)


def pack_x(plan, ref, out_a, out_b):
    last = plan.nx - 1
    for which, out in ((0, out_a), (1, out_b)):
        out[...] = ref[jnp.where(plan.high("gx", which)[0], last, 0)]


def pack_y(plan, ref, out_a, out_b):
    low, top = ref[:, 0, :], ref[:, plan.ny - 1, :]
    for which, out in ((0, out_a), (1, out_b)):
        out[...] = jnp.where(plan.high("gy", which)[0], top, low)


def tile_put(plan, tile, i, q, value):
    group = 128 // plan.ny
    r = i // group
    rows = pl.ds((i % group) * plan.ny, plan.ny)
    moved = pltpu.roll(value, r + plan.high("gz", q)[0].astype(jnp.int32), 1)
    tile[q, rows, :] = jnp.where(lanes_of(value.shape) == r, moved, tile[q, rows, :])


def tile_out(plan, tile, outs):
    for q, out in zip(plan.z_msgs, outs):
        out[...] = jnp.transpose(tile[q])[: out.shape[0], :]


def spread(plan, gots, outs):
    vals = [got[...] for got in gots]
    if len(vals) > 1:
        vals = list(z_sides(plan, vals))
    for val, out in zip(vals, outs):
        turned = jnp.transpose(val)
        for r in range(val.shape[0]):
            out[r * 128 : (r + 1) * 128, :] = jnp.broadcast_to(turned[:, r : r + 1], (128, 128))


def stack_rows(parts):
    cells = parts[0].shape[1]
    row = rows_of((8, cells))
    out = jnp.zeros((8, cells), F32)
    for k, part in enumerate(parts):
        out = jnp.where(row == k, jnp.broadcast_to(part, (8, cells)), out)
    return out


def z_sides(plan, vals):
    low, top = jnp.zeros_like(vals[0]), jnp.zeros_like(vals[0])
    for q, val in zip(plan.z_msgs, vals):
        up = plan.high("gz", q)[1]
        low = low + jnp.where(up, 0.0, val)
        top = top + jnp.where(up, val, 0.0)
    return low, top


def mobility_kernel(
    plan, press_in, sat_in, perm_in, rock_in, oil_in,
    press, sat, mob, coef, frac, xa, xb, ya, yb, total, perm, rock, oil, sem, oil_sem,
):
    kinds = oil.shape[0]
    oil_move = pltpu.make_async_copy(oil_in, oil, oil_sem)
    oil_move.start()
    size = plan.nx // CHUNKS
    moves = []
    for c in range(CHUNKS):
        cut = pl.ds(c * size, size)
        for k, (src, dst) in enumerate(
            ((sat_in, sat), (rock_in, rock), (perm_in, perm), (press_in, press))
        ):
            move = pltpu.make_async_copy(src.at[cut], dst.at[cut], sem.at[c, k])
            move.start()
            moves.append(move)

    def layer(i, acc):
        s, kind = sat[i], rock[i]
        c = jnp.full(s.shape, oil[0], F32)
        for k in range(1, kinds):
            c = jnp.where(kind == k, oil[k], c)
        water, rest = s * s, 1.0 - s
        den = water + c * rest * rest
        m = perm[i] * den
        coef[i] = c
        mob[i] = m
        frac[i] = water / den
        return acc + m

    acc = jnp.zeros((plan.ny, plan.nz), F32)
    oil_move.wait()
    for c in range(CHUNKS):
        for move in moves[4 * c : 4 * c + 3]:
            move.wait()
        acc = lax.fori_loop(c * size, (c + 1) * size, layer, acc, unroll=4)
    total[...] = acc
    for c in range(CHUNKS):
        moves[4 * c + 3].wait()
    for k, ref in enumerate((press, mob, frac)):
        pack_x(plan, ref, xa.at[k], xb.at[k])
        pack_y(plan, ref, ya.at[k], yb.at[k])


def inner_kernel(plan, press, mob, source, compress, well, res, tx, ty, tz, diag):
    shape = (plan.ny, plan.nz)
    row, lane = rows_of(shape), lanes_of(shape)

    def layer(i, carry):
        p_last, m_last, r_last = carry
        p, m = press[i], mob[i]
        t = harmonic(m_last, m)
        tx[i] = t
        flux_x = t * (p_last - p)
        t = harmonic(jnp.where(row == 0, 0.0, ahead(m, 0)), m)
        ty[i] = t
        flux_y = t * (ahead(p, 0) - p)
        t = harmonic(jnp.where(lane == 0, 0.0, ahead(m, 1)), m)
        tz[i] = t
        flux_z = t * (ahead(p, 1) - p)
        d = compress[i] + WELL_INDEX * well[i].astype(F32) * m
        diag[i] = d
        r = source[i] - d * p + flux_x + (flux_y - back(flux_y, 0)) + (flux_z - back(flux_z, 1))
        res[jnp.maximum(i - 1, 0)] = r_last - flux_x
        return p, m, r

    zero = jnp.zeros(shape, F32)
    res[plan.nx - 1] = lax.fori_loop(0, plan.nx, layer, (zero, zero, zero), unroll=2)[2]


def rim_kernel(plan, res_in, press, mob, frac, xa, xb, ya, yb, res, *rest):
    z_outs, comp = rest[:-1], rest[-1]
    nx, ny, nz = plan.nx, plan.ny, plan.nz
    last = nx - 1
    for high, k in ((False, 0), (True, last)):
        p, m = (side(plan, "gx", xa[f], xb[f], high) for f in (0, 1))
        res[k] = res[k] + harmonic(mob[k], m) * (p - press[k])
    for high, k in ((False, 0), (True, ny - 1)):
        p, m = (side(plan, "gy", ya[f], yb[f], high) for f in (0, 1))
        res[:, k, :] = res[:, k, :] + harmonic(mob[:, k, :], m) * (p - press[:, k, :])
    lane = lanes_of((ny, nz))
    wide = INTERSECTION
    for q, out in zip(plan.z_msgs, z_outs):
        up = plan.high("gz", q)[0].astype(jnp.int32)

        def layer(i, carry):
            acc = pltpu.roll(res[i], up * wide, 1)
            for k, ref in enumerate((press, mob, frac)):
                acc = jnp.where(lane < wide + k, acc, pltpu.roll(ref[i], wide + k + up, 1))
            comp[pl.ds(i * ny, ny), :] = acc
            return carry

        lax.fori_loop(0, nx, layer, 0, unroll=4)
        for k in range(nx * ny // 128):
            cut = slice(k * 128, (k + 1) * 128)
            out[:, cut] = jnp.transpose(comp[cut, :])[:MSG_ROWS, :]


def z_flux(plan, sent, got):
    wide = INTERSECTION
    out = []
    for own, other in zip(sent, got):
        t = harmonic(own[wide + 1 : wide + 2, :], other[wide + 1 : wide + 2, :])
        q = t * (other[wide : wide + 1, :] - own[wide : wide + 1, :])
        out.append((other[wide : wide + 1, :], other[wide + 2 : wide + 3, :], t, q))
    return out


def z_kernel(plan, n_msg, res, basis, rim_low, rim_top, order, *rest):
    sent, got = rest[:n_msg], rest[n_msg : 2 * n_msg]
    spec, ya, yb = rest[2 * n_msg :]
    nx, ny, nz = plan.nx, plan.ny, plan.nz
    wide = INTERSECTION
    mixes, rims = [], []
    for q, other, (_, _, _, flux) in zip(plan.z_msgs, got, z_flux(plan, sent, got)):
        up = plan.high("gz", q)[1]
        row = rows_of(other.shape)
        near = jnp.where(up, 0, wide - 1)
        flux = jnp.broadcast_to(flux, other.shape)
        mix = jnp.where(row < wide, other[...], 0.0)
        mix = jnp.where(row == near, mix - flux, mix)
        mix = jnp.where(row == wide, flux, mix)
        top, low = halves(mix)
        mixes.append(jnp.concatenate([top, low, top], axis=0))
        rims.append(jnp.where(up, rim_top[...], rim_low[...]).astype(jnp.bfloat16))
    group = 128 // ny
    for k in range(nx // group):
        value = res[k * group : (k + 1) * group].reshape(128, nz)
        top, low = halves(value)
        out = mxu(jnp.concatenate([top, low, top], axis=1), basis[...])
        for mix, rim in zip(mixes, rims):
            out = out + mxu(mix[:, k * 128 : (k + 1) * 128], rim, ((0,), (0,)))
        spec[k * group : (k + 1) * group] = out.reshape(group, ny, out.shape[1])
    tail = 2 * wide
    per = 128 // tail
    for which, ref in ((0, ya), (1, yb)):
        start = jnp.where(plan.high("gy", which)[0], ny - wide, 0)
        rows = pl.ds(pl.multiple_of(start, 8), wide)
        ref[:nx] = spec[:, rows, :nz]
        for g in range(nx // per):
            ref[nx + g] = jnp.concatenate(
                [spec[g * per + j, rows, nz:] for j in range(per)], axis=1
            )


def faces_xy_kernel(plan, mob, tx_in, ty_in, xa, xb, ya, yb, tx, ty_low, ty_top, hx, hy, ty_rim):
    nx, ny, nz = plan.nx, plan.ny, plan.nz
    for k, high in ((0, False), (1, True)):
        for f, field in ((0, 0), (1, 2)):
            hx[k, f] = side(plan, "gx", xa[field], xb[field], high)
            hy[k, f] = side(plan, "gy", ya[field], yb[field], high)
    tx[nx] = harmonic(mob[nx - 1], side(plan, "gx", xa[1], xb[1], True))
    ty_rim[0] = harmonic(mob[:, 0, :], side(plan, "gy", ya[1], yb[1], False))
    ty_rim[1] = harmonic(mob[:, ny - 1, :], side(plan, "gy", ya[1], yb[1], True))
    row = rows_of((ny, nz))

    def layer(i, carry):
        tx[i] = tx_in[i]
        ty = ty_in[i]
        ty_low[i] = jnp.where(row == 0, ty_rim[0, pl.ds(i, 1), :], ty)
        ty_top[i] = jnp.where(row == ny - 1, ty_rim[1, pl.ds(i, 1), :], back(ty, 0))
        return carry

    lax.fori_loop(0, nx, layer, 0, unroll=4)
    tx[0] = harmonic(mob[0], side(plan, "gx", xa[1], xb[1], False))


def faces_z_kernel(plan, n_msg, res, tz_in, poro, well, *rest):
    sent, got = rest[:n_msg], rest[n_msg : 2 * n_msg]
    full, tz_low, tz_top, hz, rate, inject = rest[2 * n_msg :]
    nx, ny, nz = plan.nx, plan.ny, plan.nz
    parts = z_flux(plan, sent, got)
    split = [z_sides(plan, [part[k] for part in parts]) for k in range(4)]
    rows = stack_rows([v for pair in split for v in pair])
    for k in range(nx * ny // 128):
        cut = slice(k * 128, (k + 1) * 128)
        hz[cut, :8] = jnp.transpose(rows[:, cut])
    lane = lanes_of((ny, nz))

    def layer(i, carry):
        tz = tz_in[i]
        col = hz[pl.ds(i * ny, ny), :8]
        tz_low[i] = jnp.where(lane == 0, col[:, 4:5], tz)
        tz_top[i] = jnp.where(lane == nz - 1, col[:, 5:6], back(tz, 1))
        flux = jnp.where(lane == 0, col[:, 6:7], 0.0) + jnp.where(
            lane == nz - 1, col[:, 7:8], 0.0
        )
        full[i] = res[i] + flux
        rate[i] = poro[i] / TIME_STEP
        inject[i] = INJECT_RATE * well[i].astype(F32)
        return carry

    lax.fori_loop(0, nx, layer, 0, unroll=4)


def wide_rows(plan, msg_a, msg_b, i, high):
    nx = plan.nx
    tail = 2 * INTERSECTION
    per = 128 // tail
    ends = side(plan, "gy", msg_a[nx + i // per], msg_b[nx + i // per], high)
    ends = pltpu.roll(ends, (128 - (i % per) * tail) % 128, 1)[:, :tail]
    return jnp.concatenate([side(plan, "gy", msg_a[i], msg_b[i], high), ends], axis=1)


def thrice(value):
    top, low = halves(value)
    return jnp.concatenate([top, low, top], axis=0)


def fold(value, nz):
    rows, tail = value.shape[0], value.shape[1] - nz
    ends = jnp.concatenate(
        [value[k : k + 8, nz:] for k in range(0, rows, 8)]
        + [jnp.zeros((8, nz - rows // 8 * tail), F32)],
        axis=1,
    )
    return jnp.concatenate([value[:, :nz], ends], axis=0)


def unfold(value, tail):
    rows = value.shape[0] - 8
    ends = jnp.concatenate(
        [value[rows:, k * tail : (k + 1) * tail] for k in range(rows // 8)], axis=0
    )
    return jnp.concatenate([value[:rows], ends], axis=1)


def y_kernel(plan, spec, ya, yb, basis, factors, order, modes, xa, xb):
    nx = plan.nx
    wide = INTERSECTION

    def layer(i, carry):
        low = wide_rows(plan, ya, yb, i, False)
        top = wide_rows(plan, ya, yb, i, True)
        modes[i] = mxu(basis[...], thrice(jnp.concatenate([low, spec[i], top], axis=0)))
        return carry

    lax.fori_loop(0, nx, layer, 0, unroll=4)
    low = jnp.zeros(modes.shape[1:], F32)
    top = low
    for k in range(wide):
        low = (modes[wide - 1 - k] + low) * factors[k]
        top = (modes[nx - wide + k] + top) * factors[k]
    for which, out in ((0, xa), (1, xb)):
        out[...] = fold(jnp.where(plan.high("gx", which)[0], top, low), plan.nz)


def solve_kernel(
    plan, modes, xa, xb, factors, middle, basis_y, basis_z, total, direction, *rest
):
    (dxa, dxb, dya, dyb), z_outs, (work, tile) = rest[:4], rest[4:-2], rest[-2:]
    nx, ny, nz = plan.nx, plan.ny, plan.nz
    wide = INTERSECTION
    half = nx // 2
    low = unfold(side(plan, "gx", xa[...], xb[...], False), 2 * wide)
    top = unfold(side(plan, "gx", xa[...], xb[...], True), 2 * wide)

    def inward(k, carry):
        low, top = carry
        c = factors[wide + k]
        low = (modes[k] + low) * c
        top = (modes[nx - 1 - k] + top) * c
        modes[k] = low
        modes[nx - 1 - k] = top
        return low, top

    low, top = lax.fori_loop(0, half, inward, (low, top), unroll=2)
    c, mid = factors[wide + half - 1], middle[...]
    low, top = (low + c * top) * mid, (top + c * low) * mid

    def put(i, value):
        work[pl.ds(i * ny, ny), :] = mxu(basis_y[...], thrice(value))

    put(half - 1, low)
    put(half, top)

    def outward(k, carry):
        low, top = carry
        i = half - 2 - k
        c = factors[wide + i]
        low = modes[i] + c * low
        top = modes[nx - 1 - i] + c * top
        put(i, low)
        put(nx - 1 - i, top)
        return low, top

    lax.fori_loop(0, half - 1, outward, (low, top), unroll=3)
    mean = jnp.sum(jnp.sum(total[...], axis=0, keepdims=True), axis=1, keepdims=True) / (
        nx * ny * nz
    )
    inverse = 1.0 / mean
    group = 128 // ny
    base_top, base_low = basis_z[0], basis_z[1]

    def lift(r, carry):
        high, rest_ = halves(work[pl.ds(r * 128, 128), :])
        value = mxu(high, base_top) + (mxu(rest_, base_top) + mxu(high, base_low))
        value = value * inverse
        direction[pl.ds(r * group, group)] = value.reshape(group, ny, nz)
        for q in plan.z_msgs:
            moved = pltpu.roll(value, r + plan.high("gz", q)[0].astype(jnp.int32), 1)
            tile[q] = jnp.where(lanes_of((128, nz)) == r, moved, tile[q])
        return carry

    lax.fori_loop(0, nx // group, lift, 0, unroll=2)
    pack_x(plan, direction, dxa, dxb)
    pack_y(plan, direction, dya, dyb)
    tile_out(plan, tile, z_outs)


def image_kernel(
    plan, n_dev, direction, diag, full, tx, ty_low, ty_top, tz_low, tz_top, xa, xb, ya, yb, *rest
):
    n_msg = len(plan.z_msgs)
    got = rest[:n_msg]
    image, sums = rest[n_msg : n_msg + 2]
    hz, hy = rest[n_msg + 2 : -1], rest[-1]
    nx, ny, nz = plan.nx, plan.ny, plan.nz
    spread(plan, got, hz)
    hy[0] = side(plan, "gy", ya[...], yb[...], False)
    hy[1] = side(plan, "gy", ya[...], yb[...], True)
    row, lane = rows_of((ny, nz)), lanes_of((ny, nz))

    def layer(i, carry):
        d_last, im_last, rd, da = carry
        d = direction[i]
        flux = tx[i] * (d_last - d)
        cells = pl.ds(i * ny, ny)
        y_last = jnp.where(row == 0, hy[0, pl.ds(i, 1), :], ahead(d, 0))
        y_next = jnp.where(row == ny - 1, hy[1, pl.ds(i, 1), :], back(d, 0))
        z_last = jnp.where(lane == 0, hz[0][cells, :], ahead(d, 1))
        z_next = jnp.where(lane == nz - 1, hz[-1][cells, :], back(d, 1))
        im = (
            diag[i] * d
            - flux
            + (ty_low[i] * (d - y_last) + ty_top[i] * (d - y_next))
            + (tz_low[i] * (d - z_last) + tz_top[i] * (d - z_next))
        )
        im_last = im_last + flux
        image[jnp.maximum(i - 1, 0)] = im_last
        rd = rd + full[i] * d
        da = da + jnp.where(i > 0, d_last, 0.0) * im_last
        return d, im, rd, da

    zero = jnp.zeros((ny, nz), F32)
    low = side(plan, "gx", xa[...], xb[...], False)
    top = side(plan, "gx", xa[...], xb[...], True)
    d, im, rd, da = lax.fori_loop(0, nx, layer, (low, zero, zero, zero), unroll=4)
    im = im + tx[nx] * (d - top)
    image[nx - 1] = im
    da = da + d * im
    lane = lanes_of((n_dev, 128))
    sums[...] = jnp.where(lane < 64, jnp.sum(rd), jnp.sum(da))


def sweep(plan, first, refs, x_low, x_top, hy, z_at, done):
    nx, ny, nz = plan.nx, plan.ny, plan.nz
    (start, now, frac, coef, rate, inject, gx, gy_low, gy_top, gz_low, gz_top, outflow) = refs
    row, lane = rows_of((ny, nz)), lanes_of((ny, nz))

    def upwind(g, low, high):
        return g * jnp.where(g > 0.0, low, high)

    def layer(i, carry):
        f, flow = carry
        f_next = jnp.where(i == nx - 1, x_top, frac[jnp.minimum(i + 1, nx - 1)])
        s, c = now[i], coef[i]
        flow_next = upwind(gx[i + 1], f, f_next)
        y_last = jnp.where(row == 0, hy[0, pl.ds(i, 1), :], ahead(f, 0))
        y_next = jnp.where(row == ny - 1, hy[1, pl.ds(i, 1), :], back(f, 0))
        z_low, z_top = z_at(i)
        z_last = jnp.where(lane == 0, z_low, ahead(f, 1))
        z_next = jnp.where(lane == nz - 1, z_top, back(f, 1))
        bal = (
            (flow_next - flow)
            + (upwind(gy_top[i], f, y_next) - upwind(gy_low[i], y_last, f))
            + (upwind(gz_top[i], f, z_next) - upwind(gz_low[i], z_last, f))
            - inject[i]
        )
        if not first:
            bal = bal + rate[i] * (s - start[i])
        rest = 1.0 - s
        part = c * rest
        den = s * s + part * rest
        square = den * den
        slope = 2.0 * part * s
        s = s - bal * square / (rate[i] * square + outflow[i] * jnp.abs(slope))
        done(i, s, c)
        return f_next, flow_next

    f0 = frac[0]
    lax.fori_loop(0, nx, layer, (f0, upwind(gx[0], x_low, f0)), unroll=4)


def keep(plan, new, new_frac, tile):
    def done(i, s, c):
        new[i] = s
        water, rest = s * s, 1.0 - s
        f = water / (water + c * rest * rest)
        new_frac[i] = f
        for q in plan.z_msgs:
            tile_put(plan, tile, i, q, f)

    return done


def pack_all(plan, ref, tile, outs):
    xa, xb, ya, yb = outs[:4]
    pack_x(plan, ref, xa, xb)
    pack_y(plan, ref, ya, yb)
    tile_out(plan, tile, outs[4:])


def step_of(sums):
    both = jnp.sum(sums[...], axis=0, keepdims=True)
    return both[:, 0:1] / both[:, 64:65]


def write_out(plan, i, ref, out, sem):
    size = plan.nx // CHUNKS

    @pl.when(i % size == size - 1)
    def _():
        c = i // size
        cut = pl.ds(c * size, size)
        pltpu.make_async_copy(ref.at[cut], out.at[cut], sem.at[c]).start()


def write_end(plan, ref, out, sem):
    size = plan.nx // CHUNKS
    for c in range(CHUNKS):
        cut = pl.ds(c * size, size)
        pltpu.make_async_copy(ref.at[cut], out.at[cut], sem.at[c]).wait()


def output_kernel(plan, sums, press, direction, full, image, p_out, r_out, token, p_new, r_new, p_sem, r_sem):
    step = step_of(sums)

    def layer(i, carry):
        p_new[i] = press[i] + step * direction[i]
        write_out(plan, i, p_new, p_out, p_sem)
        r_new[i] = full[i] - step * image[i]
        write_out(plan, i, r_new, r_out, r_sem)
        return carry

    lax.fori_loop(0, plan.nx, layer, 0, unroll=4)
    token[...] = jnp.zeros(token.shape, F32)
    write_end(plan, p_new, p_out, p_sem)
    write_end(plan, r_new, r_out, r_sem)


def step_kernel(plan, *refs):
    n_msg = len(plan.z_msgs)
    (sums, press, direction, tx, ty_low, ty_top, tz_low, tz_top) = refs[:8]
    (hx, hy, hz, dxa, dxb, dya, dyb) = refs[8:15]
    dhz = refs[15 : 15 + n_msg]
    (sat, frac, coef, rate, inject) = refs[15 + n_msg : 20 + n_msg]
    outs = refs[20 + n_msg :]
    (s_new, f_new, gx, gy_low, gy_top, gz_low, gz_top, outflow) = outs[:8]
    packs = outs[8 : 12 + n_msg]
    ph, fh, tile = outs[12 + n_msg :]
    nx, ny, nz = plan.nx, plan.ny, plan.nz
    step = step_of(sums)
    x_low = hx[0, 0] + step * side(plan, "gx", dxa[...], dxb[...], False)
    x_top = hx[1, 0] + step * side(plan, "gx", dxa[...], dxb[...], True)
    ph[0] = hy[0, 0] + step * side(plan, "gy", dya[...], dyb[...], False)
    ph[1] = hy[1, 0] + step * side(plan, "gy", dya[...], dyb[...], True)
    fh[0] = hy[0, 1]
    fh[1] = hy[1, 1]
    row, lane = rows_of((ny, nz)), lanes_of((ny, nz))

    def layer(i, carry):
        p, g = carry
        k = jnp.minimum(i + 1, nx - 1)
        p_next = jnp.where(i == nx - 1, x_top, press[k] + step * direction[k])
        g_next = tx[i + 1] * (p - p_next)
        gx[i + 1] = g_next
        cells = pl.ds(i * ny, ny)
        y_last = jnp.where(row == 0, ph[0, pl.ds(i, 1), :], ahead(p, 0))
        y_next = jnp.where(row == ny - 1, ph[1, pl.ds(i, 1), :], back(p, 0))
        z_low = hz[cells, 0:1] + step * dhz[0][cells, :]
        z_top = hz[cells, 1:2] + step * dhz[-1][cells, :]
        z_last = jnp.where(lane == 0, z_low, ahead(p, 1))
        z_next = jnp.where(lane == nz - 1, z_top, back(p, 1))
        parts = (
            (gy_low, ty_low[i] * (y_last - p), -1.0),
            (gy_top, ty_top[i] * (p - y_next), 1.0),
            (gz_low, tz_low[i] * (z_last - p), -1.0),
            (gz_top, tz_top[i] * (p - z_next), 1.0),
        )
        total = jnp.maximum(g_next, 0.0) - jnp.minimum(g, 0.0)
        for ref, value, sign in parts:
            ref[i] = value
            if sign > 0:
                total = total + jnp.maximum(value, 0.0)
            else:
                total = total - jnp.minimum(value, 0.0)
        outflow[i] = total
        return p_next, g_next

    p0 = press[0] + step * direction[0]
    g0 = tx[0] * (x_low - p0)
    gx[0] = g0
    lax.fori_loop(0, nx, layer, (p0, g0), unroll=4)

    def z_at(i):
        cells = pl.ds(i * ny, ny)
        return hz[cells, 2:3], hz[cells, 3:4]

    sweep(
        plan, True,
        (sat, sat, frac, coef, rate, inject, gx, gy_low, gy_top, gz_low, gz_top, outflow),
        hx[0, 1], hx[1, 1], fh, z_at, keep(plan, s_new, f_new, tile),
    )
    pack_all(plan, f_new, tile, packs)


def later_kernel(plan, last_sweep, *refs):
    n_msg = len(plan.z_msgs)
    fields = refs[:12]
    xa, xb, ya, yb = refs[12:16]
    got = refs[16 : 16 + n_msg]
    rest = refs[17 + n_msg :]
    if last_sweep:
        out, new, sem, fh, *hz = rest

        def done(i, s, c):
            new[i] = s
            write_out(plan, i, new, out, sem)
    else:
        new, new_frac = rest[:2]
        packs = rest[2 : 6 + n_msg]
        tile, fh, *hz = rest[6 + n_msg :]
        done = keep(plan, new, new_frac, tile)
    ny = plan.ny
    spread(plan, got, hz)
    fh[0] = side(plan, "gy", ya[...], yb[...], False)
    fh[1] = side(plan, "gy", ya[...], yb[...], True)

    def z_at(i):
        cells = pl.ds(i * ny, ny)
        return hz[0][cells, :], hz[-1][cells, :]

    sweep(
        plan, False, fields,
        side(plan, "gx", xa[...], xb[...], False), side(plan, "gx", xa[...], xb[...], True),
        fh, z_at, done,
    )
    if last_sweep:
        write_end(plan, new, out, sem)
    else:
        pack_all(plan, new_frac, tile, packs)


def per_device(
    counts, pressure, source, saturation, permeability, compress, porosity, rock_type, well_mask, oil_factor
):
    nx, ny, nz = pressure.shape
    wide = INTERSECTION
    plan = Plan(nx, ny, nz, counts)
    n_msg = len(plan.z_msgs)
    n_dev = counts["gx"] * counts["gy"] * counts["gz"]
    cells = nx * ny
    my, mz = ny + 2 * wide, nz + 2 * wide
    table_y, eigen_y = sine_basis(my)
    table_z, eigen_z = sine_basis(mz)
    factors, middle = sweep_factors(wide + nx // 2, eigen_y, eigen_z)
    const = lambda v: jnp.asarray(v, F32)
    factors, middle = const(factors), const(middle)
    rim = np.zeros((2, MSG_ROWS, mz))
    rim[0, :wide] = table_z[:wide]
    rim[0, wide] = table_z[wide]
    rim[1, :wide] = table_z[mz - wide :]
    rim[1, wide] = table_z[mz - wide - 1]

    def parts(v):
        v = np.asarray(v, np.float32)
        top = v.astype(jnp.bfloat16)
        return top, (v - top.astype(np.float32)).astype(jnp.bfloat16)

    def left(v):
        top, low = parts(v)
        return jnp.asarray(np.concatenate([top, top, low], axis=1))

    def right(v):
        top, low = parts(v)
        return jnp.asarray(np.concatenate([top, top, low], axis=0))

    rims = [jnp.concatenate([right(v)], axis=0).astype(F32) for v in rim]

    def swap(axis, a, b):
        return (
            lax.ppermute(a, axis, plan.perm(axis, 0)),
            lax.ppermute(b, axis, plan.perm(axis, 1)),
        )

    def swap_z(msgs):
        return [lax.ppermute(v, "gz", plan.perm("gz", q)) for q, v in zip(plan.z_msgs, msgs)]

    full_shape = (nx, ny, nz)
    x_face, y_face, z_face = (ny, nz), (nx, nz), (cells // 128, 128)
    face_shapes = [x_face, x_face, y_face, y_face] + [z_face] * n_msg
    tile = (2, 128, nz)
    spreads = [(cells, 128)] * n_msg
    dma = pltpu.SemaphoreType.DMA

    def exchange(packs):
        z = swap_z(packs[4:])
        y = swap("gy", packs[2], packs[3])
        x = swap("gx", packs[0], packs[1])
        return [*x, *y, *z]

    press, sat, mob, coef, frac, xa, xb, ya, yb, total = call(
        functools.partial(mobility_kernel, plan),
        [full_shape] * 5 + [(3,) + x_face] * 2 + [(3,) + y_face] * 2 + [x_face],
        (pressure, saturation, permeability, rock_type, oil_factor),
        hbm=(0, 1, 2, 3, 4),
        scratch=[full_shape, pltpu.VMEM(full_shape, jnp.int32),
                 pltpu.SMEM(oil_factor.shape, F32), dma((CHUNKS, 4)), dma],
    )
    ya, yb = swap("gy", ya, yb)
    xa, xb = swap("gx", xa, xb)
    res, tx, ty, tz, diag = call(
        functools.partial(inner_kernel, plan),
        [full_shape] * 5,
        (press, mob, source, compress, well_mask),
    )
    res, *sent = call(
        functools.partial(rim_kernel, plan),
        [full_shape] + [(MSG_ROWS, cells)] * n_msg,
        (res, press, mob, frac, xa, xb, ya, yb),
        scratch=[(cells, nz)],
        aliases={0: 0},
    )
    got = swap_z(sent)
    tx, ty_low, ty_top, hx, hy = call(
        functools.partial(faces_xy_kernel, plan),
        [(nx + 1, ny, nz)] + [full_shape] * 2 + [(2, 2) + x_face, (2, 2) + y_face],
        (mob, tx, ty, xa, xb, ya, yb),
        scratch=[(2,) + y_face],
    )
    spec, sa, sb = call(
        functools.partial(z_kernel, plan, n_msg),
        [(nx, ny, mz)] + [(nx + nx * 2 * wide // 128, wide, nz)] * 2,
        (res, right(table_z[wide : wide + nz]), *rims, hx, *sent, *got),
    )
    sa, sb = swap("gy", sa, sb)
    full, tz_low, tz_top, hz, rate, inject = call(
        functools.partial(faces_z_kernel, plan, n_msg),
        [full_shape] * 3 + [(cells, 128)] + [full_shape] * 2,
        (res, tz, porosity, well_mask, *sent, *got),
    )
    modes, ma, mb = call(
        functools.partial(y_kernel, plan),
        [(nx, my, mz), (my + 8, nz), (my + 8, nz)],
        (spec, sa, sb, left(table_y), factors, hz),
    )
    ma, mb = swap("gx", ma, mb)
    direction, *packs = call(
        functools.partial(solve_kernel, plan),
        [full_shape] + face_shapes,
        (modes, ma, mb, factors, middle, left(table_y[wide : wide + ny]),
         jnp.asarray(np.stack(parts(table_z[:, wide : wide + nz]))), total),
        scratch=[(cells, mz), tile],
    )
    dhalo = exchange(packs)
    image, sums, *dhz = call(
        functools.partial(image_kernel, plan, n_dev),
        [full_shape, (n_dev, 128)] + spreads,
        (direction, diag, full, tx, ty_low, ty_top, tz_low, tz_top, *dhalo),
        scratch=[(2,) + y_face],
    )
    sums = lax.all_to_all(sums, AXES, 0, 0, tiled=True)
    outs = call(
        functools.partial(step_kernel, plan),
        [full_shape] * 2 + [(nx + 1, ny, nz)] + [full_shape] * 5 + face_shapes,
        (sums, press, direction, tx, ty_low, ty_top, tz_low, tz_top,
         hx, hy, hz, *dhalo[:4], *dhz, sat, frac, coef, rate, inject),
        scratch=[(2,) + y_face] * 2 + [tile],
        limit=40,
    )
    current, frac, *flows = outs[:8]
    packs = outs[8:]
    p_new, r_new, token = call(
        functools.partial(output_kernel, plan),
        [full_shape] * 2 + [(8, 128)],
        (sums, press, direction, full, image),
        hbm_out=(0, 1),
        scratch=[full_shape] * 2 + [dma((CHUNKS,))] * 2,
    )
    for sweep_index in range(1, NEWTON):
        halo = exchange(packs)
        last_sweep = sweep_index == NEWTON - 1
        outs = call(
            functools.partial(later_kernel, plan, last_sweep),
            [full_shape] if last_sweep else [full_shape] * 2 + face_shapes,
            (sat, current, frac, coef, rate, inject, *flows, *halo, token),
            scratch=([full_shape, dma((CHUNKS,))] if last_sweep else [tile])
            + [(2,) + y_face] + spreads,
            hbm_out=(0,) if last_sweep else (),
        )
        current = outs[0]
        if not last_sweep:
            frac, packs = outs[1], outs[2:]
    return p_new, r_new, current


def solution(mesh):
    spec = P(*AXES)
    return jax.shard_map(
        functools.partial(per_device, dict(mesh.shape)),
        mesh=mesh,
        in_specs=(spec,) * 8 + (P(),),
        out_specs=(spec,) * 3,
        check_vma=False,
    )
```

```python
import functools
import math

import jax
import jax.numpy as jnp
import numpy as np
from jax import lax
from jax.experimental import pallas as pl
from jax.experimental.pallas import tpu as pltpu
from jax.sharding import PartitionSpec as P


INTERSECTION = 8
NEWTON = 3

WELL_INDEX = 4.0
INJECT_RATE = 2.0
TIME_STEP = 0.05

AXES = ("gx", "gy", "gz")
F32 = jnp.float32
MSG_ROWS = 16
CHUNKS = 4


def sine_basis(length):
    points = np.arange(length) + 1
    angles = np.outer(points, points) % (2 * (length + 1)) * (math.pi / (length + 1))
    table = math.sqrt(2.0 / (length + 1)) * np.sin(angles)
    eigen = 2.0 - 2.0 * np.cos(points * (math.pi / (length + 1)))
    return table, eigen


def sweep_factors(count, skip, eigen_y, eigen_z):
    shift = 2.0 + eigen_y[:, None] + eigen_z[None, :]
    factors = []
    last = np.zeros_like(shift)
    for _ in range(count):
        last = 1.0 / (shift - last)
        factors.append(last)
    factors = np.stack(factors)
    reach = np.cumprod(factors[skip:], axis=0)
    return factors, reach, 1.0 / (1.0 - last * last)


def pairs(count, periodic, parity):
    if periodic and count % 2:
        step = 1 if parity == 0 else -1
        return [(i, (i + step) % count) for i in range(count)]
    out = []
    for i in range(parity, count, 2):
        j = i + 1
        if periodic:
            j = j % count
        if j < count:
            out += [(i, j), (j, i)]
    return out


def harmonic(one, two):
    return 2.0 * one * two / (one + two)


def rows_of(shape):
    return lax.broadcasted_iota(jnp.int32, shape, 0)


def lanes_of(shape):
    return lax.broadcasted_iota(jnp.int32, shape, 1)


def back(value, axis):
    return pltpu.roll(value, value.shape[axis] - 1, axis)


def ahead(value, axis):
    return pltpu.roll(value, 1, axis)


class Plan:
    def __init__(self, nx, ny, nz, counts):
        self.nx, self.ny, self.nz = nx, ny, nz
        self.counts = counts
        self.z_msgs = [q for q in (0, 1) if pairs(counts["gz"], False, q)]

    def perm(self, axis, which):
        return pairs(self.counts[axis], axis != "gz", which)

    def high(self, axis, which):
        if axis != "gz" and self.counts[axis] % 2:
            return (which == 0, which == 1)
        up = (lax.axis_index(axis) % 2) == which
        return (up, up)


def call(kernel, outs, args, scratch=(), aliases=None, hbm=(), hbm_out=(), limit=28):
    def spec(k, remote):
        return pl.BlockSpec(memory_space=pltpu.HBM if k in remote else pltpu.VMEM)

    args = [
        pltpu.with_memory_space_constraint(v, pltpu.HBM) if k in hbm else v
        for k, v in enumerate(args)
    ]
    return pl.pallas_call(
        kernel,
        out_shape=[jax.ShapeDtypeStruct(s, F32) for s in outs],
        in_specs=[spec(k, hbm) for k in range(len(args))],
        out_specs=[spec(k, hbm_out) for k in range(len(outs))],
        scratch_shapes=[pltpu.VMEM(v, F32) if isinstance(v, tuple) else v for v in scratch],
        input_output_aliases=aliases or {},
        compiler_params=pltpu.CompilerParams(vmem_limit_bytes=limit << 20),
    )(*args)


def halves(value):
    top = value.astype(jnp.bfloat16)
    return top, (value - top.astype(F32)).astype(jnp.bfloat16)


def mxu(one, two, dims=((1,), (0,))):
    return lax.dot_general(one, two, (dims, ((), ())), preferred_element_type=F32)


def side(plan, axis, ref_a, ref_b, high):
    a_high = plan.high(axis, 0)[1]
    if high:
        return jnp.where(a_high, ref_a, ref_b)
    return jnp.where(a_high, ref_b, ref_a)


def pack_x(plan, ref, out_a, out_b):
    last = plan.nx - 1
    for which, out in ((0, out_a), (1, out_b)):
        out[...] = ref[jnp.where(plan.high("gx", which)[0], last, 0)]


def pack_y(plan, ref, out_a, out_b):
    low, top = ref[:, 0, :], ref[:, plan.ny - 1, :]
    for which, out in ((0, out_a), (1, out_b)):
        out[...] = jnp.where(plan.high("gy", which)[0], top, low)


def tile_put(plan, tile, i, q, value):
    group = 128 // plan.ny
    r = i // group
    rows = pl.ds((i % group) * plan.ny, plan.ny)
    moved = pltpu.roll(value, r + plan.high("gz", q)[0].astype(jnp.int32), 1)
    tile[q, rows, :] = jnp.where(lanes_of(value.shape) == r, moved, tile[q, rows, :])


def tile_out(plan, tile, outs):
    for q, out in zip(plan.z_msgs, outs):
        out[...] = jnp.transpose(tile[q])[: out.shape[0], :]


def spread(plan, gots, outs):
    vals = [got[...] for got in gots]
    if len(vals) > 1:
        vals = list(z_sides(plan, vals))
    for val, out in zip(vals, outs):
        turned = jnp.transpose(val)
        for r in range(val.shape[0]):
            out[r * 128 : (r + 1) * 128, :] = jnp.broadcast_to(turned[:, r : r + 1], (128, 128))


def stack_rows(parts):
    cells = parts[0].shape[1]
    row = rows_of((8, cells))
    out = jnp.zeros((8, cells), F32)
    for k, part in enumerate(parts):
        out = jnp.where(row == k, jnp.broadcast_to(part, (8, cells)), out)
    return out


def z_sides(plan, vals):
    low, top = jnp.zeros_like(vals[0]), jnp.zeros_like(vals[0])
    for q, val in zip(plan.z_msgs, vals):
        up = plan.high("gz", q)[1]
        low = low + jnp.where(up, 0.0, val)
        top = top + jnp.where(up, val, 0.0)
    return low, top


def mobility_kernel(
    plan, press_in, sat_in, perm_in, rock_in, oil_in,
    press, sat, mob, coef, frac, xa, xb, ya, yb, total, perm, rock, oil, sem, oil_sem,
):
    kinds = oil.shape[0]
    oil_move = pltpu.make_async_copy(oil_in, oil, oil_sem)
    oil_move.start()
    size = plan.nx // CHUNKS
    moves = []
    for c in range(CHUNKS):
        cut = pl.ds(c * size, size)
        for k, (src, dst) in enumerate(
            ((sat_in, sat), (rock_in, rock), (perm_in, perm), (press_in, press))
        ):
            move = pltpu.make_async_copy(src.at[cut], dst.at[cut], sem.at[c, k])
            move.start()
            moves.append(move)

    def layer(i, acc):
        s, kind = sat[i], rock[i]
        c = jnp.full(s.shape, oil[0], F32)
        for k in range(1, kinds):
            c = jnp.where(kind == k, oil[k], c)
        water, rest = s * s, 1.0 - s
        den = water + c * rest * rest
        m = perm[i] * den
        coef[i] = c
        mob[i] = m
        frac[i] = water / den
        return acc + m

    acc = jnp.zeros((plan.ny, plan.nz), F32)
    oil_move.wait()
    for c in range(CHUNKS):
        for move in moves[4 * c : 4 * c + 3]:
            move.wait()
        acc = lax.fori_loop(c * size, (c + 1) * size, layer, acc, unroll=4)
    total[...] = acc
    for c in range(CHUNKS):
        moves[4 * c + 3].wait()
    for k, ref in enumerate((press, mob, frac)):
        pack_x(plan, ref, xa.at[k], xb.at[k])
        pack_y(plan, ref, ya.at[k], yb.at[k])


def inner_kernel(plan, press, mob, source, compress, well, res, tx, ty, tz, diag):
    shape = (plan.ny, plan.nz)
    row, lane = rows_of(shape), lanes_of(shape)

    def layer(i, carry):
        p_last, m_last, r_last = carry
        p, m = press[i], mob[i]
        t = harmonic(m_last, m)
        tx[i] = t
        flux_x = t * (p_last - p)
        t = harmonic(jnp.where(row == 0, 0.0, ahead(m, 0)), m)
        ty[i] = t
        flux_y = t * (ahead(p, 0) - p)
        t = harmonic(jnp.where(lane == 0, 0.0, ahead(m, 1)), m)
        tz[i] = t
        flux_z = t * (ahead(p, 1) - p)
        d = compress[i] + WELL_INDEX * well[i].astype(F32) * m
        diag[i] = d
        r = source[i] - d * p + flux_x + (flux_y - back(flux_y, 0)) + (flux_z - back(flux_z, 1))
        res[jnp.maximum(i - 1, 0)] = r_last - flux_x
        return p, m, r

    zero = jnp.zeros(shape, F32)
    res[plan.nx - 1] = lax.fori_loop(0, plan.nx, layer, (zero, zero, zero), unroll=4)[2]


def rim_kernel(plan, res_in, press, mob, frac, xa, xb, ya, yb, res, *rest):
    z_outs, comp = rest[:-1], rest[-1]
    nx, ny, nz = plan.nx, plan.ny, plan.nz
    last = nx - 1
    for high, k in ((False, 0), (True, last)):
        p, m = (side(plan, "gx", xa[f], xb[f], high) for f in (0, 1))
        res[k] = res[k] + harmonic(mob[k], m) * (p - press[k])
    for high, k in ((False, 0), (True, ny - 1)):
        p, m = (side(plan, "gy", ya[f], yb[f], high) for f in (0, 1))
        res[:, k, :] = res[:, k, :] + harmonic(mob[:, k, :], m) * (p - press[:, k, :])
    lane = lanes_of((ny, nz))
    wide = INTERSECTION
    for q, out in zip(plan.z_msgs, z_outs):
        up = plan.high("gz", q)[0].astype(jnp.int32)

        def layer(i, carry):
            acc = pltpu.roll(res[i], up * wide, 1)
            for k, ref in enumerate((press, mob, frac)):
                acc = jnp.where(lane < wide + k, acc, pltpu.roll(ref[i], wide + k + up, 1))
            comp[pl.ds(i * ny, ny), :] = acc
            return carry

        lax.fori_loop(0, nx, layer, 0, unroll=4)
        for k in range(nx * ny // 128):
            cut = slice(k * 128, (k + 1) * 128)
            out[:, cut] = jnp.transpose(comp[cut, :])[:MSG_ROWS, :]


def z_flux(sent, got):
    wide = INTERSECTION
    out = []
    for own, other in zip(sent, got):
        t = harmonic(own[wide + 1 : wide + 2, :], other[wide + 1 : wide + 2, :])
        q = t * (other[wide : wide + 1, :] - own[wide : wide + 1, :])
        out.append((other[wide : wide + 1, :], other[wide + 2 : wide + 3, :], t, q))
    return out


def z_kernel(plan, n_msg, res, basis, rim_low, rim_top, order, *rest):
    sent, got = rest[:n_msg], rest[n_msg : 2 * n_msg]
    spec, ya, yb = rest[2 * n_msg :]
    nx, ny, nz = plan.nx, plan.ny, plan.nz
    wide = INTERSECTION
    mixes, rims = [], []
    for q, other, (_, _, _, flux) in zip(plan.z_msgs, got, z_flux(sent, got)):
        up = plan.high("gz", q)[1]
        row = rows_of(other.shape)
        near = jnp.where(up, 0, wide - 1)
        flux = jnp.broadcast_to(flux, other.shape)
        mix = jnp.where(row < wide, other[...], 0.0)
        mix = jnp.where(row == near, mix - flux, mix)
        mix = jnp.where(row == wide, flux, mix)
        top, low = halves(mix)
        mixes.append(jnp.concatenate([top, low, top], axis=0))
        rims.append(jnp.where(up, rim_top[...], rim_low[...]).astype(jnp.bfloat16))
    group = 128 // ny
    for k in range(nx // group):
        value = res[k * group : (k + 1) * group].reshape(128, nz)
        top, low = halves(value)
        out = mxu(jnp.concatenate([top, low, top], axis=1), basis[...])
        for mix, rim in zip(mixes, rims):
            out = out + mxu(mix[:, k * 128 : (k + 1) * 128], rim, ((0,), (0,)))
        spec[k * group : (k + 1) * group] = out.reshape(group, ny, out.shape[1])
    tail = 2 * wide
    per = 128 // tail
    for which, ref in ((0, ya), (1, yb)):
        start = jnp.where(plan.high("gy", which)[0], ny - wide, 0)
        rows = pl.ds(pl.multiple_of(start, 8), wide)
        ref[:nx] = spec[:, rows, :nz]
        for g in range(nx // per):
            ref[nx + g] = jnp.concatenate(
                [spec[g * per + j, rows, nz:] for j in range(per)], axis=1
            )


def faces_xy_kernel(
    plan, mob, press, sat, coef, poro, well, tx_in, ty_in, xa, xb, ya, yb,
    tx, ty_low, ty_top, gx, gy_low, gy_top, hx, hy, rate, inject, square, pull, push, ty_rim,
):
    nx, ny, nz = plan.nx, plan.ny, plan.nz
    for k, high in ((0, False), (1, True)):
        for f, field in ((0, 0), (1, 2)):
            hx[k, f] = side(plan, "gx", xa[field], xb[field], high)
            hy[k, f] = side(plan, "gy", ya[field], yb[field], high)
    ty_rim[0] = harmonic(mob[:, 0, :], side(plan, "gy", ya[1], yb[1], False))
    ty_rim[1] = harmonic(mob[:, ny - 1, :], side(plan, "gy", ya[1], yb[1], True))
    row = rows_of((ny, nz))
    t_first = harmonic(mob[0], side(plan, "gx", xa[1], xb[1], False))

    def layer(i, p_last):
        p = press[i]
        t = jnp.where(i == 0, t_first, tx_in[i])
        tx[i] = t
        gx[i] = t * (p_last - p)
        t = ty_in[i]
        low = jnp.where(row == 0, ty_rim[0, pl.ds(i, 1), :], t)
        top = jnp.where(row == ny - 1, ty_rim[1, pl.ds(i, 1), :], back(t, 0))
        ty_low[i] = low
        ty_top[i] = top
        y_last = jnp.where(row == 0, hy[0, 0, pl.ds(i, 1), :], ahead(p, 0))
        y_next = jnp.where(row == ny - 1, hy[1, 0, pl.ds(i, 1), :], back(p, 0))
        gy_low[i] = low * (y_last - p)
        gy_top[i] = top * (p - y_next)
        speed = poro[i] / TIME_STEP
        s, c = sat[i], coef[i]
        rest = 1.0 - s
        part = c * rest
        den = s * s + part * rest
        den = den * den
        rate[i] = speed
        inject[i] = INJECT_RATE * well[i].astype(F32)
        square[i] = den
        pull[i] = speed * den
        push[i] = jnp.abs(2.0 * part * s)
        return p

    p = lax.fori_loop(0, nx, layer, hx[0, 0], unroll=4)
    t = harmonic(mob[nx - 1], side(plan, "gx", xa[1], xb[1], True))
    tx[nx] = t
    gx[nx] = t * (p - hx[1, 0])


def faces_z_kernel(plan, n_msg, res, press, tz_in, *rest):
    sent, got = rest[:n_msg], rest[n_msg : 2 * n_msg]
    full, tz_low, tz_top, gz_low, gz_top = rest[2 * n_msg : 2 * n_msg + 5]
    fz, hz = rest[2 * n_msg + 5 : -1], rest[-1]
    nx, ny, nz = plan.nx, plan.ny, plan.nz
    parts = z_flux(sent, got)
    split = [z_sides(plan, [part[k] for part in parts]) for k in range(4)]
    rows = stack_rows([v for pair in split for v in pair])
    for k in range(nx * ny // 128):
        cut = slice(k * 128, (k + 1) * 128)
        hz[cut, :8] = jnp.transpose(rows[:, cut])
    lane = lanes_of((ny, nz))

    def layer(i, carry):
        t, p = tz_in[i], press[i]
        cells = pl.ds(i * ny, ny)
        col = hz[cells, :8]
        in_low, in_top = col[:, 6:7], col[:, 7:8]
        tz_low[i] = jnp.where(lane == 0, col[:, 4:5], t)
        tz_top[i] = jnp.where(lane == nz - 1, col[:, 5:6], back(t, 1))
        g = t * (ahead(p, 1) - p)
        gz_low[i] = jnp.where(lane == 0, in_low, g)
        gz_top[i] = jnp.where(lane == nz - 1, -in_top, back(g, 1))
        flux = jnp.where(lane == 0, in_low, 0.0) + jnp.where(lane == nz - 1, in_top, 0.0)
        full[i] = res[i] + flux
        if len(fz) == 1:
            fz[0][cells, :] = jnp.broadcast_to(col[:, 2:3] + col[:, 3:4], (ny, nz))
        else:
            for k, out in enumerate(fz):
                out[cells, :] = jnp.broadcast_to(col[:, 2 + k : 3 + k], (ny, nz))
        return carry

    lax.fori_loop(0, nx, layer, 0, unroll=4)


def wide_rows(plan, msg_a, msg_b, i, high):
    nx = plan.nx
    tail = 2 * INTERSECTION
    per = 128 // tail
    ends = side(plan, "gy", msg_a[nx + i // per], msg_b[nx + i // per], high)
    ends = pltpu.roll(ends, (128 - (i % per) * tail) % 128, 1)[:, :tail]
    return jnp.concatenate([side(plan, "gy", msg_a[i], msg_b[i], high), ends], axis=1)


def thrice(value):
    top, low = halves(value)
    return jnp.concatenate([top, low, top], axis=0)


def fold(value, nz):
    rows, tail = value.shape[0], value.shape[1] - nz
    ends = jnp.concatenate(
        [value[k : k + 8, nz:] for k in range(0, rows, 8)]
        + [jnp.zeros((8, nz - rows // 8 * tail), F32)],
        axis=1,
    )
    return jnp.concatenate([value[:, :nz], ends], axis=0)


def unfold(value, tail):
    rows = value.shape[0] - 8
    ends = jnp.concatenate(
        [value[rows:, k * tail : (k + 1) * tail] for k in range(rows // 8)], axis=0
    )
    return jnp.concatenate([value[:rows], ends], axis=1)


def y_modes(plan, spec, ya, yb, basis, i):
    low = wide_rows(plan, ya, yb, i, False)
    top = wide_rows(plan, ya, yb, i, True)
    return mxu(basis[...], thrice(jnp.concatenate([low, spec[i], top], axis=0)))


def y_edge_kernel(plan, spec, ya, yb, basis, factors, order, edge, xa, xb):
    nx = plan.nx
    wide = INTERSECTION

    def layer(i, carry):
        edge[i] = y_modes(plan, spec, ya, yb, basis, jnp.where(i < wide, i, nx - 2 * wide + i))
        return carry

    lax.fori_loop(0, 2 * wide, layer, 0, unroll=4)
    low = jnp.zeros(edge.shape[1:], F32)
    top = low
    for k in range(wide):
        low = (edge[wide - 1 - k] + low) * factors[k]
        top = (edge[wide + k] + top) * factors[k]
    for which, out in ((0, xa), (1, xb)):
        out[...] = fold(jnp.where(plan.high("gx", which)[0], top, low), plan.nz)


def y_mid_kernel(plan, spec, ya, yb, basis, factors, edge, zed):
    nx = plan.nx
    wide = INTERSECTION

    def layer(i, carry):
        zed[i] = y_modes(plan, spec, ya, yb, basis, i)
        return carry

    lax.fori_loop(wide, nx - wide, layer, 0, unroll=4)

    def outer(k, carry):
        low, top = carry
        c = factors[wide + k]
        low = (edge[k] + low) * c
        top = (edge[2 * wide - 1 - k] + top) * c
        zed[k] = low
        zed[nx - 1 - k] = top
        return low, top

    def inner(k, carry):
        low, top = carry
        c = factors[wide + k]
        low = (zed[k] + low) * c
        top = (zed[nx - 1 - k] + top) * c
        zed[k] = low
        zed[nx - 1 - k] = top
        return low, top

    zero = jnp.zeros(edge.shape[1:], F32)
    carry = lax.fori_loop(0, wide, outer, (zero, zero), unroll=2)
    lax.fori_loop(wide, nx // 2, inner, carry, unroll=2)


def solve_kernel(
    plan, zed, xa, xb, factors, reach, middle, basis_y, basis_z, total, direction, *rest
):
    (dxa, dxb, dya, dyb), z_outs, (work, tile) = rest[:4], rest[4:-2], rest[-2:]
    nx, ny, nz = plan.nx, plan.ny, plan.nz
    wide = INTERSECTION
    half = nx // 2
    low_in = unfold(side(plan, "gx", xa[...], xb[...], False), 2 * wide)
    top_in = unfold(side(plan, "gx", xa[...], xb[...], True), 2 * wide)
    low = zed[half - 1] + reach[half - 1] * low_in
    top = zed[half] + reach[half - 1] * top_in
    c, mid = factors[wide + half - 1], middle[...]
    low, top = (low + c * top) * mid, (top + c * low) * mid

    def put(i, value):
        work[pl.ds(i * ny, ny), :] = mxu(basis_y[...], thrice(value))

    put(half - 1, low)
    put(half, top)

    def outward(k, carry):
        low, top = carry
        i = half - 2 - k
        c = factors[wide + i]
        far = reach[i]
        low = (zed[i] + far * low_in) + c * low
        top = (zed[nx - 1 - i] + far * top_in) + c * top
        put(i, low)
        put(nx - 1 - i, top)
        return low, top

    lax.fori_loop(0, half - 1, outward, (low, top), unroll=3)
    mean = jnp.sum(jnp.sum(total[...], axis=0, keepdims=True), axis=1, keepdims=True) / (
        nx * ny * nz
    )
    inverse = 1.0 / mean
    group = 128 // ny
    base_top, base_low = basis_z[0], basis_z[1]

    def lift(r, carry):
        high, rest_ = halves(work[pl.ds(r * 128, 128), :])
        value = mxu(high, base_top) + (mxu(rest_, base_top) + mxu(high, base_low))
        value = value * inverse
        direction[pl.ds(r * group, group)] = value.reshape(group, ny, nz)
        for q in plan.z_msgs:
            moved = pltpu.roll(value, r + plan.high("gz", q)[0].astype(jnp.int32), 1)
            tile[q] = jnp.where(lanes_of((128, nz)) == r, moved, tile[q])
        return carry

    lax.fori_loop(0, nx // group, lift, 0, unroll=2)
    pack_x(plan, direction, dxa, dxb)
    pack_y(plan, direction, dya, dyb)
    tile_out(plan, tile, z_outs)


def image_kernel(
    plan, n_dev, direction, diag, full, tx, ty_low, ty_top, tz_low, tz_top, xa, xb, ya, yb, *rest
):
    n_msg = len(plan.z_msgs)
    got = rest[:n_msg]
    image, sums, gx, gy_low, gy_top, gz_low, gz_top, hy = rest[n_msg : n_msg + 8]
    hz = rest[n_msg + 8 :]
    nx, ny, nz = plan.nx, plan.ny, plan.nz
    spread(plan, got, hz)
    hy[0] = side(plan, "gy", ya[...], yb[...], False)
    hy[1] = side(plan, "gy", ya[...], yb[...], True)
    row, lane = rows_of((ny, nz)), lanes_of((ny, nz))

    def layer(i, carry):
        d_last, im_last, rd, da = carry
        d = direction[i]
        flux = tx[i] * (d_last - d)
        gx[i] = flux
        cells = pl.ds(i * ny, ny)
        y_last = jnp.where(row == 0, hy[0, pl.ds(i, 1), :], ahead(d, 0))
        y_next = jnp.where(row == ny - 1, hy[1, pl.ds(i, 1), :], back(d, 0))
        z_last = jnp.where(lane == 0, hz[0][cells, :], ahead(d, 1))
        z_next = jnp.where(lane == nz - 1, hz[-1][cells, :], back(d, 1))
        im = diag[i] * d - flux
        for ref, g, sign in (
            (gy_low, ty_low[i] * (y_last - d), -1),
            (gy_top, ty_top[i] * (d - y_next), 1),
            (gz_low, tz_low[i] * (z_last - d), -1),
            (gz_top, tz_top[i] * (d - z_next), 1),
        ):
            ref[i] = g
            im = im + g if sign > 0 else im - g
        im_last = im_last + flux
        image[jnp.maximum(i - 1, 0)] = im_last
        rd = rd + full[i] * d
        da = da + jnp.where(i > 0, d_last, 0.0) * im_last
        return d, im, rd, da

    zero = jnp.zeros((ny, nz), F32)
    low = side(plan, "gx", xa[...], xb[...], False)
    top = side(plan, "gx", xa[...], xb[...], True)
    d, im, rd, da = lax.fori_loop(0, nx, layer, (low, zero, zero, zero), unroll=4)
    flux = tx[nx] * (d - top)
    gx[nx] = flux
    im = im + flux
    image[nx - 1] = im
    da = da + d * im
    lane = lanes_of((n_dev, 128))
    sums[...] = jnp.where(lane < 64, jnp.sum(rd), jnp.sum(da))


def upwind(g, low, high):
    return g * jnp.where(g > 0.0, low, high)


def sweep(plan, refs, x_low, x_top, hy, z_at, done):
    nx, ny, nz = plan.nx, plan.ny, plan.nz
    (start, now, frac, coef, rate, inject, gx, gy_low, gy_top, gz_low, gz_top, outflow) = refs
    row, lane = rows_of((ny, nz)), lanes_of((ny, nz))

    def layer(i, carry):
        f, flow = carry
        f_next = jnp.where(i == nx - 1, x_top, frac[jnp.minimum(i + 1, nx - 1)])
        s, c = now[i], coef[i]
        flow_next = upwind(gx[i + 1], f, f_next)
        y_last = jnp.where(row == 0, hy[0, pl.ds(i, 1), :], ahead(f, 0))
        y_next = jnp.where(row == ny - 1, hy[1, pl.ds(i, 1), :], back(f, 0))
        z_low, z_top = z_at(i)
        z_last = jnp.where(lane == 0, z_low, ahead(f, 1))
        z_next = jnp.where(lane == nz - 1, z_top, back(f, 1))
        bal = (
            (flow_next - flow)
            + (upwind(gy_top[i], f, y_next) - upwind(gy_low[i], y_last, f))
            + (upwind(gz_top[i], f, z_next) - upwind(gz_low[i], z_last, f))
            + (rate[i] * (s - start[i]) - inject[i])
        )
        rest = 1.0 - s
        part = c * rest
        den = s * s + part * rest
        square = den * den
        slope = 2.0 * part * s
        s = s - bal * square / (rate[i] * square + outflow[i] * jnp.abs(slope))
        done(i, s, c)
        return f_next, flow_next

    f0 = frac[0]
    lax.fori_loop(0, nx, layer, (f0, upwind(gx[0], x_low, f0)), unroll=4)


def keep(plan, new, new_frac, tile):
    def done(i, s, c):
        new[i] = s
        water, rest = s * s, 1.0 - s
        f = water / (water + c * rest * rest)
        new_frac[i] = f
        for q in plan.z_msgs:
            tile_put(plan, tile, i, q, f)

    return done


def pack_all(plan, ref, tile, outs):
    xa, xb, ya, yb = outs[:4]
    pack_x(plan, ref, xa, xb)
    pack_y(plan, ref, ya, yb)
    tile_out(plan, tile, outs[4:])


def step_of(sums):
    both = jnp.sum(sums[...], axis=0, keepdims=True)
    return both[:, 0:1] / both[:, 64:65]


def write_out(plan, i, ref, out, sem):
    size = plan.nx // CHUNKS

    @pl.when(i % size == size - 1)
    def _():
        c = i // size
        cut = pl.ds(c * size, size)
        pltpu.make_async_copy(ref.at[cut], out.at[cut], sem.at[c]).start()


def write_end(plan, ref, out, sem):
    size = plan.nx // CHUNKS
    for c in range(CHUNKS):
        cut = pl.ds(c * size, size)
        pltpu.make_async_copy(ref.at[cut], out.at[cut], sem.at[c]).wait()


def output_kernel(plan, sums, press, direction, full, image, p_out, r_out, token, p_new, r_new, p_sem, r_sem):
    step = step_of(sums)

    def layer(i, carry):
        p_new[i] = press[i] + step * direction[i]
        write_out(plan, i, p_new, p_out, p_sem)
        r_new[i] = full[i] - step * image[i]
        write_out(plan, i, r_new, r_out, r_sem)
        return carry

    lax.fori_loop(0, plan.nx, layer, 0, unroll=4)
    token[...] = jnp.zeros(token.shape, F32)
    write_end(plan, p_new, p_out, p_sem)
    write_end(plan, r_new, r_out, r_sem)


def step_kernel(plan, *refs):
    n_msg = len(plan.z_msgs)
    sums, still, move = refs[0], refs[1:6], refs[6:11]
    (sat, frac, coef, inject, square, pull, push, hx, hy) = refs[11:20]
    fz = refs[20 : 20 + n_msg]
    outs = refs[20 + n_msg :]
    (s_new, f_new, gx, gy_low, gy_top, gz_low, gz_top, outflow) = outs[:8]
    packs = outs[8 : 12 + n_msg]
    tile = outs[-1]
    nx, ny, nz = plan.nx, plan.ny, plan.nz
    step = step_of(sums)
    row, lane = rows_of((ny, nz)), lanes_of((ny, nz))
    done = keep(plan, s_new, f_new, tile)

    def flux(k, i):
        return still[k][i] + step * move[k][i]

    def layer(i, carry):
        f, g, flow = carry
        f_next = jnp.where(i == nx - 1, hx[1, 1], frac[jnp.minimum(i + 1, nx - 1)])
        g_next = flux(0, i + 1)
        gx[i + 1] = g_next
        flow_next = upwind(g_next, f, f_next)
        out = jnp.maximum(g_next, 0.0) - jnp.minimum(g, 0.0)
        bal = flow_next - flow - inject[i]
        cells = pl.ds(i * ny, ny)
        y_last = jnp.where(row == 0, hy[0, 1, pl.ds(i, 1), :], ahead(f, 0))
        y_next = jnp.where(row == ny - 1, hy[1, 1, pl.ds(i, 1), :], back(f, 0))
        z_last = jnp.where(lane == 0, fz[0][cells, :], ahead(f, 1))
        z_next = jnp.where(lane == nz - 1, fz[-1][cells, :], back(f, 1))
        for k, ref, other, low in (
            (1, gy_low, y_last, True),
            (2, gy_top, y_next, False),
            (3, gz_low, z_last, True),
            (4, gz_top, z_next, False),
        ):
            value = flux(k, i)
            ref[i] = value
            if low:
                out = out - jnp.minimum(value, 0.0)
                bal = bal - upwind(value, other, f)
            else:
                out = out + jnp.maximum(value, 0.0)
                bal = bal + upwind(value, f, other)
        outflow[i] = out
        done(i, sat[i] - bal * square[i] / (pull[i] + out * push[i]), coef[i])
        return f_next, g_next, flow_next

    f0, g0 = frac[0], flux(0, 0)
    gx[0] = g0
    lax.fori_loop(0, nx, layer, (f0, g0, upwind(g0, hx[0, 1], f0)), unroll=4)
    pack_all(plan, f_new, tile, packs)


def later_kernel(plan, last_sweep, *refs):
    n_msg = len(plan.z_msgs)
    fields = refs[:12]
    xa, xb, ya, yb = refs[12:16]
    got = refs[16 : 16 + n_msg]
    rest = refs[17 + n_msg :]
    if last_sweep:
        out, new, sem, fh, *hz = rest

        def done(i, s, c):
            new[i] = s
            write_out(plan, i, new, out, sem)
    else:
        new, new_frac = rest[:2]
        packs = rest[2 : 6 + n_msg]
        tile, fh, *hz = rest[6 + n_msg :]
        done = keep(plan, new, new_frac, tile)
    ny = plan.ny
    spread(plan, got, hz)
    fh[0] = side(plan, "gy", ya[...], yb[...], False)
    fh[1] = side(plan, "gy", ya[...], yb[...], True)

    def z_at(i):
        cells = pl.ds(i * ny, ny)
        return hz[0][cells, :], hz[-1][cells, :]

    sweep(
        plan, fields,
        side(plan, "gx", xa[...], xb[...], False), side(plan, "gx", xa[...], xb[...], True),
        fh, z_at, done,
    )
    if last_sweep:
        write_end(plan, new, out, sem)
    else:
        pack_all(plan, new_frac, tile, packs)


def per_device(
    counts, pressure, source, saturation, permeability, compress, porosity, rock_type, well_mask, oil_factor
):
    nx, ny, nz = pressure.shape
    wide = INTERSECTION
    plan = Plan(nx, ny, nz, counts)
    n_msg = len(plan.z_msgs)
    n_dev = counts["gx"] * counts["gy"] * counts["gz"]
    cells = nx * ny
    my, mz = ny + 2 * wide, nz + 2 * wide
    table_y, eigen_y = sine_basis(my)
    table_z, eigen_z = sine_basis(mz)
    factors, reach, middle = sweep_factors(wide + nx // 2, wide, eigen_y, eigen_z)
    const = lambda v: jnp.asarray(v, F32)
    factors, reach, middle = const(factors), const(reach), const(middle)
    rim = np.zeros((2, MSG_ROWS, mz))
    rim[0, :wide] = table_z[:wide]
    rim[0, wide] = table_z[wide]
    rim[1, :wide] = table_z[mz - wide :]
    rim[1, wide] = table_z[mz - wide - 1]

    def parts(v):
        v = np.asarray(v, np.float32)
        top = v.astype(jnp.bfloat16)
        return top, (v - top.astype(np.float32)).astype(jnp.bfloat16)

    def left(v):
        top, low = parts(v)
        return jnp.asarray(np.concatenate([top, top, low], axis=1))

    def right(v):
        top, low = parts(v)
        return jnp.asarray(np.concatenate([top, top, low], axis=0))

    rims = [jnp.concatenate([right(v)], axis=0).astype(F32) for v in rim]

    def send(value, axis, which):
        return lax.ppermute(value, axis, plan.perm(axis, which))

    def swap(axis, a, b):
        return send(a, axis, 0), send(b, axis, 1)

    def swap_z(msgs):
        return [send(v, "gz", q) for q, v in zip(plan.z_msgs, msgs)]

    full_shape = (nx, ny, nz)
    x_face, y_face, z_face = (ny, nz), (nx, nz), (cells // 128, 128)
    face_shapes = [x_face, x_face, y_face, y_face] + [z_face] * n_msg
    tile = (2, 128, nz)
    spreads = [(cells, 128)] * n_msg
    dma = pltpu.SemaphoreType.DMA

    def exchange(packs):
        z = swap_z(packs[4:])
        y = swap("gy", packs[2], packs[3])
        x = swap("gx", packs[0], packs[1])
        return [*x, *y, *z]

    press, sat, mob, coef, frac, xa, xb, ya, yb, total = call(
        functools.partial(mobility_kernel, plan),
        [full_shape] * 5 + [(3,) + x_face] * 2 + [(3,) + y_face] * 2 + [x_face],
        (pressure, saturation, permeability, rock_type, oil_factor),
        hbm=(0, 1, 2, 3, 4),
        scratch=[full_shape, pltpu.VMEM(full_shape, jnp.int32),
                 pltpu.SMEM(oil_factor.shape, F32), dma((CHUNKS, 4)), dma],
    )
    ya, yb = swap("gy", ya, yb)
    xa, xb = swap("gx", xa, xb)
    res, tx, ty, tz, diag = call(
        functools.partial(inner_kernel, plan),
        [full_shape] * 5,
        (press, mob, source, compress, well_mask),
    )
    res, *sent = call(
        functools.partial(rim_kernel, plan),
        [full_shape] + [(MSG_ROWS, cells)] * n_msg,
        (res, press, mob, frac, xa, xb, ya, yb),
        scratch=[(cells, nz)],
        aliases={0: 0},
    )
    got = swap_z(sent)
    tx, ty_low, ty_top, gx, gy_low, gy_top, hx, hy, rate, inject, square, pull, push = call(
        functools.partial(faces_xy_kernel, plan),
        [(nx + 1, ny, nz)] + [full_shape] * 2 + [(nx + 1, ny, nz)] + [full_shape] * 2
        + [(2, 2) + x_face, (2, 2) + y_face] + [full_shape] * 5,
        (mob, press, sat, coef, porosity, well_mask, tx, ty, xa, xb, ya, yb),
        scratch=[(2,) + y_face],
    )
    spec, sa, sb = call(
        functools.partial(z_kernel, plan, n_msg),
        [(nx, ny, mz)] + [(nx + nx * 2 * wide // 128, wide, nz)] * 2,
        (res, right(table_z[wide : wide + nz]), *rims, hx, *sent, *got),
    )
    sa, sb = swap("gy", sa, sb)
    full, tz_low, tz_top, gz_low, gz_top, *fz = call(
        functools.partial(faces_z_kernel, plan, n_msg),
        [full_shape] * 5 + spreads,
        (res, press, tz, *sent, *got),
        scratch=[(cells, 128)],
    )
    edge, ma, mb = call(
        functools.partial(y_edge_kernel, plan),
        [(2 * wide, my, mz), (my + 8, nz), (my + 8, nz)],
        (spec, sa, sb, left(table_y), factors, gz_low),
    )
    ma, mb = swap("gx", ma, mb)
    (zed,) = call(
        functools.partial(y_mid_kernel, plan),
        [(nx, my, mz)],
        (spec, sa, sb, left(table_y), factors, edge),
    )
    direction, *packs = call(
        functools.partial(solve_kernel, plan),
        [full_shape] + face_shapes,
        (zed, ma, mb, factors, reach, middle, left(table_y[wide : wide + ny]),
         jnp.asarray(np.stack(parts(table_z[:, wide : wide + nz]))), total),
        scratch=[(cells, mz), tile],
    )
    dhalo = exchange(packs)
    image, sums, *moves = call(
        functools.partial(image_kernel, plan, n_dev),
        [full_shape, (n_dev, 128), (nx + 1, ny, nz)] + [full_shape] * 4,
        (direction, diag, full, tx, ty_low, ty_top, tz_low, tz_top, *dhalo),
        scratch=[(2,) + y_face] + spreads,
    )
    sums = lax.all_to_all(sums, AXES, 0, 0, tiled=True)
    outs = call(
        functools.partial(step_kernel, plan),
        [full_shape] * 2 + [(nx + 1, ny, nz)] + [full_shape] * 5 + face_shapes,
        (sums, gx, gy_low, gy_top, gz_low, gz_top, *moves,
         sat, frac, coef, inject, square, pull, push, hx, hy, *fz),
        scratch=[tile],
        limit=40,
    )
    current, frac, *flows = outs[:8]
    packs = outs[8:]
    p_new, r_new, token = call(
        functools.partial(output_kernel, plan),
        [full_shape] * 2 + [(8, 128)],
        (sums, press, direction, full, image),
        hbm_out=(0, 1),
        scratch=[full_shape] * 2 + [dma((CHUNKS,))] * 2,
    )
    for sweep_index in range(1, NEWTON):
        halo = exchange(packs)
        last_sweep = sweep_index == NEWTON - 1
        outs = call(
            functools.partial(later_kernel, plan, last_sweep),
            [full_shape] if last_sweep else [full_shape] * 2 + face_shapes,
            (sat, current, frac, coef, rate, inject, *flows, *halo, token),
            scratch=([full_shape, dma((CHUNKS,))] if last_sweep else [tile])
            + [(2,) + y_face] + spreads,
            hbm_out=(0,) if last_sweep else (),
        )
        current = outs[0]
        if not last_sweep:
            frac, packs = outs[1], outs[2:]
    return p_new, r_new, current


def solution(mesh):
    spec = P(*AXES)

    def body(*args):
        return per_device(dict(mesh.shape), *args)

    return jax.shard_map(
        body,
        mesh=mesh,
        in_specs=(spec,) * 8 + (P(),),
        out_specs=(spec,) * 3,
        check_vma=False,
    )
```

```python
import functools
import math

import jax
import jax.numpy as jnp
import numpy as np
from jax import lax
from jax.experimental import pallas as pl
from jax.experimental.pallas import tpu as pltpu
from jax.sharding import PartitionSpec as P


INTERSECTION = 8
NEWTON = 3

WELL_INDEX = 4.0
INJECT_RATE = 2.0
TIME_STEP = 0.05

AXES = ("gx", "gy", "gz")
F32 = jnp.float32
MSG_ROWS = 16
CHUNKS = 4


def sine_basis(length):
    points = np.arange(length) + 1
    angles = np.outer(points, points) % (2 * (length + 1)) * (math.pi / (length + 1))
    table = math.sqrt(2.0 / (length + 1)) * np.sin(angles)
    eigen = 2.0 - 2.0 * np.cos(points * (math.pi / (length + 1)))
    return table, eigen


def sweep_factors(count, skip, eigen_y, eigen_z):
    shift = 2.0 + eigen_y[:, None] + eigen_z[None, :]
    factors = []
    last = np.zeros_like(shift)
    for _ in range(count):
        last = 1.0 / (shift - last)
        factors.append(last)
    factors = np.stack(factors)
    reach = np.cumprod(factors[skip:], axis=0)
    return factors, reach, 1.0 / (1.0 - last * last)


def pairs(count, periodic, parity):
    if periodic and count % 2:
        step = 1 if parity == 0 else -1
        return [(i, (i + step) % count) for i in range(count)]
    out = []
    for i in range(parity, count, 2):
        j = i + 1
        if periodic:
            j = j % count
        if j < count:
            out += [(i, j), (j, i)]
    return out


def harmonic(one, two):
    return 2.0 * one * two / (one + two)


def rows_of(shape):
    return lax.broadcasted_iota(jnp.int32, shape, 0)


def lanes_of(shape):
    return lax.broadcasted_iota(jnp.int32, shape, 1)


def back(value, axis):
    return pltpu.roll(value, value.shape[axis] - 1, axis)


def ahead(value, axis):
    return pltpu.roll(value, 1, axis)


def from_above(value, halo):
    first = rows_of((8, value.shape[1])) == 0
    fill = jnp.broadcast_to(halo, (8, value.shape[1]))
    tiles = []
    for k in range(0, value.shape[0], 8):
        turned = pltpu.roll(value[k : k + 8], 1, 0)
        tiles.append(jnp.where(first, fill, turned))
        fill = turned
    return jnp.concatenate(tiles, axis=0)


def from_below(value, halo):
    last = rows_of((8, value.shape[1])) == 7
    fill = jnp.broadcast_to(halo, (8, value.shape[1]))
    tiles = []
    for k in range(value.shape[0] - 8, -1, -8):
        turned = pltpu.roll(value[k : k + 8], 7, 0)
        tiles.append(jnp.where(last, fill, turned))
        fill = turned
    return jnp.concatenate(tiles[::-1], axis=0)


class Plan:
    def __init__(self, nx, ny, nz, counts):
        self.nx, self.ny, self.nz = nx, ny, nz
        self.counts = counts
        self.z_msgs = [q for q in (0, 1) if pairs(counts["gz"], False, q)]

    def perm(self, axis, which):
        return pairs(self.counts[axis], axis != "gz", which)

    def high(self, axis, which):
        if axis != "gz" and self.counts[axis] % 2:
            return (which == 0, which == 1)
        up = (lax.axis_index(axis) % 2) == which
        return (up, up)


def call(kernel, outs, args, scratch=(), aliases=None, hbm=(), hbm_out=(), limit=28):
    def spec(k, remote):
        return pl.BlockSpec(memory_space=pltpu.HBM if k in remote else pltpu.VMEM)

    args = [
        pltpu.with_memory_space_constraint(v, pltpu.HBM) if k in hbm else v
        for k, v in enumerate(args)
    ]
    return pl.pallas_call(
        kernel,
        out_shape=[jax.ShapeDtypeStruct(s, F32) for s in outs],
        in_specs=[spec(k, hbm) for k in range(len(args))],
        out_specs=[spec(k, hbm_out) for k in range(len(outs))],
        scratch_shapes=[pltpu.VMEM(v, F32) if isinstance(v, tuple) else v for v in scratch],
        input_output_aliases=aliases or {},
        compiler_params=pltpu.CompilerParams(vmem_limit_bytes=limit << 20),
    )(*args)


def halves(value):
    top = value.astype(jnp.bfloat16)
    return top, (value - top.astype(F32)).astype(jnp.bfloat16)


def mxu(one, two, dims=((1,), (0,))):
    return lax.dot_general(one, two, (dims, ((), ())), preferred_element_type=F32)


def side(plan, axis, ref_a, ref_b, high):
    a_high = plan.high(axis, 0)[1]
    if high:
        return jnp.where(a_high, ref_a, ref_b)
    return jnp.where(a_high, ref_b, ref_a)


def pack_x(plan, ref, out_a, out_b):
    last = plan.nx - 1
    for which, out in ((0, out_a), (1, out_b)):
        out[...] = ref[jnp.where(plan.high("gx", which)[0], last, 0)]


def pack_y(plan, ref, out_a, out_b):
    low, top = ref[:, 0, :], ref[:, plan.ny - 1, :]
    for which, out in ((0, out_a), (1, out_b)):
        out[...] = jnp.where(plan.high("gy", which)[0], top, low)


def tile_put(plan, tile, i, q, value):
    group = 128 // plan.ny
    r = i // group
    rows = pl.ds((i % group) * plan.ny, plan.ny)
    moved = pltpu.roll(value, r + plan.high("gz", q)[0].astype(jnp.int32), 1)
    tile[q, rows, :] = jnp.where(lanes_of(value.shape) == r, moved, tile[q, rows, :])


def tile_out(plan, tile, outs):
    for q, out in zip(plan.z_msgs, outs):
        out[...] = jnp.transpose(tile[q])[: out.shape[0], :]


def spread(plan, gots, outs):
    vals = [got[...] for got in gots]
    if len(vals) > 1:
        vals = list(z_sides(plan, vals))
    for val, out in zip(vals, outs):
        turned = jnp.transpose(val)
        for r in range(val.shape[0]):
            out[r * 128 : (r + 1) * 128, :] = jnp.broadcast_to(turned[:, r : r + 1], (128, 128))


def stack_rows(parts):
    cells = parts[0].shape[1]
    row = rows_of((8, cells))
    out = jnp.zeros((8, cells), F32)
    for k, part in enumerate(parts):
        out = jnp.where(row == k, jnp.broadcast_to(part, (8, cells)), out)
    return out


def z_sides(plan, vals):
    low, top = jnp.zeros_like(vals[0]), jnp.zeros_like(vals[0])
    for q, val in zip(plan.z_msgs, vals):
        up = plan.high("gz", q)[1]
        low = low + jnp.where(up, 0.0, val)
        top = top + jnp.where(up, val, 0.0)
    return low, top


def mobility_kernel(
    plan, press_in, sat_in, perm_in, rock_in, oil_in,
    press, sat, mob, coef, frac, xa, xb, ya, yb, total, perm, rock, oil, sem, oil_sem,
):
    kinds = oil.shape[0]
    oil_move = pltpu.make_async_copy(oil_in, oil, oil_sem)
    oil_move.start()
    size = plan.nx // CHUNKS
    moves = []
    for c in range(CHUNKS):
        cut = pl.ds(c * size, size)
        for k, (src, dst) in enumerate(
            ((sat_in, sat), (rock_in, rock), (perm_in, perm), (press_in, press))
        ):
            move = pltpu.make_async_copy(src.at[cut], dst.at[cut], sem.at[c, k])
            move.start()
            moves.append(move)

    def layer(i, acc):
        s, kind = sat[i], rock[i]
        c = jnp.full(s.shape, oil[0], F32)
        for k in range(1, kinds):
            c = jnp.where(kind == k, oil[k], c)
        water, rest = s * s, 1.0 - s
        den = water + c * rest * rest
        m = perm[i] * den
        coef[i] = c
        mob[i] = m
        frac[i] = water / den
        return acc + m

    acc = jnp.zeros((plan.ny, plan.nz), F32)
    oil_move.wait()
    for c in range(CHUNKS):
        for move in moves[4 * c : 4 * c + 3]:
            move.wait()
        acc = lax.fori_loop(c * size, (c + 1) * size, layer, acc, unroll=4)
    total[...] = acc
    for c in range(CHUNKS):
        moves[4 * c + 3].wait()
    for k, ref in enumerate((press, mob, frac)):
        pack_x(plan, ref, xa.at[k], xb.at[k])
        pack_y(plan, ref, ya.at[k], yb.at[k])


def inner_kernel(plan, press, mob, frac, source, compress, well, res, tx, ty, tz, diag, *comps):
    shape = (plan.ny, plan.nz)
    row, lane = rows_of(shape), lanes_of(shape)

    def layer(i, carry):
        p_last, m_last, r_last = carry
        p, m = press[i], mob[i]
        t = harmonic(m_last, m)
        tx[i] = t
        flux_x = t * (p_last - p)
        t = harmonic(jnp.where(row == 0, 0.0, ahead(m, 0)), m)
        ty[i] = t
        flux_y = t * (ahead(p, 0) - p)
        t = harmonic(jnp.where(lane == 0, 0.0, ahead(m, 1)), m)
        tz[i] = t
        flux_z = t * (ahead(p, 1) - p)
        d = compress[i] + WELL_INDEX * well[i].astype(F32) * m
        diag[i] = d
        r = source[i] - d * p + flux_x + (flux_y - back(flux_y, 0)) + (flux_z - back(flux_z, 1))
        res[jnp.maximum(i - 1, 0)] = r_last - flux_x
        for q, comp in zip(plan.z_msgs, comps):
            lead = plan.high("gz", q)[0].astype(jnp.int32) + INTERSECTION
            mix = jnp.where(
                lane <= INTERSECTION, pltpu.roll(p, lead, 1), pltpu.roll(m, lead + 1, 1)
            )
            comp[pl.ds(i * plan.ny, plan.ny), :] = jnp.where(
                lane <= INTERSECTION + 1, mix, pltpu.roll(frac[i], lead + 2, 1)
            )
        return p, m, r

    zero = jnp.zeros(shape, F32)
    res[plan.nx - 1] = lax.fori_loop(0, plan.nx, layer, (zero, zero, zero), unroll=4)[2]


def rim_kernel(plan, res_in, press, mob, xa, xb, ya, yb, *rest):
    n_msg = len(plan.z_msgs)
    comps, res, z_outs = rest[:n_msg], rest[n_msg], rest[n_msg + 1 :]
    nx, ny, nz = plan.nx, plan.ny, plan.nz
    last = nx - 1
    for high, k in ((False, 0), (True, last)):
        p, m = (side(plan, "gx", xa[f], xb[f], high) for f in (0, 1))
        res[k] = res[k] + harmonic(mob[k], m) * (p - press[k])
    for high, k in ((False, 0), (True, ny - 1)):
        p, m = (side(plan, "gy", ya[f], yb[f], high) for f in (0, 1))
        res[:, k, :] = res[:, k, :] + harmonic(mob[:, k, :], m) * (p - press[:, k, :])
    wide = INTERSECTION
    group = 128 // ny
    for q, out, comp in zip(plan.z_msgs, z_outs, comps):
        up = plan.high("gz", q)[0].astype(jnp.int32)
        lane = lanes_of((128, nz))
        for k in range(nx // group):
            cut = slice(k * 128, (k + 1) * 128)
            value = pltpu.roll(res[k * group : (k + 1) * group].reshape(128, nz), up * wide, 1)
            value = jnp.where(lane < wide, value, comp[cut, :])
            out[:, cut] = jnp.transpose(value)[:MSG_ROWS, :]


def z_flux(sent, got):
    wide = INTERSECTION
    out = []
    for own, other in zip(sent, got):
        t = harmonic(own[wide + 1 : wide + 2, :], other[wide + 1 : wide + 2, :])
        q = t * (other[wide : wide + 1, :] - own[wide : wide + 1, :])
        out.append((other[wide : wide + 1, :], other[wide + 2 : wide + 3, :], t, q))
    return out


def z_kernel(plan, n_msg, res, basis, rim_low, rim_top, order, *rest):
    sent, got = rest[:n_msg], rest[n_msg : 2 * n_msg]
    spec, ya, yb = rest[2 * n_msg :]
    nx, ny, nz = plan.nx, plan.ny, plan.nz
    wide = INTERSECTION
    mixes, rims = [], []
    for q, other, (_, _, _, flux) in zip(plan.z_msgs, got, z_flux(sent, got)):
        up = plan.high("gz", q)[1]
        row = rows_of(other.shape)
        near = jnp.where(up, 0, wide - 1)
        flux = jnp.broadcast_to(flux, other.shape)
        mix = jnp.where(row < wide, other[...], 0.0)
        mix = jnp.where(row == near, mix - flux, mix)
        mix = jnp.where(row == wide, flux, mix)
        top, low = halves(mix)
        mixes.append(jnp.concatenate([top, low, top], axis=0))
        rims.append(jnp.where(up, rim_top[...], rim_low[...]).astype(jnp.bfloat16))
    group = 128 // ny
    for k in range(nx // group):
        value = res[k * group : (k + 1) * group].reshape(128, nz)
        top, low = halves(value)
        out = mxu(jnp.concatenate([top, low, top], axis=1), basis[...])
        for mix, rim in zip(mixes, rims):
            out = out + mxu(mix[:, k * 128 : (k + 1) * 128], rim, ((0,), (0,)))
        spec[k * group : (k + 1) * group] = out.reshape(group, ny, out.shape[1])
    tail = 2 * wide
    per = 128 // tail
    for which, ref in ((0, ya), (1, yb)):
        start = jnp.where(plan.high("gy", which)[0], ny - wide, 0)
        rows = pl.ds(pl.multiple_of(start, 8), wide)
        ref[:nx] = spec[:, rows, :nz]
        for g in range(nx // per):
            ref[nx + g] = jnp.concatenate(
                [spec[g * per + j, rows, nz:] for j in range(per)], axis=1
            )


def faces_xy_kernel(
    plan, mob, press, sat, coef, poro, well, tx_in, ty_in, xa, xb, ya, yb,
    tx, ty_low, ty_top, gx, gy_low, gy_top, hx, hy, rate, inject, anchor, square, pull, push, ty_rim,
):
    nx, ny, nz = plan.nx, plan.ny, plan.nz
    for k, high in ((0, False), (1, True)):
        for f, field in ((0, 0), (1, 2)):
            hx[k, f] = side(plan, "gx", xa[field], xb[field], high)
            hy[k, f] = side(plan, "gy", ya[field], yb[field], high)
    ty_rim[0] = harmonic(mob[:, 0, :], side(plan, "gy", ya[1], yb[1], False))
    ty_rim[1] = harmonic(mob[:, ny - 1, :], side(plan, "gy", ya[1], yb[1], True))
    row = rows_of((ny, nz))
    t_first = harmonic(mob[0], side(plan, "gx", xa[1], xb[1], False))

    def layer(i, p_last):
        p = press[i]
        t = jnp.where(i == 0, t_first, tx_in[i])
        tx[i] = t
        gx[i] = t * (p_last - p)
        t = ty_in[i]
        low = jnp.where(row == 0, ty_rim[0, pl.ds(i, 1), :], t)
        top = jnp.where(row == ny - 1, ty_rim[1, pl.ds(i, 1), :], back(t, 0))
        ty_low[i] = low
        ty_top[i] = top
        y_last = jnp.where(row == 0, hy[0, 0, pl.ds(i, 1), :], ahead(p, 0))
        y_next = jnp.where(row == ny - 1, hy[1, 0, pl.ds(i, 1), :], back(p, 0))
        gy_low[i] = low * (y_last - p)
        gy_top[i] = top * (p - y_next)
        speed = poro[i] / TIME_STEP
        s, c = sat[i], coef[i]
        rest = 1.0 - s
        part = c * rest
        den = s * s + part * rest
        den = den * den
        rate[i] = speed
        gain = INJECT_RATE * well[i].astype(F32)
        inject[i] = gain
        anchor[i] = speed * s + gain
        square[i] = den
        pull[i] = speed * den
        push[i] = jnp.abs(2.0 * part * s)
        return p

    p = lax.fori_loop(0, nx, layer, hx[0, 0], unroll=4)
    t = harmonic(mob[nx - 1], side(plan, "gx", xa[1], xb[1], True))
    tx[nx] = t
    gx[nx] = t * (p - hx[1, 0])


def faces_z_kernel(plan, n_msg, res, press, tz_in, *rest):
    sent, got = rest[:n_msg], rest[n_msg : 2 * n_msg]
    full, tz_low, tz_top, gz_low, gz_top = rest[2 * n_msg : 2 * n_msg + 5]
    fz, hz = rest[2 * n_msg + 5 : -1], rest[-1]
    nx, ny, nz = plan.nx, plan.ny, plan.nz
    parts = z_flux(sent, got)
    split = [z_sides(plan, [part[k] for part in parts]) for k in range(4)]
    rows = stack_rows([v for pair in split for v in pair])
    for k in range(nx * ny // 128):
        cut = slice(k * 128, (k + 1) * 128)
        hz[cut, :8] = jnp.transpose(rows[:, cut])
    lane = lanes_of((ny, nz))

    def layer(i, carry):
        t, p = tz_in[i], press[i]
        cells = pl.ds(i * ny, ny)
        col = hz[cells, :8]
        in_low, in_top = col[:, 6:7], col[:, 7:8]
        tz_low[i] = jnp.where(lane == 0, col[:, 4:5], t)
        tz_top[i] = jnp.where(lane == nz - 1, col[:, 5:6], back(t, 1))
        g = t * (ahead(p, 1) - p)
        gz_low[i] = jnp.where(lane == 0, in_low, g)
        gz_top[i] = jnp.where(lane == nz - 1, -in_top, back(g, 1))
        flux = jnp.where(lane == 0, in_low, 0.0) + jnp.where(lane == nz - 1, in_top, 0.0)
        full[i] = res[i] + flux
        if len(fz) == 1:
            fz[0][cells, :] = jnp.broadcast_to(col[:, 2:3] + col[:, 3:4], (ny, nz))
        else:
            for k, out in enumerate(fz):
                out[cells, :] = jnp.broadcast_to(col[:, 2 + k : 3 + k], (ny, nz))
        return carry

    lax.fori_loop(0, nx, layer, 0, unroll=4)


def wide_rows(plan, msg_a, msg_b, i, high):
    nx = plan.nx
    tail = 2 * INTERSECTION
    per = 128 // tail
    ends = side(plan, "gy", msg_a[nx + i // per], msg_b[nx + i // per], high)
    ends = pltpu.roll(ends, (128 - (i % per) * tail) % 128, 1)[:, :tail]
    return jnp.concatenate([side(plan, "gy", msg_a[i], msg_b[i], high), ends], axis=1)


def thrice(value):
    top, low = halves(value)
    return jnp.concatenate([top, low, top], axis=0)


def fold(value, nz):
    rows, tail = value.shape[0], value.shape[1] - nz
    ends = jnp.concatenate(
        [value[k : k + 8, nz:] for k in range(0, rows, 8)]
        + [jnp.zeros((8, nz - rows // 8 * tail), F32)],
        axis=1,
    )
    return jnp.concatenate([value[:, :nz], ends], axis=0)


def unfold(value, tail):
    rows = value.shape[0] - 8
    ends = jnp.concatenate(
        [value[rows:, k * tail : (k + 1) * tail] for k in range(rows // 8)], axis=0
    )
    return jnp.concatenate([value[:rows], ends], axis=1)


def y_modes(plan, spec, ya, yb, basis, i):
    low = wide_rows(plan, ya, yb, i, False)
    top = wide_rows(plan, ya, yb, i, True)
    return mxu(basis[...], thrice(jnp.concatenate([low, spec[i], top], axis=0)))


def y_edge_kernel(plan, spec, ya, yb, basis, factors, order, edge, xa, xb):
    nx = plan.nx
    wide = INTERSECTION

    def layer(i, carry):
        edge[i] = y_modes(plan, spec, ya, yb, basis, jnp.where(i < wide, i, nx - 2 * wide + i))
        return carry

    lax.fori_loop(0, 2 * wide, layer, 0, unroll=16)
    low = jnp.zeros(edge.shape[1:], F32)
    top = low
    for k in range(wide):
        low = (edge[wide - 1 - k] + low) * factors[k]
        top = (edge[wide + k] + top) * factors[k]
    for which, out in ((0, xa), (1, xb)):
        out[...] = fold(jnp.where(plan.high("gx", which)[0], top, low), plan.nz)


def y_mid_kernel(plan, spec, ya, yb, basis, factors, edge, zed):
    nx = plan.nx
    wide = INTERSECTION

    def layer(i, carry):
        zed[i] = y_modes(plan, spec, ya, yb, basis, i)
        return carry

    lax.fori_loop(wide, nx - wide, layer, 0, unroll=8)

    def outer(k, carry):
        low, top = carry
        c = factors[wide + k]
        low = (edge[k] + low) * c
        top = (edge[2 * wide - 1 - k] + top) * c
        zed[k] = low
        zed[nx - 1 - k] = top
        return low, top

    def inner(k, carry):
        low, top = carry
        c = factors[wide + k]
        low = (zed[k] + low) * c
        top = (zed[nx - 1 - k] + top) * c
        zed[k] = low
        zed[nx - 1 - k] = top
        return low, top

    zero = jnp.zeros(edge.shape[1:], F32)
    carry = lax.fori_loop(0, wide, outer, (zero, zero), unroll=2)
    lax.fori_loop(wide, nx // 2, inner, carry, unroll=2)


def solve_kernel(
    plan, zed, xa, xb, factors, reach, middle, basis_y, basis_z, total, direction, *rest
):
    (dxa, dxb, dya, dyb), z_outs, (work, tile) = rest[:4], rest[4:-2], rest[-2:]
    nx, ny, nz = plan.nx, plan.ny, plan.nz
    wide = INTERSECTION
    half = nx // 2
    low_in = unfold(side(plan, "gx", xa[...], xb[...], False), 2 * wide)
    top_in = unfold(side(plan, "gx", xa[...], xb[...], True), 2 * wide)
    low = zed[half - 1] + reach[half - 1] * low_in
    top = zed[half] + reach[half - 1] * top_in
    c, mid = factors[wide + half - 1], middle[...]
    low, top = (low + c * top) * mid, (top + c * low) * mid

    def put(i, value):
        work[pl.ds(i * ny, ny), :] = mxu(basis_y[...], thrice(value))

    put(half - 1, low)
    put(half, top)

    def outward(k, carry):
        low, top = carry
        i = half - 2 - k
        c = factors[wide + i]
        far = reach[i]
        low = (zed[i] + far * low_in) + c * low
        top = (zed[nx - 1 - i] + far * top_in) + c * top
        put(i, low)
        put(nx - 1 - i, top)
        return low, top

    lax.fori_loop(0, half - 1, outward, (low, top), unroll=15)
    mean = jnp.sum(jnp.sum(total[...], axis=0, keepdims=True), axis=1, keepdims=True) / (
        nx * ny * nz
    )
    inverse = 1.0 / mean
    group = 128 // ny
    base_top, base_low = basis_z[0], basis_z[1]

    def lift(r, carry):
        high, rest_ = halves(work[pl.ds(r * 128, 128), :])
        value = mxu(high, base_top) + (mxu(rest_, base_top) + mxu(high, base_low))
        value = value * inverse
        direction[pl.ds(r * group, group)] = value.reshape(group, ny, nz)
        for q in plan.z_msgs:
            moved = pltpu.roll(value, r + plan.high("gz", q)[0].astype(jnp.int32), 1)
            tile[q] = jnp.where(lanes_of((128, nz)) == r, moved, tile[q])
        return carry

    lax.fori_loop(0, nx // group, lift, 0, unroll=8)
    pack_x(plan, direction, dxa, dxb)
    pack_y(plan, direction, dya, dyb)
    tile_out(plan, tile, z_outs)


def image_kernel(
    plan, n_dev, direction, diag, full, tx, ty_low, ty_top, tz_low, tz_top, xa, xb, ya, yb, *rest
):
    n_msg = len(plan.z_msgs)
    got = rest[:n_msg]
    image, sums, gx, gy_low, gy_top, gz_low, gz_top, hy = rest[n_msg : n_msg + 8]
    hz = rest[n_msg + 8 :]
    nx, ny, nz = plan.nx, plan.ny, plan.nz
    spread(plan, got, hz)
    hy[0] = side(plan, "gy", ya[...], yb[...], False)
    hy[1] = side(plan, "gy", ya[...], yb[...], True)
    lane = lanes_of((ny, nz))

    def layer(i, carry):
        d_last, im_last, rd, da = carry
        d = direction[i]
        flux = tx[i] * (d_last - d)
        gx[i] = flux
        y_last = from_above(d, hy[0, pl.ds(i, 1), :])
        y_next = from_below(d, hy[1, pl.ds(i, 1), :])
        cells = pl.ds(i * ny, ny)
        z_last = jnp.where(lane == 0, hz[0][cells, :], ahead(d, 1))
        z_next = jnp.where(lane == nz - 1, hz[-1][cells, :], back(d, 1))
        im = diag[i] * d - flux
        for ref, g, sign in (
            (gy_low, ty_low[i] * (y_last - d), -1),
            (gy_top, ty_top[i] * (d - y_next), 1),
            (gz_low, tz_low[i] * (z_last - d), -1),
            (gz_top, tz_top[i] * (d - z_next), 1),
        ):
            ref[i] = g
            im = im + g if sign > 0 else im - g
        im_last = im_last + flux
        image[jnp.maximum(i - 1, 0)] = im_last
        rd = rd + full[i] * d
        da = da + jnp.where(i > 0, d_last, 0.0) * im_last
        return d, im, rd, da

    zero = jnp.zeros((ny, nz), F32)
    low = side(plan, "gx", xa[...], xb[...], False)
    top = side(plan, "gx", xa[...], xb[...], True)
    d, im, rd, da = lax.fori_loop(0, nx, layer, (low, zero, zero, zero), unroll=16)
    flux = tx[nx] * (d - top)
    gx[nx] = flux
    im = im + flux
    image[nx - 1] = im
    da = da + d * im
    lane = lanes_of((n_dev, 128))
    sums[...] = jnp.where(lane < 64, jnp.sum(rd), jnp.sum(da))


def upwind(g, low, high):
    return g * jnp.where(g > 0.0, low, high)


def sweep(plan, refs, x_low, x_top, hy, z_at, done):
    nx, ny, nz = plan.nx, plan.ny, plan.nz
    (now, frac, coef, rate, anchor, gx, gy_low, gy_top, gz_low, gz_top, outflow) = refs
    lane = lanes_of((ny, nz))

    def layer(i, carry):
        f, flow = carry
        f_next = jnp.where(i == nx - 1, x_top, frac[jnp.minimum(i + 1, nx - 1)])
        s, c = now[i], coef[i]
        flow_next = upwind(gx[i + 1], f, f_next)
        y_last = from_above(f, hy[0, pl.ds(i, 1), :])
        y_next = from_below(f, hy[1, pl.ds(i, 1), :])
        z_low, z_top = z_at(i)
        z_last = jnp.where(lane == 0, z_low, ahead(f, 1))
        z_next = jnp.where(lane == nz - 1, z_top, back(f, 1))
        bal = (
            (flow_next - flow)
            + (upwind(gy_top[i], f, y_next) - upwind(gy_low[i], y_last, f))
            + (upwind(gz_top[i], f, z_next) - upwind(gz_low[i], z_last, f))
            + (rate[i] * s - anchor[i])
        )
        rest = 1.0 - s
        part = c * rest
        den = s * s + part * rest
        square = den * den
        s = s - bal * square / (rate[i] * square + outflow[i] * jnp.abs(part * s))
        done(i, s, c)
        return f_next, flow_next

    f0 = frac[0]
    lax.fori_loop(0, nx, layer, (f0, upwind(gx[0], x_low, f0)), unroll=16)


def keep(plan, new, new_frac, tile):
    def done(i, s, c):
        new[i] = s
        water, rest = s * s, 1.0 - s
        f = water / (water + c * rest * rest)
        new_frac[i] = f
        for q in plan.z_msgs:
            tile_put(plan, tile, i, q, f)

    return done


def pack_all(plan, ref, tile, outs):
    xa, xb, ya, yb = outs[:4]
    pack_x(plan, ref, xa, xb)
    pack_y(plan, ref, ya, yb)
    tile_out(plan, tile, outs[4:])


def step_of(sums):
    both = jnp.sum(sums[...], axis=0, keepdims=True)
    return both[:, 0:1] / both[:, 64:65]


def write_out(plan, i, ref, out, sem):
    size = plan.nx // CHUNKS

    @pl.when(i % size == size - 1)
    def _():
        c = i // size
        cut = pl.ds(c * size, size)
        pltpu.make_async_copy(ref.at[cut], out.at[cut], sem.at[c]).start()


def write_end(plan, ref, out, sem):
    size = plan.nx // CHUNKS
    for c in range(CHUNKS):
        cut = pl.ds(c * size, size)
        pltpu.make_async_copy(ref.at[cut], out.at[cut], sem.at[c]).wait()


def output_kernel(plan, sums, press, direction, full, image, p_out, r_out, token, p_new, r_new, p_sem, r_sem):
    step = step_of(sums)

    def layer(i, carry):
        p_new[i] = press[i] + step * direction[i]
        write_out(plan, i, p_new, p_out, p_sem)
        r_new[i] = full[i] - step * image[i]
        write_out(plan, i, r_new, r_out, r_sem)
        return carry

    lax.fori_loop(0, plan.nx, layer, 0, unroll=4)
    token[...] = jnp.zeros(token.shape, F32)
    write_end(plan, p_new, p_out, p_sem)
    write_end(plan, r_new, r_out, r_sem)


def step_kernel(plan, *refs):
    n_msg = len(plan.z_msgs)
    sums, still, move = refs[0], refs[1:6], refs[6:11]
    (sat, frac, coef, inject, square, pull, push, hx, hy) = refs[11:20]
    fz = refs[20 : 20 + n_msg]
    outs = refs[20 + n_msg :]
    (s_new, f_new, gx, gy_low, gy_top, gz_low, gz_top, outflow) = outs[:8]
    packs = outs[8 : 12 + n_msg]
    tile = outs[-1]
    nx, ny, nz = plan.nx, plan.ny, plan.nz
    step = step_of(sums)
    lane = lanes_of((ny, nz))
    done = keep(plan, s_new, f_new, tile)

    def flux(k, i):
        return still[k][i] + step * move[k][i]

    def layer(i, carry):
        f, g, flow = carry
        f_next = jnp.where(i == nx - 1, hx[1, 1], frac[jnp.minimum(i + 1, nx - 1)])
        g_next = flux(0, i + 1)
        gx[i + 1] = g_next
        flow_next = upwind(g_next, f, f_next)
        out = jnp.maximum(g_next, 0.0) - jnp.minimum(g, 0.0)
        bal = flow_next - flow - inject[i]
        cells = pl.ds(i * ny, ny)
        y_last = from_above(f, hy[0, 1, pl.ds(i, 1), :])
        y_next = from_below(f, hy[1, 1, pl.ds(i, 1), :])
        z_last = jnp.where(lane == 0, fz[0][cells, :], ahead(f, 1))
        z_next = jnp.where(lane == nz - 1, fz[-1][cells, :], back(f, 1))
        for k, ref, other, low in (
            (1, gy_low, y_last, True),
            (2, gy_top, y_next, False),
            (3, gz_low, z_last, True),
            (4, gz_top, z_next, False),
        ):
            value = flux(k, i)
            ref[i] = value
            if low:
                out = out - jnp.minimum(value, 0.0)
                bal = bal - upwind(value, other, f)
            else:
                out = out + jnp.maximum(value, 0.0)
                bal = bal + upwind(value, f, other)
        outflow[i] = out + out
        done(i, sat[i] - bal * square[i] / (pull[i] + out * push[i]), coef[i])
        return f_next, g_next, flow_next

    f0, g0 = frac[0], flux(0, 0)
    gx[0] = g0
    lax.fori_loop(0, nx, layer, (f0, g0, upwind(g0, hx[0, 1], f0)), unroll=16)
    pack_all(plan, f_new, tile, packs)


def later_kernel(plan, last_sweep, *refs):
    n_msg = len(plan.z_msgs)
    fields = refs[:11]
    xa, xb, ya, yb = refs[11:15]
    got = refs[15 : 15 + n_msg]
    rest = refs[16 + n_msg :]
    if last_sweep:
        out, new, sem, fh, *hz = rest

        def done(i, s, c):
            new[i] = s
            write_out(plan, i, new, out, sem)
    else:
        new, new_frac = rest[:2]
        packs = rest[2 : 6 + n_msg]
        tile, fh, *hz = rest[6 + n_msg :]
        done = keep(plan, new, new_frac, tile)
    spread(plan, got, hz)
    fh[0] = side(plan, "gy", ya[...], yb[...], False)
    fh[1] = side(plan, "gy", ya[...], yb[...], True)

    def z_at(i):
        cells = pl.ds(i * plan.ny, plan.ny)
        return hz[0][cells, :], hz[-1][cells, :]

    sweep(
        plan, fields,
        side(plan, "gx", xa[...], xb[...], False), side(plan, "gx", xa[...], xb[...], True),
        fh, z_at, done,
    )
    if last_sweep:
        write_end(plan, new, out, sem)
    else:
        pack_all(plan, new_frac, tile, packs)


def per_device(
    counts, pressure, source, saturation, permeability, compress, porosity, rock_type, well_mask, oil_factor
):
    nx, ny, nz = pressure.shape
    wide = INTERSECTION
    plan = Plan(nx, ny, nz, counts)
    n_msg = len(plan.z_msgs)
    n_dev = counts["gx"] * counts["gy"] * counts["gz"]
    cells = nx * ny
    my, mz = ny + 2 * wide, nz + 2 * wide
    table_y, eigen_y = sine_basis(my)
    table_z, eigen_z = sine_basis(mz)
    factors, reach, middle = sweep_factors(wide + nx // 2, wide, eigen_y, eigen_z)
    const = lambda v: jnp.asarray(v, F32)
    factors, reach, middle = const(factors), const(reach), const(middle)
    rim = np.zeros((2, MSG_ROWS, mz))
    rim[0, :wide] = table_z[:wide]
    rim[0, wide] = table_z[wide]
    rim[1, :wide] = table_z[mz - wide :]
    rim[1, wide] = table_z[mz - wide - 1]

    def parts(v):
        v = np.asarray(v, np.float32)
        top = v.astype(jnp.bfloat16)
        return top, (v - top.astype(np.float32)).astype(jnp.bfloat16)

    def left(v):
        top, low = parts(v)
        return jnp.asarray(np.concatenate([top, top, low], axis=1))

    def right(v):
        top, low = parts(v)
        return jnp.asarray(np.concatenate([top, top, low], axis=0))

    rims = [jnp.concatenate([right(v)], axis=0).astype(F32) for v in rim]

    def send(value, axis, which):
        return lax.ppermute(value, axis, plan.perm(axis, which))

    def swap(axis, a, b):
        return send(a, axis, 0), send(b, axis, 1)

    def swap_z(msgs):
        return [send(v, "gz", q) for q, v in zip(plan.z_msgs, msgs)]

    full_shape = (nx, ny, nz)
    x_face, y_face, z_face = (ny, nz), (nx, nz), (cells // 128, 128)
    face_shapes = [x_face, x_face, y_face, y_face] + [z_face] * n_msg
    tile = (2, 128, nz)
    spreads = [(cells, 128)] * n_msg
    dma = pltpu.SemaphoreType.DMA

    def exchange(packs):
        z = swap_z(packs[4:])
        y = swap("gy", packs[2], packs[3])
        x = swap("gx", packs[0], packs[1])
        return [*x, *y, *z]

    press, sat, mob, coef, frac, xa, xb, ya, yb, total = call(
        functools.partial(mobility_kernel, plan),
        [full_shape] * 5 + [(3,) + x_face] * 2 + [(3,) + y_face] * 2 + [x_face],
        (pressure, saturation, permeability, rock_type, oil_factor),
        hbm=(0, 1, 2, 3, 4),
        scratch=[full_shape, pltpu.VMEM(full_shape, jnp.int32),
                 pltpu.SMEM(oil_factor.shape, F32), dma((CHUNKS, 4)), dma],
    )
    ya, yb = swap("gy", ya, yb)
    xa, xb = swap("gx", xa, xb)
    res, tx, ty, tz, diag, *comps = call(
        functools.partial(inner_kernel, plan),
        [full_shape] * 5 + [(cells, nz)] * n_msg,
        (press, mob, frac, source, compress, well_mask),
    )
    res, *sent = call(
        functools.partial(rim_kernel, plan),
        [full_shape] + [(MSG_ROWS, cells)] * n_msg,
        (res, press, mob, xa, xb, ya, yb, *comps),
        aliases={0: 0},
    )
    got = swap_z(sent)
    tx, ty_low, ty_top, gx, gy_low, gy_top, hx, hy, rate, inject, anchor, square, pull, push = call(
        functools.partial(faces_xy_kernel, plan),
        [(nx + 1, ny, nz)] + [full_shape] * 2 + [(nx + 1, ny, nz)] + [full_shape] * 2
        + [(2, 2) + x_face, (2, 2) + y_face] + [full_shape] * 6,
        (mob, press, sat, coef, porosity, well_mask, tx, ty, xa, xb, ya, yb),
        scratch=[(2,) + y_face],
    )
    spec, sa, sb = call(
        functools.partial(z_kernel, plan, n_msg),
        [(nx, ny, mz)] + [(nx + nx * 2 * wide // 128, wide, nz)] * 2,
        (res, right(table_z[wide : wide + nz]), *rims, hx, *sent, *got),
    )
    sa, sb = swap("gy", sa, sb)
    full, tz_low, tz_top, gz_low, gz_top, *fz = call(
        functools.partial(faces_z_kernel, plan, n_msg),
        [full_shape] * 5 + spreads,
        (res, press, tz, *sent, *got),
        scratch=[(cells, 128)],
    )
    edge, ma, mb = call(
        functools.partial(y_edge_kernel, plan),
        [(2 * wide, my, mz), (my + 8, nz), (my + 8, nz)],
        (spec, sa, sb, left(table_y), factors, gz_low),
    )
    ma, mb = swap("gx", ma, mb)
    (zed,) = call(
        functools.partial(y_mid_kernel, plan),
        [(nx, my, mz)],
        (spec, sa, sb, left(table_y), factors, edge),
    )
    direction, *packs = call(
        functools.partial(solve_kernel, plan),
        [full_shape] + face_shapes,
        (zed, ma, mb, factors, reach, middle, left(table_y[wide : wide + ny]),
         jnp.asarray(np.stack(parts(table_z[:, wide : wide + nz]))), total),
        scratch=[(cells, mz), tile],
    )
    dhalo = exchange(packs)
    image, sums, *moves = call(
        functools.partial(image_kernel, plan, n_dev),
        [full_shape, (n_dev, 128), (nx + 1, ny, nz)] + [full_shape] * 4,
        (direction, diag, full, tx, ty_low, ty_top, tz_low, tz_top, *dhalo),
        scratch=[(2,) + y_face] + spreads,
    )
    sums = lax.all_to_all(sums, AXES, 0, 0, tiled=True)
    outs = call(
        functools.partial(step_kernel, plan),
        [full_shape] * 2 + [(nx + 1, ny, nz)] + [full_shape] * 5 + face_shapes,
        (sums, gx, gy_low, gy_top, gz_low, gz_top, *moves,
         sat, frac, coef, inject, square, pull, push, hx, hy, *fz),
        scratch=[tile],
        limit=40,
    )
    current, frac, *flows = outs[:8]
    packs = outs[8:]
    p_new, r_new, token = call(
        functools.partial(output_kernel, plan),
        [full_shape] * 2 + [(8, 128)],
        (sums, press, direction, full, image),
        hbm_out=(0, 1),
        scratch=[full_shape] * 2 + [dma((CHUNKS,))] * 2,
    )
    for sweep_index in range(1, NEWTON):
        halo = exchange(packs)
        last_sweep = sweep_index == NEWTON - 1
        outs = call(
            functools.partial(later_kernel, plan, last_sweep),
            [full_shape] if last_sweep else [full_shape] * 2 + face_shapes,
            (current, frac, coef, rate, anchor, *flows, *halo, token),
            scratch=([full_shape, dma((CHUNKS,))] if last_sweep else [tile])
            + [(2,) + y_face] + spreads,
            hbm_out=(0,) if last_sweep else (),
        )
        current = outs[0]
        if not last_sweep:
            frac, packs = outs[1], outs[2:]
    return p_new, r_new, current


def solution(mesh):
    spec = P(*AXES)

    def body(*args):
        return per_device(dict(mesh.shape), *args)

    return jax.shard_map(
        body,
        mesh=mesh,
        in_specs=(spec,) * 8 + (P(),),
        out_specs=(spec,) * 3,
        check_vma=False,
    )
```

```python
import functools
import math

import jax
import jax.numpy as jnp
import numpy as np
from jax import lax
from jax.experimental import pallas as pl
from jax.experimental.pallas import tpu as pltpu
from jax.sharding import PartitionSpec as P


INTERSECTION = 8
NEWTON = 3

WELL_INDEX = 4.0
INJECT_RATE = 2.0
TIME_STEP = 0.05

AXES = ("gx", "gy", "gz")
F32 = jnp.float32
MSG_ROWS = 16
CHUNKS = 4


def sine_basis(length):
    points = np.arange(length) + 1
    angles = np.outer(points, points) % (2 * (length + 1)) * (math.pi / (length + 1))
    table = math.sqrt(2.0 / (length + 1)) * np.sin(angles)
    eigen = 2.0 - 2.0 * np.cos(points * (math.pi / (length + 1)))
    return table, eigen


def sweep_factors(count, skip, eigen_y, eigen_z):
    shift = 2.0 + eigen_y[:, None] + eigen_z[None, :]
    factors = []
    last = np.zeros_like(shift)
    for _ in range(count):
        last = 1.0 / (shift - last)
        factors.append(last)
    factors = np.stack(factors)
    reach = np.cumprod(factors[skip:], axis=0)
    return factors, reach, 1.0 / (1.0 - last * last)


def pairs(count, periodic, parity):
    if periodic and count % 2:
        step = 1 if parity == 0 else -1
        return [(i, (i + step) % count) for i in range(count)]
    out = []
    for i in range(parity, count, 2):
        j = i + 1
        if periodic:
            j = j % count
        if j < count:
            out += [(i, j), (j, i)]
    return out


def harmonic(one, two):
    return 2.0 * one * two / (one + two)


def rows_of(shape):
    return lax.broadcasted_iota(jnp.int32, shape, 0)


def lanes_of(shape):
    return lax.broadcasted_iota(jnp.int32, shape, 1)


def back(value, axis):
    return pltpu.roll(value, value.shape[axis] - 1, axis)


def ahead(value, axis):
    return pltpu.roll(value, 1, axis)


def from_above(value, halo):
    first = rows_of((8, value.shape[1])) == 0
    fill = jnp.broadcast_to(halo, (8, value.shape[1]))
    tiles = []
    for k in range(0, value.shape[0], 8):
        turned = pltpu.roll(value[k : k + 8], 1, 0)
        tiles.append(jnp.where(first, fill, turned))
        fill = turned
    return jnp.concatenate(tiles, axis=0)


def from_below(value, halo):
    last = rows_of((8, value.shape[1])) == 7
    fill = jnp.broadcast_to(halo, (8, value.shape[1]))
    tiles = []
    for k in range(value.shape[0] - 8, -1, -8):
        turned = pltpu.roll(value[k : k + 8], 7, 0)
        tiles.append(jnp.where(last, fill, turned))
        fill = turned
    return jnp.concatenate(tiles[::-1], axis=0)


class Plan:
    def __init__(self, nx, ny, nz, counts):
        self.nx, self.ny, self.nz = nx, ny, nz
        self.counts = counts
        self.z_msgs = [q for q in (0, 1) if pairs(counts["gz"], False, q)]

    def perm(self, axis, which):
        return pairs(self.counts[axis], axis != "gz", which)

    def high(self, axis, which):
        if axis != "gz" and self.counts[axis] % 2:
            return (which == 0, which == 1)
        up = (lax.axis_index(axis) % 2) == which
        return (up, up)


def call(kernel, outs, args, scratch=(), aliases=None, hbm=(), hbm_out=(), limit=28):
    def spec(k, remote):
        return pl.BlockSpec(memory_space=pltpu.HBM if k in remote else pltpu.VMEM)

    args = [
        pltpu.with_memory_space_constraint(v, pltpu.HBM) if k in hbm else v
        for k, v in enumerate(args)
    ]
    return pl.pallas_call(
        kernel,
        out_shape=[jax.ShapeDtypeStruct(s, F32) for s in outs],
        in_specs=[spec(k, hbm) for k in range(len(args))],
        out_specs=[spec(k, hbm_out) for k in range(len(outs))],
        scratch_shapes=[pltpu.VMEM(v, F32) if isinstance(v, tuple) else v for v in scratch],
        input_output_aliases=aliases or {},
        compiler_params=pltpu.CompilerParams(vmem_limit_bytes=limit << 20),
    )(*args)


def halves(value):
    top = value.astype(jnp.bfloat16)
    return top, (value - top.astype(F32)).astype(jnp.bfloat16)


def mxu(one, two, dims=((1,), (0,))):
    return lax.dot_general(one, two, (dims, ((), ())), preferred_element_type=F32)


def side(plan, axis, ref_a, ref_b, high):
    a_high = plan.high(axis, 0)[1]
    if high:
        return jnp.where(a_high, ref_a, ref_b)
    return jnp.where(a_high, ref_b, ref_a)


def pack_x(plan, ref, out_a, out_b):
    last = plan.nx - 1
    for which, out in ((0, out_a), (1, out_b)):
        out[...] = ref[jnp.where(plan.high("gx", which)[0], last, 0)]


def pack_y(plan, ref, out_a, out_b):
    low, top = ref[:, 0, :], ref[:, plan.ny - 1, :]
    for which, out in ((0, out_a), (1, out_b)):
        out[...] = jnp.where(plan.high("gy", which)[0], top, low)


def tile_put(plan, tile, i, q, value):
    group = 128 // plan.ny
    r = i // group
    rows = pl.ds((i % group) * plan.ny, plan.ny)
    moved = pltpu.roll(value, r + plan.high("gz", q)[0].astype(jnp.int32), 1)
    tile[q, rows, :] = jnp.where(lanes_of(value.shape) == r, moved, tile[q, rows, :])


def tile_out(plan, tile, outs):
    for q, out in zip(plan.z_msgs, outs):
        out[...] = jnp.transpose(tile[q])[: out.shape[0], :]


def spread(plan, gots, outs):
    vals = [got[...] for got in gots]
    if len(vals) > 1:
        vals = list(z_sides(plan, vals))
    for val, out in zip(vals, outs):
        turned = jnp.transpose(val)
        for r in range(val.shape[0]):
            out[r * 128 : (r + 1) * 128, :] = jnp.broadcast_to(turned[:, r : r + 1], (128, 128))


def stack_rows(parts):
    cells = parts[0].shape[1]
    row = rows_of((8, cells))
    out = jnp.zeros((8, cells), F32)
    for k, part in enumerate(parts):
        out = jnp.where(row == k, jnp.broadcast_to(part, (8, cells)), out)
    return out


def z_sides(plan, vals):
    low, top = jnp.zeros_like(vals[0]), jnp.zeros_like(vals[0])
    for q, val in zip(plan.z_msgs, vals):
        up = plan.high("gz", q)[1]
        low = low + jnp.where(up, 0.0, val)
        top = top + jnp.where(up, val, 0.0)
    return low, top


def mobility_kernel(
    plan, press_in, sat_in, perm_in, rock_in, oil_in,
    press, sat, mob, coef, frac, xa, xb, ya, yb, fa, fb, total, perm, rock, oil, sem, oil_sem,
):
    kinds = oil.shape[0]
    oil_move = pltpu.make_async_copy(oil_in, oil, oil_sem)
    oil_move.start()
    size = plan.nx // CHUNKS
    moves = []
    for c in range(CHUNKS):
        cut = pl.ds(c * size, size)
        for k, (src, dst) in enumerate(
            ((sat_in, sat), (rock_in, rock), (perm_in, perm), (press_in, press))
        ):
            move = pltpu.make_async_copy(src.at[cut], dst.at[cut], sem.at[c, k])
            move.start()
            moves.append(move)

    def layer(i, acc):
        s, kind = sat[i], rock[i]
        c = jnp.full(s.shape, oil[0], F32)
        for k in range(1, kinds):
            c = jnp.where(kind == k, oil[k], c)
        water, rest = s * s, 1.0 - s
        den = water + c * rest * rest
        m = perm[i] * den
        coef[i] = c
        mob[i] = m
        frac[i] = water / den
        return acc + m

    acc = jnp.zeros((plan.ny, plan.nz), F32)
    oil_move.wait()
    for c in range(CHUNKS):
        for move in moves[4 * c : 4 * c + 3]:
            move.wait()
        acc = lax.fori_loop(c * size, (c + 1) * size, layer, acc, unroll=4)
    total[...] = acc
    for c in range(CHUNKS):
        moves[4 * c + 3].wait()
    for k, ref in enumerate((press, mob)):
        pack_x(plan, ref, xa.at[k], xb.at[k])
    pack_x(plan, frac, fa, fb)
    for k, ref in enumerate((press, mob, frac)):
        pack_y(plan, ref, ya.at[k], yb.at[k])


def inner_kernel(plan, press, mob, frac, source, compress, well, res, tx, ty, tz, diag, *comps):
    shape = (plan.ny, plan.nz)
    row, lane = rows_of(shape), lanes_of(shape)

    def layer(i, carry):
        p_last, m_last, r_last = carry
        p, m = press[i], mob[i]
        t = harmonic(m_last, m)
        tx[i] = t
        flux_x = t * (p_last - p)
        t = harmonic(jnp.where(row == 0, 0.0, ahead(m, 0)), m)
        ty[i] = t
        flux_y = t * (ahead(p, 0) - p)
        t = harmonic(jnp.where(lane == 0, 0.0, ahead(m, 1)), m)
        tz[i] = t
        flux_z = t * (ahead(p, 1) - p)
        d = compress[i] + WELL_INDEX * well[i].astype(F32) * m
        diag[i] = d
        r = source[i] - d * p + flux_x + (flux_y - back(flux_y, 0)) + (flux_z - back(flux_z, 1))
        res[jnp.maximum(i - 1, 0)] = r_last - flux_x
        for q, comp in zip(plan.z_msgs, comps):
            lead = plan.high("gz", q)[0].astype(jnp.int32) + INTERSECTION
            mix = jnp.where(
                lane <= INTERSECTION, pltpu.roll(p, lead, 1), pltpu.roll(m, lead + 1, 1)
            )
            comp[pl.ds(i * plan.ny, plan.ny), :] = jnp.where(
                lane <= INTERSECTION + 1, mix, pltpu.roll(frac[i], lead + 2, 1)
            )
        return p, m, r

    zero = jnp.zeros(shape, F32)
    res[plan.nx - 1] = lax.fori_loop(0, plan.nx, layer, (zero, zero, zero), unroll=4)[2]


def rim_kernel(plan, res_in, press, mob, xa, xb, ya, yb, *rest):
    n_msg = len(plan.z_msgs)
    comps, res, z_outs = rest[:n_msg], rest[n_msg], rest[n_msg + 1 :]
    nx, ny, nz = plan.nx, plan.ny, plan.nz
    last = nx - 1
    for high, k in ((False, 0), (True, last)):
        p, m = (side(plan, "gx", xa[f], xb[f], high) for f in (0, 1))
        res[k] = res[k] + harmonic(mob[k], m) * (p - press[k])
    for high, k in ((False, 0), (True, ny - 1)):
        p, m = (side(plan, "gy", ya[f], yb[f], high) for f in (0, 1))
        res[:, k, :] = res[:, k, :] + harmonic(mob[:, k, :], m) * (p - press[:, k, :])
    wide = INTERSECTION
    group = 128 // ny
    for q, out, comp in zip(plan.z_msgs, z_outs, comps):
        up = plan.high("gz", q)[0].astype(jnp.int32)
        lane = lanes_of((128, nz))
        blocks = nx // group
        for k in range(blocks):
            value = pltpu.roll(res[k * group : (k + 1) * group].reshape(128, nz), up * wide, 1)
            value = jnp.where(lane < wide, value, comp[k * 128 : (k + 1) * 128, :])
            turned = jnp.transpose(value)
            out[k * wide : (k + 1) * wide, :] = turned[:wide]
            for f in range(3):
                row = blocks * (wide + f) + k
                out[row : row + 1, :] = turned[wide + f : wide + f + 1]


def z_flux(sent, got):
    out = []
    for own, other in zip(sent, got):
        blocks = own.shape[0] // (INTERSECTION + 3)
        first = blocks * INTERSECTION
        (p, m), (p_far, m_far, f_far) = (
            [ref[first + k * blocks : first + (k + 1) * blocks, :] for k in range(count)]
            for ref, count in ((own, 2), (other, 3))
        )
        t = harmonic(m, m_far)
        out.append((p_far, f_far, t, t * (p_far - p)))
    return out


def y_parts(plan):
    wide, nx = INTERSECTION, plan.nx
    return (
        list(range(wide)) + list(range(nx - wide, nx)),
        list(range(wide, nx - wide)),
    )


def z_kernel(plan, n_msg, res, basis, rim_low, rim_top, order, *rest):
    sent, got = rest[:n_msg], rest[n_msg : 2 * n_msg]
    spec, *outs = rest[2 * n_msg :]
    nx, ny, nz = plan.nx, plan.ny, plan.nz
    wide = INTERSECTION
    row = rows_of((wide, 128))
    fluxes = [part[3] for part in z_flux(sent, got)]
    ups = [plan.high("gz", q)[1] for q in plan.z_msgs]
    rims = [jnp.where(up, rim_top[...], rim_low[...]).astype(jnp.bfloat16) for up in ups]
    group = 128 // ny
    for k in range(nx // group):
        value = res[k * group : (k + 1) * group].reshape(128, nz)
        top, low = halves(value)
        out = mxu(jnp.concatenate([top, low, top], axis=1), basis[...])
        for up, other, flux, rim in zip(ups, got, fluxes, rims):
            flux = jnp.broadcast_to(flux[k : k + 1, :], (wide, 128))
            mix = other[k * wide : (k + 1) * wide, :]
            mix = jnp.where(row == jnp.where(up, 0, wide - 1), mix - flux, mix)
            mix = jnp.concatenate([mix, jnp.where(row == 0, flux, 0.0)], axis=0)
            out = out + mxu(thrice(mix), rim, ((0,), (0,)))
        spec[k * group : (k + 1) * group] = out.reshape(group, ny, out.shape[1])
    tail = 2 * wide
    per = 128 // tail
    for which in (0, 1):
        start = jnp.where(plan.high("gy", which)[0], ny - wide, 0)
        rows = pl.ds(pl.multiple_of(start, 8), wide)
        for layers, ref in zip(y_parts(plan), outs[which::2]):
            count = len(layers)
            for g in range(count // per):
                group = layers[g * per : (g + 1) * per]
                for j, i in enumerate(group):
                    ref[g * per + j] = spec[i, rows, :nz]
                ref[count + g] = jnp.concatenate([spec[i, rows, nz:] for i in group], axis=1)


def faces_xy_kernel(
    plan, mob, press, sat, coef, poro, well, tx_in, ty_in, xa, xb, ya, yb,
    tx, ty_low, ty_top, gx, gy_low, gy_top, hy, rate, inject, anchor, square, pull, push, ty_rim,
):
    nx, ny, nz = plan.nx, plan.ny, plan.nz
    x_low, x_top = (side(plan, "gx", xa[0], xb[0], high) for high in (False, True))
    for k, high in ((0, False), (1, True)):
        for f, field in ((0, 0), (1, 2)):
            hy[k, f] = side(plan, "gy", ya[field], yb[field], high)
    ty_rim[0] = harmonic(mob[:, 0, :], side(plan, "gy", ya[1], yb[1], False))
    ty_rim[1] = harmonic(mob[:, ny - 1, :], side(plan, "gy", ya[1], yb[1], True))
    row = rows_of((ny, nz))
    t_first = harmonic(mob[0], side(plan, "gx", xa[1], xb[1], False))

    def layer(i, p_last):
        p = press[i]
        t = jnp.where(i == 0, t_first, tx_in[i])
        tx[i] = t
        gx[i] = t * (p_last - p)
        t = ty_in[i]
        low = jnp.where(row == 0, ty_rim[0, pl.ds(i, 1), :], t)
        top = jnp.where(row == ny - 1, ty_rim[1, pl.ds(i, 1), :], back(t, 0))
        ty_low[i] = low
        ty_top[i] = top
        y_last = jnp.where(row == 0, hy[0, 0, pl.ds(i, 1), :], ahead(p, 0))
        y_next = jnp.where(row == ny - 1, hy[1, 0, pl.ds(i, 1), :], back(p, 0))
        gy_low[i] = low * (y_last - p)
        gy_top[i] = top * (p - y_next)
        speed = poro[i] / TIME_STEP
        s, c = sat[i], coef[i]
        rest = 1.0 - s
        part = c * rest
        den = s * s + part * rest
        den = den * den
        rate[i] = speed
        gain = INJECT_RATE * well[i].astype(F32)
        inject[i] = gain
        anchor[i] = speed * s + gain
        square[i] = den
        pull[i] = speed * den
        push[i] = jnp.abs(2.0 * part * s)
        return p

    p = lax.fori_loop(0, nx, layer, x_low, unroll=4)
    t = harmonic(mob[nx - 1], side(plan, "gx", xa[1], xb[1], True))
    tx[nx] = t
    gx[nx] = t * (p - x_top)


def z_ends(plan, n_msg):
    lane = lanes_of((plan.ny, plan.nz))
    low, top = lane == 0, lane == plan.nz - 1
    if n_msg == 1:
        up = plan.high("gz", plan.z_msgs[0])[1]
        low, top = low & jnp.logical_not(up), top & up
    return low, top


def residual_kernel(plan, n_msg, res, *rest):
    sent, got = rest[:n_msg], rest[n_msg : 2 * n_msg]
    full, hz, *fz = rest[2 * n_msg :]
    nx, ny, nz = plan.nx, plan.ny, plan.nz
    parts = z_flux(sent, got)
    if n_msg == 1:
        vals = list(parts[0][1:])
    else:
        vals = [v for k in (1, 2, 3) for v in z_sides(plan, [part[k] for part in parts])]
    for k in range(nx * ny // 128):
        rows = stack_rows([v[k : k + 1, :] for v in vals])
        hz[k * 128 : (k + 1) * 128, :8] = jnp.transpose(rows)
    at_low, at_top = z_ends(plan, n_msg)

    def layer(i, carry):
        cells = pl.ds(i * ny, ny)
        col = hz[cells, :8]
        in_low, in_top = (
            jnp.broadcast_to(col[:, k : k + 1], (ny, nz))
            for k in ((2, 2) if n_msg == 1 else (4, 5))
        )
        full[i] = res[i] + (jnp.where(at_low, in_low, 0.0) + jnp.where(at_top, in_top, 0.0))
        for k, out in enumerate(fz):
            out[cells, :] = jnp.broadcast_to(col[:, k : k + 1], (ny, nz))
        return carry

    lax.fori_loop(0, nx, layer, 0, unroll=8)


def faces_z_kernel(plan, n_msg, press, tz_in, hz, order, tz_low, tz_top, gz_low, gz_top):
    ny, nz = plan.ny, plan.nz
    at_low, at_top = z_ends(plan, n_msg)

    def layer(i, carry):
        t, p = tz_in[i], press[i]
        col = hz[pl.ds(i * ny, ny), :8]
        t_low, t_top, in_low, in_top = (
            jnp.broadcast_to(col[:, k : k + 1], (ny, nz))
            for k in ((1, 1, 2, 2) if n_msg == 1 else (2, 3, 4, 5))
        )
        tz_low[i] = jnp.where(at_low, t_low, t)
        tz_top[i] = jnp.where(at_top, t_top, back(t, 1))
        g = t * (ahead(p, 1) - p)
        gz_low[i] = jnp.where(at_low, in_low, g)
        gz_top[i] = jnp.where(at_top, -in_top, back(g, 1))
        return carry

    lax.fori_loop(0, plan.nx, layer, 0, unroll=8)


def wide_rows(plan, msg_a, msg_b, j, count, high):
    tail = 2 * INTERSECTION
    per = 128 // tail
    ends = side(plan, "gy", msg_a[count + j // per], msg_b[count + j // per], high)
    ends = pltpu.roll(ends, (128 - (j % per) * tail) % 128, 1)[:, :tail]
    return jnp.concatenate([side(plan, "gy", msg_a[j], msg_b[j], high), ends], axis=1)


def thrice(value):
    top, low = halves(value)
    return jnp.concatenate([top, low, top], axis=0)


def fold(value, nz):
    rows, tail = value.shape[0], value.shape[1] - nz
    ends = jnp.concatenate(
        [value[k : k + 8, nz:] for k in range(0, rows, 8)]
        + [jnp.zeros((8, nz - rows // 8 * tail), F32)],
        axis=1,
    )
    return jnp.concatenate([value[:, :nz], ends], axis=0)


def unfold(value, tail):
    rows = value.shape[0] - 8
    ends = jnp.concatenate(
        [value[rows:, k * tail : (k + 1) * tail] for k in range(rows // 8)], axis=0
    )
    return jnp.concatenate([value[:rows], ends], axis=1)


def y_modes(plan, spec, ya, yb, basis, i, j, count):
    low = wide_rows(plan, ya, yb, j, count, False)
    top = wide_rows(plan, ya, yb, j, count, True)
    return mxu(basis[...], thrice(jnp.concatenate([low, spec[i], top], axis=0)))


def y_edge_kernel(plan, spec, ya, yb, basis, factors, order, edge, xa, xb):
    nx = plan.nx
    wide = INTERSECTION

    def layer(i, carry):
        k = jnp.where(i < wide, i, nx - 2 * wide + i)
        edge[i] = y_modes(plan, spec, ya, yb, basis, k, i, 2 * wide)
        return carry

    lax.fori_loop(0, 2 * wide, layer, 0, unroll=16)
    low = jnp.zeros(edge.shape[1:], F32)
    top = low
    for k in range(wide):
        low = (edge[wide - 1 - k] + low) * factors[k]
        top = (edge[wide + k] + top) * factors[k]
    for which, out in ((0, xa), (1, xb)):
        out[...] = fold(jnp.where(plan.high("gx", which)[0], top, low), plan.nz)


def y_mid_kernel(plan, spec, ya, yb, basis, factors, edge, zed):
    nx = plan.nx
    wide = INTERSECTION

    def layer(i, carry):
        zed[i] = y_modes(plan, spec, ya, yb, basis, i, i - wide, nx - 2 * wide)
        return carry

    lax.fori_loop(wide, nx - wide, layer, 0, unroll=8)

    def outer(k, carry):
        low, top = carry
        c = factors[wide + k]
        low = (edge[k] + low) * c
        top = (edge[2 * wide - 1 - k] + top) * c
        zed[k] = low
        zed[nx - 1 - k] = top
        return low, top

    def inner(k, carry):
        low, top = carry
        c = factors[wide + k]
        low = (zed[k] + low) * c
        top = (zed[nx - 1 - k] + top) * c
        zed[k] = low
        zed[nx - 1 - k] = top
        return low, top

    zero = jnp.zeros(edge.shape[1:], F32)
    carry = lax.fori_loop(0, wide, outer, (zero, zero), unroll=2)
    lax.fori_loop(wide, nx // 2, inner, carry, unroll=2)


def solve_kernel(
    plan, zed, xa, xb, factors, reach, middle, basis_y, basis_z, total, fa, fb, order, direction, *rest
):
    (dxa, dxb, dya, dyb), z_outs, (work, tile) = rest[:4], rest[4:-2], rest[-2:]
    nx, ny, nz = plan.nx, plan.ny, plan.nz
    wide = INTERSECTION
    half = nx // 2
    low_in = unfold(side(plan, "gx", xa[...], xb[...], False), 2 * wide)
    top_in = unfold(side(plan, "gx", xa[...], xb[...], True), 2 * wide)
    low = zed[half - 1] + reach[half - 1] * low_in
    top = zed[half] + reach[half - 1] * top_in
    c, mid = factors[wide + half - 1], middle[...]
    low, top = (low + c * top) * mid, (top + c * low) * mid

    def put(i, value):
        work[pl.ds(i * ny, ny), :] = mxu(basis_y[...], thrice(value))

    put(half - 1, low)
    put(half, top)

    def outward(k, carry):
        low, top = carry
        i = half - 2 - k
        c = factors[wide + i]
        far = reach[i]
        low = (zed[i] + far * low_in) + c * low
        top = (zed[nx - 1 - i] + far * top_in) + c * top
        put(i, low)
        put(nx - 1 - i, top)
        return low, top

    lax.fori_loop(0, half - 1, outward, (low, top), unroll=15)
    mean = jnp.sum(jnp.sum(total[...], axis=0, keepdims=True), axis=1, keepdims=True) / (
        nx * ny * nz
    )
    inverse = 1.0 / mean
    group = 128 // ny
    base_top, base_low = basis_z[0], basis_z[1]

    def lift(r, carry):
        high, rest_ = halves(work[pl.ds(r * 128, 128), :])
        value = mxu(high, base_top) + (mxu(rest_, base_top) + mxu(high, base_low))
        value = value * inverse
        direction[pl.ds(r * group, group)] = value.reshape(group, ny, nz)
        for q in plan.z_msgs:
            moved = pltpu.roll(value, r + plan.high("gz", q)[0].astype(jnp.int32), 1)
            tile[q] = jnp.where(lanes_of((128, nz)) == r, moved, tile[q])
        return carry

    lax.fori_loop(0, nx // group, lift, 0, unroll=8)
    pack_x(plan, direction, dxa.at[0], dxb.at[0])
    dxa[1] = fa[...]
    dxb[1] = fb[...]
    pack_y(plan, direction, dya, dyb)
    tile_out(plan, tile, z_outs)


def image_kernel(
    plan, n_dev, direction, diag, full, tx, ty_low, ty_top, tz_low, tz_top, xa, xb, ya, yb, *rest
):
    n_msg = len(plan.z_msgs)
    got = rest[:n_msg]
    image, sums, gx, gy_low, gy_top, gz_low, gz_top, hy = rest[n_msg : n_msg + 8]
    hz = rest[n_msg + 8 :]
    nx, ny, nz = plan.nx, plan.ny, plan.nz
    spread(plan, got, hz)
    hy[0] = side(plan, "gy", ya[...], yb[...], False)
    hy[1] = side(plan, "gy", ya[...], yb[...], True)
    lane = lanes_of((ny, nz))

    def layer(i, carry):
        d_last, im_last, rd, da = carry
        d = direction[i]
        flux = tx[i] * (d_last - d)
        gx[i] = flux
        y_last = from_above(d, hy[0, pl.ds(i, 1), :])
        y_next = from_below(d, hy[1, pl.ds(i, 1), :])
        cells = pl.ds(i * ny, ny)
        z_last = jnp.where(lane == 0, hz[0][cells, :], ahead(d, 1))
        z_next = jnp.where(lane == nz - 1, hz[-1][cells, :], back(d, 1))
        im = diag[i] * d - flux
        for ref, g, sign in (
            (gy_low, ty_low[i] * (y_last - d), -1),
            (gy_top, ty_top[i] * (d - y_next), 1),
            (gz_low, tz_low[i] * (z_last - d), -1),
            (gz_top, tz_top[i] * (d - z_next), 1),
        ):
            ref[i] = g
            im = im + g if sign > 0 else im - g
        im_last = im_last + flux
        image[jnp.maximum(i - 1, 0)] = im_last
        rd = rd + full[i] * d
        da = da + jnp.where(i > 0, d_last, 0.0) * im_last
        return d, im, rd, da

    zero = jnp.zeros((ny, nz), F32)
    low = side(plan, "gx", xa[0], xb[0], False)
    top = side(plan, "gx", xa[0], xb[0], True)
    d, im, rd, da = lax.fori_loop(0, nx, layer, (low, zero, zero, zero), unroll=16)
    flux = tx[nx] * (d - top)
    gx[nx] = flux
    im = im + flux
    image[nx - 1] = im
    da = da + d * im
    lane = lanes_of((n_dev, 128))
    sums[...] = jnp.where(lane < 64, jnp.sum(rd), jnp.sum(da))


def upwind(g, low, high):
    return g * jnp.where(g > 0.0, low, high)


def sweep(plan, refs, x_low, x_top, hy, z_at, done):
    nx, ny, nz = plan.nx, plan.ny, plan.nz
    (now, frac, coef, rate, anchor, gx, gy_low, gy_top, gz_low, gz_top, outflow) = refs
    lane = lanes_of((ny, nz))

    def layer(i, carry):
        f, flow = carry
        f_next = jnp.where(i == nx - 1, x_top, frac[jnp.minimum(i + 1, nx - 1)])
        s, c = now[i], coef[i]
        flow_next = upwind(gx[i + 1], f, f_next)
        y_last = from_above(f, hy[0, pl.ds(i, 1), :])
        y_next = from_below(f, hy[1, pl.ds(i, 1), :])
        z_low, z_top = z_at(i)
        z_last = jnp.where(lane == 0, z_low, ahead(f, 1))
        z_next = jnp.where(lane == nz - 1, z_top, back(f, 1))
        bal = (
            (flow_next - flow)
            + (upwind(gy_top[i], f, y_next) - upwind(gy_low[i], y_last, f))
            + (upwind(gz_top[i], f, z_next) - upwind(gz_low[i], z_last, f))
            + (rate[i] * s - anchor[i])
        )
        rest = 1.0 - s
        part = c * rest
        den = s * s + part * rest
        square = den * den
        s = s - bal * square / (rate[i] * square + outflow[i] * jnp.abs(part * s))
        done(i, s, c)
        return f_next, flow_next

    f0 = frac[0]
    lax.fori_loop(0, nx, layer, (f0, upwind(gx[0], x_low, f0)), unroll=16)


def keep(plan, new, new_frac, tile):
    def done(i, s, c):
        new[i] = s
        water, rest = s * s, 1.0 - s
        f = water / (water + c * rest * rest)
        new_frac[i] = f
        for q in plan.z_msgs:
            tile_put(plan, tile, i, q, f)

    return done


def pack_all(plan, ref, tile, outs):
    xa, xb, ya, yb = outs[:4]
    pack_x(plan, ref, xa, xb)
    pack_y(plan, ref, ya, yb)
    tile_out(plan, tile, outs[4:])


def step_of(sums):
    both = jnp.sum(sums[...], axis=0, keepdims=True)
    return both[:, 0:1] / both[:, 64:65]


def write_out(plan, i, ref, out, sem):
    size = plan.nx // CHUNKS

    @pl.when(i % size == size - 1)
    def _():
        c = i // size
        cut = pl.ds(c * size, size)
        pltpu.make_async_copy(ref.at[cut], out.at[cut], sem.at[c]).start()


def write_end(plan, ref, out, sem):
    size = plan.nx // CHUNKS
    for c in range(CHUNKS):
        cut = pl.ds(c * size, size)
        pltpu.make_async_copy(ref.at[cut], out.at[cut], sem.at[c]).wait()


def output_kernel(plan, sums, press, direction, full, image, p_out, r_out, token, p_new, r_new, p_sem, r_sem):
    step = step_of(sums)

    def layer(i, carry):
        p_new[i] = press[i] + step * direction[i]
        write_out(plan, i, p_new, p_out, p_sem)
        r_new[i] = full[i] - step * image[i]
        write_out(plan, i, r_new, r_out, r_sem)
        return carry

    lax.fori_loop(0, plan.nx, layer, 0, unroll=4)
    token[...] = jnp.zeros(token.shape, F32)
    write_end(plan, p_new, p_out, p_sem)
    write_end(plan, r_new, r_out, r_sem)


def step_kernel(plan, *refs):
    n_msg = len(plan.z_msgs)
    sums, still, move = refs[0], refs[1:6], refs[6:11]
    (sat, frac, coef, inject, square, pull, push, xa, xb, hy) = refs[11:21]
    fz = refs[21 : 21 + n_msg]
    outs = refs[21 + n_msg :]
    (s_new, f_new, gx, gy_low, gy_top, gz_low, gz_top, outflow) = outs[:8]
    packs = outs[8 : 12 + n_msg]
    tile = outs[-1]
    nx, ny, nz = plan.nx, plan.ny, plan.nz
    step = step_of(sums)
    lane = lanes_of((ny, nz))
    done = keep(plan, s_new, f_new, tile)
    x_low, x_top = (side(plan, "gx", xa[1], xb[1], high) for high in (False, True))

    def flux(k, i):
        return still[k][i] + step * move[k][i]

    def layer(i, carry):
        f, g, flow = carry
        f_next = jnp.where(i == nx - 1, x_top, frac[jnp.minimum(i + 1, nx - 1)])
        g_next = flux(0, i + 1)
        gx[i + 1] = g_next
        flow_next = upwind(g_next, f, f_next)
        out = jnp.maximum(g_next, 0.0) - jnp.minimum(g, 0.0)
        bal = flow_next - flow - inject[i]
        cells = pl.ds(i * ny, ny)
        y_last = from_above(f, hy[0, 1, pl.ds(i, 1), :])
        y_next = from_below(f, hy[1, 1, pl.ds(i, 1), :])
        z_last = jnp.where(lane == 0, fz[0][cells, :], ahead(f, 1))
        z_next = jnp.where(lane == nz - 1, fz[-1][cells, :], back(f, 1))
        for k, ref, other, low in (
            (1, gy_low, y_last, True),
            (2, gy_top, y_next, False),
            (3, gz_low, z_last, True),
            (4, gz_top, z_next, False),
        ):
            value = flux(k, i)
            ref[i] = value
            if low:
                out = out - jnp.minimum(value, 0.0)
                bal = bal - upwind(value, other, f)
            else:
                out = out + jnp.maximum(value, 0.0)
                bal = bal + upwind(value, f, other)
        outflow[i] = out + out
        done(i, sat[i] - bal * square[i] / (pull[i] + out * push[i]), coef[i])
        return f_next, g_next, flow_next

    f0, g0 = frac[0], flux(0, 0)
    gx[0] = g0
    lax.fori_loop(0, nx, layer, (f0, g0, upwind(g0, x_low, f0)), unroll=16)
    pack_all(plan, f_new, tile, packs)


def later_kernel(plan, last_sweep, *refs):
    n_msg = len(plan.z_msgs)
    fields = refs[:11]
    xa, xb, ya, yb = refs[11:15]
    got = refs[15 : 15 + n_msg]
    rest = refs[16 + n_msg :]
    if last_sweep:
        out, new, sem, fh, *hz = rest

        def done(i, s, c):
            new[i] = s
            write_out(plan, i, new, out, sem)
    else:
        new, new_frac = rest[:2]
        packs = rest[2 : 6 + n_msg]
        tile, fh, *hz = rest[6 + n_msg :]
        done = keep(plan, new, new_frac, tile)
    spread(plan, got, hz)
    fh[0] = side(plan, "gy", ya[...], yb[...], False)
    fh[1] = side(plan, "gy", ya[...], yb[...], True)

    def z_at(i):
        cells = pl.ds(i * plan.ny, plan.ny)
        return hz[0][cells, :], hz[-1][cells, :]

    sweep(
        plan, fields,
        side(plan, "gx", xa[...], xb[...], False), side(plan, "gx", xa[...], xb[...], True),
        fh, z_at, done,
    )
    if last_sweep:
        write_end(plan, new, out, sem)
    else:
        pack_all(plan, new_frac, tile, packs)


def per_device(
    counts, pressure, source, saturation, permeability, compress, porosity, rock_type, well_mask, oil_factor
):
    nx, ny, nz = pressure.shape
    wide = INTERSECTION
    plan = Plan(nx, ny, nz, counts)
    n_msg = len(plan.z_msgs)
    n_dev = counts["gx"] * counts["gy"] * counts["gz"]
    cells = nx * ny
    my, mz = ny + 2 * wide, nz + 2 * wide
    table_y, eigen_y = sine_basis(my)
    table_z, eigen_z = sine_basis(mz)
    factors, reach, middle = sweep_factors(wide + nx // 2, wide, eigen_y, eigen_z)
    const = lambda v: jnp.asarray(v, F32)
    factors, reach, middle = const(factors), const(reach), const(middle)
    rim = np.zeros((2, MSG_ROWS, mz))
    rim[0, :wide] = table_z[:wide]
    rim[0, wide] = table_z[wide]
    rim[1, :wide] = table_z[mz - wide :]
    rim[1, wide] = table_z[mz - wide - 1]

    def parts(v):
        v = np.asarray(v, np.float32)
        top = v.astype(jnp.bfloat16)
        return top, (v - top.astype(np.float32)).astype(jnp.bfloat16)

    def left(v):
        top, low = parts(v)
        return jnp.asarray(np.concatenate([top, top, low], axis=1))

    def right(v):
        top, low = parts(v)
        return jnp.asarray(np.concatenate([top, top, low], axis=0))

    rims = [jnp.concatenate([right(v)], axis=0).astype(F32) for v in rim]

    def send(value, axis, which):
        return lax.ppermute(value, axis, plan.perm(axis, which))

    def swap(axis, a, b):
        return send(a, axis, 0), send(b, axis, 1)

    def swap_z(msgs):
        return [send(v, "gz", q) for q, v in zip(plan.z_msgs, msgs)]

    full_shape = (nx, ny, nz)
    x_face, y_face, z_face = (ny, nz), (nx, nz), (cells // 128, 128)
    face_shapes = [x_face, x_face, y_face, y_face] + [z_face] * n_msg
    tile = (2, 128, nz)
    spreads = [(cells, 128)] * n_msg
    dma = pltpu.SemaphoreType.DMA

    def exchange(packs):
        z = swap_z(packs[4:])
        y = swap("gy", packs[2], packs[3])
        x = swap("gx", packs[0], packs[1])
        return [*x, *y, *z]

    press, sat, mob, coef, frac, xa, xb, ya, yb, fa, fb, total = call(
        functools.partial(mobility_kernel, plan),
        [full_shape] * 5 + [(2,) + x_face] * 2 + [(3,) + y_face] * 2 + [x_face] * 3,
        (pressure, saturation, permeability, rock_type, oil_factor),
        hbm=(0, 1, 2, 3, 4),
        scratch=[full_shape, pltpu.VMEM(full_shape, jnp.int32),
                 pltpu.SMEM(oil_factor.shape, F32), dma((CHUNKS, 4)), dma],
    )
    ya, yb = swap("gy", ya, yb)
    xa, xb = swap("gx", xa, xb)
    res, tx, ty, tz, diag, *comps = call(
        functools.partial(inner_kernel, plan),
        [full_shape] * 5 + [(cells, nz)] * n_msg,
        (press, mob, frac, source, compress, well_mask),
    )
    res, *sent = call(
        functools.partial(rim_kernel, plan),
        [full_shape] + [((wide + 3) * cells // 128, 128)] * n_msg,
        (res, press, mob, xa, xb, ya, yb, *comps),
        aliases={0: 0},
    )
    got = swap_z(sent)
    tx, ty_low, ty_top, gx, gy_low, gy_top, hy, rate, inject, anchor, square, pull, push = call(
        functools.partial(faces_xy_kernel, plan),
        [(nx + 1, ny, nz)] + [full_shape] * 2 + [(nx + 1, ny, nz)] + [full_shape] * 2
        + [(2, 2) + y_face] + [full_shape] * 6,
        (mob, press, sat, coef, porosity, well_mask, tx, ty, xa, xb, ya, yb),
        scratch=[(2,) + y_face],
    )
    slabs = [
        (len(v) + len(v) * 2 * wide // 128, wide, nz) for v in y_parts(plan) for _ in (0, 1)
    ]
    spec, *slab = call(
        functools.partial(z_kernel, plan, n_msg),
        [(nx, ny, mz)] + slabs,
        (res, right(table_z[wide : wide + nz]), *rims, hy, *sent, *got),
    )
    edge_slab = swap("gy", *slab[:2])
    mid_slab = swap("gy", *slab[2:])
    full, hz, *fz = call(
        functools.partial(residual_kernel, plan, n_msg),
        [full_shape] + [(cells, 128)] + spreads,
        (res, *sent, *got),
    )
    edge, ma, mb = call(
        functools.partial(y_edge_kernel, plan),
        [(2 * wide, my, mz), (my + 8, nz), (my + 8, nz)],
        (spec, *edge_slab, left(table_y), factors, full),
    )
    ma, mb = swap("gx", ma, mb)
    (zed,) = call(
        functools.partial(y_mid_kernel, plan),
        [(nx, my, mz)],
        (spec, *mid_slab, left(table_y), factors, edge),
    )
    tz_low, tz_top, gz_low, gz_top = call(
        functools.partial(faces_z_kernel, plan, n_msg),
        [full_shape] * 4,
        (press, tz, hz, edge),
    )
    direction, *packs = call(
        functools.partial(solve_kernel, plan),
        [full_shape] + [(2,) + x_face] * 2 + face_shapes[2:],
        (zed, ma, mb, factors, reach, middle, left(table_y[wide : wide + ny]),
         jnp.asarray(np.stack(parts(table_z[:, wide : wide + nz]))), total, fa, fb, gz_low),
        scratch=[(cells, mz), tile],
    )
    dhalo = exchange(packs)
    image, sums, *moves = call(
        functools.partial(image_kernel, plan, n_dev),
        [full_shape, (n_dev, 128), (nx + 1, ny, nz)] + [full_shape] * 4,
        (direction, diag, full, tx, ty_low, ty_top, tz_low, tz_top, *dhalo),
        scratch=[(2,) + y_face] + spreads,
    )
    sums = lax.all_to_all(sums, AXES, 0, 0, tiled=True)
    outs = call(
        functools.partial(step_kernel, plan),
        [full_shape] * 2 + [(nx + 1, ny, nz)] + [full_shape] * 5 + face_shapes,
        (sums, gx, gy_low, gy_top, gz_low, gz_top, *moves,
         sat, frac, coef, inject, square, pull, push, *dhalo[:2], hy, *fz),
        scratch=[tile],
        limit=40,
    )
    current, frac, *flows = outs[:8]
    packs = outs[8:]
    p_new, r_new, token = call(
        functools.partial(output_kernel, plan),
        [full_shape] * 2 + [(8, 128)],
        (sums, press, direction, full, image),
        hbm_out=(0, 1),
        scratch=[full_shape] * 2 + [dma((CHUNKS,))] * 2,
    )
    for sweep_index in range(1, NEWTON):
        halo = exchange(packs)
        last_sweep = sweep_index == NEWTON - 1
        outs = call(
            functools.partial(later_kernel, plan, last_sweep),
            [full_shape] if last_sweep else [full_shape] * 2 + face_shapes,
            (current, frac, coef, rate, anchor, *flows, *halo, token),
            scratch=([full_shape, dma((CHUNKS,))] if last_sweep else [tile])
            + [(2,) + y_face] + spreads,
            hbm_out=(0,) if last_sweep else (),
        )
        current = outs[0]
        if not last_sweep:
            frac, packs = outs[1], outs[2:]
    return p_new, r_new, current


def solution(mesh):
    spec = P(*AXES)

    def body(*args):
        return per_device(dict(mesh.shape), *args)

    return jax.shard_map(
        body,
        mesh=mesh,
        in_specs=(spec,) * 8 + (P(),),
        out_specs=(spec,) * 3,
        check_vma=False,
    )
```

```python
import functools
import math

import jax
import jax.numpy as jnp
import numpy as np
from jax import lax
from jax.experimental import pallas as pl
from jax.experimental.pallas import tpu as pltpu
from jax.sharding import PartitionSpec as P


INTERSECTION = 8
NEWTON = 3

WELL_INDEX = 4.0
INJECT_RATE = 2.0
TIME_STEP = 0.05

AXES = ("gx", "gy", "gz")
F32 = jnp.float32
MSG_ROWS = 16
CHUNKS = 2


def sine_basis(length):
    points = np.arange(length) + 1
    angles = np.outer(points, points) % (2 * (length + 1)) * (math.pi / (length + 1))
    table = math.sqrt(2.0 / (length + 1)) * np.sin(angles)
    eigen = 2.0 - 2.0 * np.cos(points * (math.pi / (length + 1)))
    return table, eigen


def sweep_factors(count, skip, eigen_y, eigen_z):
    shift = 2.0 + eigen_y[:, None] + eigen_z[None, :]
    factors = []
    last = np.zeros_like(shift)
    for _ in range(count):
        last = 1.0 / (shift - last)
        factors.append(last)
    factors = np.stack(factors)
    reach = np.cumprod(factors[skip:], axis=0)
    return factors, reach, 1.0 / (1.0 - last * last)


def pairs(count, periodic, parity):
    if periodic and count % 2:
        step = 1 if parity == 0 else -1
        return [(i, (i + step) % count) for i in range(count)]
    out = []
    for i in range(parity, count, 2):
        j = i + 1
        if periodic:
            j = j % count
        if j < count:
            out += [(i, j), (j, i)]
    return out


def harmonic(one, two):
    return 2.0 * one * two / (one + two)


def rows_of(shape):
    return lax.broadcasted_iota(jnp.int32, shape, 0)


def lanes_of(shape):
    return lax.broadcasted_iota(jnp.int32, shape, 1)


def back(value, axis):
    return pltpu.roll(value, value.shape[axis] - 1, axis)


def ahead(value, axis):
    return pltpu.roll(value, 1, axis)


def from_above(value, halo):
    first = rows_of((8, value.shape[1])) == 0
    fill = jnp.broadcast_to(halo, (8, value.shape[1]))
    tiles = []
    for k in range(0, value.shape[0], 8):
        turned = pltpu.roll(value[k : k + 8], 1, 0)
        tiles.append(jnp.where(first, fill, turned))
        fill = turned
    return jnp.concatenate(tiles, axis=0)


def from_below(value, halo):
    last = rows_of((8, value.shape[1])) == 7
    fill = jnp.broadcast_to(halo, (8, value.shape[1]))
    tiles = []
    for k in range(value.shape[0] - 8, -1, -8):
        turned = pltpu.roll(value[k : k + 8], 7, 0)
        tiles.append(jnp.where(last, fill, turned))
        fill = turned
    return jnp.concatenate(tiles[::-1], axis=0)


class Plan:
    def __init__(self, nx, ny, nz, counts):
        self.nx, self.ny, self.nz = nx, ny, nz
        self.counts = counts
        self.z_msgs = [q for q in (0, 1) if pairs(counts["gz"], False, q)]

    def perm(self, axis, which):
        return pairs(self.counts[axis], axis != "gz", which)

    def high(self, axis, which):
        if axis != "gz" and self.counts[axis] % 2:
            return (which == 0, which == 1)
        up = (lax.axis_index(axis) % 2) == which
        return (up, up)


def call(kernel, outs, args, scratch=(), aliases=None, hbm=(), hbm_out=(), limit=28):
    def spec(k, remote):
        return pl.BlockSpec(memory_space=pltpu.HBM if k in remote else pltpu.VMEM)

    args = [
        pltpu.with_memory_space_constraint(v, pltpu.HBM) if k in hbm else v
        for k, v in enumerate(args)
    ]
    return pl.pallas_call(
        kernel,
        out_shape=[jax.ShapeDtypeStruct(s, F32) for s in outs],
        in_specs=[spec(k, hbm) for k in range(len(args))],
        out_specs=[spec(k, hbm_out) for k in range(len(outs))],
        scratch_shapes=[pltpu.VMEM(v, F32) if isinstance(v, tuple) else v for v in scratch],
        input_output_aliases=aliases or {},
        compiler_params=pltpu.CompilerParams(vmem_limit_bytes=limit << 20),
    )(*args)


def halves(value):
    top = value.astype(jnp.bfloat16)
    return top, (value - top.astype(F32)).astype(jnp.bfloat16)


def mxu(one, two, dims=((1,), (0,))):
    return lax.dot_general(one, two, (dims, ((), ())), preferred_element_type=F32)


def side(plan, axis, ref_a, ref_b, high):
    a_high = plan.high(axis, 0)[1]
    if high:
        return jnp.where(a_high, ref_a, ref_b)
    return jnp.where(a_high, ref_b, ref_a)


def pack_x(plan, ref, out_a, out_b):
    last = plan.nx - 1
    for which, out in ((0, out_a), (1, out_b)):
        out[...] = ref[jnp.where(plan.high("gx", which)[0], last, 0)]


def pack_y(plan, ref, out_a, out_b):
    low, top = ref[:, 0, :], ref[:, plan.ny - 1, :]
    for which, out in ((0, out_a), (1, out_b)):
        out[...] = jnp.where(plan.high("gy", which)[0], top, low)


def tile_put(plan, tile, i, q, value):
    group = 128 // plan.ny
    r = i // group
    rows = pl.ds((i % group) * plan.ny, plan.ny)
    moved = pltpu.roll(value, r + plan.high("gz", q)[0].astype(jnp.int32), 1)
    tile[q, rows, :] = jnp.where(lanes_of(value.shape) == r, moved, tile[q, rows, :])


def tile_out(plan, tile, outs):
    for q, out in zip(plan.z_msgs, outs):
        out[...] = jnp.transpose(tile[q])[: out.shape[0], :]


def spread(plan, gots, outs):
    vals = [got[...] for got in gots]
    if len(vals) > 1:
        vals = list(z_sides(plan, vals))
    for val, out in zip(vals, outs):
        high = val.astype(jnp.bfloat16)
        mid, low = halves(val - high.astype(F32))
        split = jnp.concatenate([v.astype(F32) for v in (high, mid, low)], axis=0)
        blocks = val.shape[0]
        shape = (3 * blocks, blocks * 128)
        pick = (rows_of(shape) % blocks == lanes_of(shape) // 128).astype(F32).astype(jnp.bfloat16)
        wide = mxu(split.astype(jnp.bfloat16), pick, ((0,), (0,)))
        for r in range(blocks):
            out[r * 128 : (r + 1) * 128, :] = wide[:, r * 128 : (r + 1) * 128]


def stack_rows(parts):
    cells = parts[0].shape[1]
    row = rows_of((8, cells))
    out = jnp.zeros((8, cells), F32)
    for k, part in enumerate(parts):
        out = jnp.where(row == k, jnp.broadcast_to(part, (8, cells)), out)
    return out


def z_sides(plan, vals):
    low, top = jnp.zeros_like(vals[0]), jnp.zeros_like(vals[0])
    for q, val in zip(plan.z_msgs, vals):
        up = plan.high("gz", q)[1]
        low = low + jnp.where(up, 0.0, val)
        top = top + jnp.where(up, val, 0.0)
    return low, top


def mobility_kernel(
    plan, press_in, sat_in, perm_in, rock_in, oil_in,
    press, sat, mob, coef, frac, xa, xb, ya, yb, fa, fb, total, perm, rock, oil, sem, oil_sem,
):
    kinds = oil.shape[0]
    oil_move = pltpu.make_async_copy(oil_in, oil, oil_sem)
    oil_move.start()
    size = plan.nx // CHUNKS
    moves = []
    for c in range(CHUNKS):
        cut = pl.ds(c * size, size)
        for k, (src, dst) in enumerate(
            ((sat_in, sat), (rock_in, rock), (perm_in, perm), (press_in, press))
        ):
            move = pltpu.make_async_copy(src.at[cut], dst.at[cut], sem.at[c, k])
            move.start()
            moves.append(move)

    def layer(i, acc):
        s, kind = sat[i], rock[i]
        c = jnp.full(s.shape, oil[0], F32)
        for k in range(1, kinds):
            c = jnp.where(kind == k, oil[k], c)
        water, rest = s * s, 1.0 - s
        den = water + c * rest * rest
        m = perm[i] * den
        coef[i] = c
        mob[i] = m
        frac[i] = water / den
        return acc + m

    acc = jnp.zeros((plan.ny, plan.nz), F32)
    oil_move.wait()
    for c in range(CHUNKS):
        for move in moves[4 * c : 4 * c + 3]:
            move.wait()
        acc = lax.fori_loop(c * size, (c + 1) * size, layer, acc, unroll=4)
    total[...] = acc
    for c in range(CHUNKS):
        moves[4 * c + 3].wait()
    for k, ref in enumerate((press, mob)):
        pack_x(plan, ref, xa.at[k], xb.at[k])
    pack_x(plan, frac, fa, fb)
    for k, ref in enumerate((press, mob, frac)):
        pack_y(plan, ref, ya.at[k], yb.at[k])


def inner_kernel(plan, press, mob, frac, source, compress, well, res, tx, ty, tz, diag, *comps):
    shape = (plan.ny, plan.nz)
    row, lane = rows_of(shape), lanes_of(shape)

    def layer(i, carry):
        p_last, m_last, r_last = carry
        p, m = press[i], mob[i]
        t = harmonic(m_last, m)
        tx[i] = t
        flux_x = t * (p_last - p)
        t = harmonic(jnp.where(row == 0, 0.0, ahead(m, 0)), m)
        ty[i] = t
        flux_y = t * (ahead(p, 0) - p)
        t = harmonic(jnp.where(lane == 0, 0.0, ahead(m, 1)), m)
        tz[i] = t
        flux_z = t * (ahead(p, 1) - p)
        d = compress[i] + WELL_INDEX * well[i].astype(F32) * m
        diag[i] = d
        r = source[i] - d * p + flux_x + (flux_y - back(flux_y, 0)) + (flux_z - back(flux_z, 1))
        res[jnp.maximum(i - 1, 0)] = r_last - flux_x
        for q, comp in zip(plan.z_msgs, comps):
            lead = plan.high("gz", q)[0].astype(jnp.int32) + INTERSECTION
            mix = jnp.where(
                lane <= INTERSECTION, pltpu.roll(p, lead, 1), pltpu.roll(m, lead + 1, 1)
            )
            comp[pl.ds(i * plan.ny, plan.ny), :] = jnp.where(
                lane <= INTERSECTION + 1, mix, pltpu.roll(frac[i], lead + 2, 1)
            )
        return p, m, r

    zero = jnp.zeros(shape, F32)
    res[plan.nx - 1] = lax.fori_loop(0, plan.nx, layer, (zero, zero, zero), unroll=4)[2]


def rim_kernel(plan, res_in, press, mob, xa, xb, ya, yb, *rest):
    n_msg = len(plan.z_msgs)
    comps, res, z_outs = rest[:n_msg], rest[n_msg], rest[n_msg + 1 :]
    nx, ny, nz = plan.nx, plan.ny, plan.nz
    last = nx - 1
    for high, k in ((False, 0), (True, last)):
        p, m = (side(plan, "gx", xa[f], xb[f], high) for f in (0, 1))
        res[k] = res[k] + harmonic(mob[k], m) * (p - press[k])
    for high, k in ((False, 0), (True, ny - 1)):
        p, m = (side(plan, "gy", ya[f], yb[f], high) for f in (0, 1))
        res[:, k, :] = res[:, k, :] + harmonic(mob[:, k, :], m) * (p - press[:, k, :])
    wide = INTERSECTION
    group = 128 // ny
    for q, out, comp in zip(plan.z_msgs, z_outs, comps):
        up = plan.high("gz", q)[0].astype(jnp.int32)
        lane = lanes_of((128, nz))
        blocks = nx // group
        for k in range(blocks):
            value = pltpu.roll(res[k * group : (k + 1) * group].reshape(128, nz), up * wide, 1)
            value = jnp.where(lane < wide, value, comp[k * 128 : (k + 1) * 128, :])
            turned = jnp.transpose(value)
            out[k * wide : (k + 1) * wide, :] = turned[:wide]
            for f in range(3):
                row = blocks * (wide + f) + k
                out[row : row + 1, :] = turned[wide + f : wide + f + 1]


def z_flux(sent, got):
    out = []
    for own, other in zip(sent, got):
        blocks = own.shape[0] // (INTERSECTION + 3)
        first = blocks * INTERSECTION
        (p, m), (p_far, m_far, f_far) = (
            [ref[first + k * blocks : first + (k + 1) * blocks, :] for k in range(count)]
            for ref, count in ((own, 2), (other, 3))
        )
        t = harmonic(m, m_far)
        out.append((p_far, f_far, t, t * (p_far - p)))
    return out


def y_parts(plan):
    wide, nx = INTERSECTION, plan.nx
    return (
        list(range(wide)) + list(range(nx - wide, nx)),
        list(range(wide, nx - wide)),
    )


def z_kernel(plan, n_msg, res, basis, rim_low, rim_top, order, *rest):
    sent, got = rest[:n_msg], rest[n_msg : 2 * n_msg]
    spec, *outs = rest[2 * n_msg :]
    nx, ny, nz = plan.nx, plan.ny, plan.nz
    wide = INTERSECTION
    row = rows_of((wide, 128))
    fluxes = [part[3] for part in z_flux(sent, got)]
    ups = [plan.high("gz", q)[1] for q in plan.z_msgs]
    rims = [jnp.where(up, rim_top[...], rim_low[...]).astype(jnp.bfloat16) for up in ups]
    group = 128 // ny
    for k in range(nx // group):
        value = res[k * group : (k + 1) * group].reshape(128, nz)
        top, low = halves(value)
        out = mxu(jnp.concatenate([top, low, top], axis=1), basis[...])
        for up, other, flux, rim in zip(ups, got, fluxes, rims):
            flux = jnp.broadcast_to(flux[k : k + 1, :], (wide, 128))
            mix = other[k * wide : (k + 1) * wide, :]
            mix = jnp.where(row == jnp.where(up, 0, wide - 1), mix - flux, mix)
            mix = jnp.concatenate([mix, jnp.where(row == 0, flux, 0.0)], axis=0)
            out = out + mxu(thrice(mix), rim, ((0,), (0,)))
        spec[k * group : (k + 1) * group] = out.reshape(group, ny, out.shape[1])
    tail = 2 * wide
    per = 128 // tail
    for which in (0, 1):
        start = jnp.where(plan.high("gy", which)[0], ny - wide, 0)
        rows = pl.ds(pl.multiple_of(start, 8), wide)
        for layers, ref in zip(y_parts(plan), outs[which::2]):
            count = len(layers)
            for g in range(count // per):
                group = layers[g * per : (g + 1) * per]
                for j, i in enumerate(group):
                    ref[g * per + j] = spec[i, rows, :nz]
                ref[count + g] = jnp.concatenate([spec[i, rows, nz:] for i in group], axis=1)


def faces_xy_kernel(
    plan, mob, press, sat, coef, poro, well, tx_in, ty_in, xa, xb, ya, yb,
    tx, ty_low, ty_top, gx, gy_low, gy_top, hy, rate, inject, anchor, square, pull, push, ty_rim,
):
    nx, ny, nz = plan.nx, plan.ny, plan.nz
    x_low, x_top = (side(plan, "gx", xa[0], xb[0], high) for high in (False, True))
    for k, high in ((0, False), (1, True)):
        for f, field in ((0, 0), (1, 2)):
            hy[k, f] = side(plan, "gy", ya[field], yb[field], high)
    ty_rim[0] = harmonic(mob[:, 0, :], side(plan, "gy", ya[1], yb[1], False))
    ty_rim[1] = harmonic(mob[:, ny - 1, :], side(plan, "gy", ya[1], yb[1], True))
    row = rows_of((ny, nz))
    t_first = harmonic(mob[0], side(plan, "gx", xa[1], xb[1], False))

    def layer(i, p_last):
        p = press[i]
        t = jnp.where(i == 0, t_first, tx_in[i])
        tx[i] = t
        gx[i] = t * (p_last - p)
        t = ty_in[i]
        low = jnp.where(row == 0, ty_rim[0, pl.ds(i, 1), :], t)
        top = jnp.where(row == ny - 1, ty_rim[1, pl.ds(i, 1), :], back(t, 0))
        ty_low[i] = low
        ty_top[i] = top
        y_last = jnp.where(row == 0, hy[0, 0, pl.ds(i, 1), :], ahead(p, 0))
        y_next = jnp.where(row == ny - 1, hy[1, 0, pl.ds(i, 1), :], back(p, 0))
        gy_low[i] = low * (y_last - p)
        gy_top[i] = top * (p - y_next)
        speed = poro[i] / TIME_STEP
        s, c = sat[i], coef[i]
        rest = 1.0 - s
        part = c * rest
        den = s * s + part * rest
        den = den * den
        rate[i] = speed
        gain = INJECT_RATE * well[i].astype(F32)
        inject[i] = gain
        anchor[i] = speed * s + gain
        square[i] = den
        pull[i] = speed * den
        push[i] = jnp.abs(2.0 * part * s)
        return p

    p = lax.fori_loop(0, nx, layer, x_low, unroll=4)
    t = harmonic(mob[nx - 1], side(plan, "gx", xa[1], xb[1], True))
    tx[nx] = t
    gx[nx] = t * (p - x_top)


def z_ends(plan, n_msg):
    lane = lanes_of((plan.ny, plan.nz))
    low, top = lane == 0, lane == plan.nz - 1
    if n_msg == 1:
        up = plan.high("gz", plan.z_msgs[0])[1]
        low, top = low & jnp.logical_not(up), top & up
    return low, top


def residual_kernel(plan, n_msg, res, *rest):
    sent, got = rest[:n_msg], rest[n_msg : 2 * n_msg]
    full, hz, *fz = rest[2 * n_msg :]
    nx, ny, nz = plan.nx, plan.ny, plan.nz
    parts = z_flux(sent, got)
    if n_msg == 1:
        vals = list(parts[0][1:])
    else:
        vals = [v for k in (1, 2, 3) for v in z_sides(plan, [part[k] for part in parts])]
    for k in range(nx * ny // 128):
        rows = stack_rows([v[k : k + 1, :] for v in vals])
        hz[k * 128 : (k + 1) * 128, :8] = jnp.transpose(rows)
    at_low, at_top = z_ends(plan, n_msg)

    def layer(i, carry):
        cells = pl.ds(i * ny, ny)
        col = hz[cells, :8]
        in_low, in_top = (
            jnp.broadcast_to(col[:, k : k + 1], (ny, nz))
            for k in ((2, 2) if n_msg == 1 else (4, 5))
        )
        full[i] = res[i] + (jnp.where(at_low, in_low, 0.0) + jnp.where(at_top, in_top, 0.0))
        for k, out in enumerate(fz):
            out[cells, :] = jnp.broadcast_to(col[:, k : k + 1], (ny, nz))
        return carry

    lax.fori_loop(0, nx, layer, 0, unroll=8)


def faces_z_kernel(plan, n_msg, press, tz_in, hz, order, tz_low, tz_top, gz_low, gz_top):
    ny, nz = plan.ny, plan.nz
    at_low, at_top = z_ends(plan, n_msg)

    def layer(i, carry):
        t, p = tz_in[i], press[i]
        col = hz[pl.ds(i * ny, ny), :8]
        t_low, t_top, in_low, in_top = (
            jnp.broadcast_to(col[:, k : k + 1], (ny, nz))
            for k in ((1, 1, 2, 2) if n_msg == 1 else (2, 3, 4, 5))
        )
        tz_low[i] = jnp.where(at_low, t_low, t)
        tz_top[i] = jnp.where(at_top, t_top, back(t, 1))
        g = t * (ahead(p, 1) - p)
        gz_low[i] = jnp.where(at_low, in_low, g)
        gz_top[i] = jnp.where(at_top, -in_top, back(g, 1))
        return carry

    lax.fori_loop(0, plan.nx, layer, 0, unroll=8)


def wide_rows(plan, msg_a, msg_b, j, count, high):
    tail = 2 * INTERSECTION
    per = 128 // tail
    ends = side(plan, "gy", msg_a[count + j // per], msg_b[count + j // per], high)
    ends = pltpu.roll(ends, (128 - (j % per) * tail) % 128, 1)[:, :tail]
    return jnp.concatenate([side(plan, "gy", msg_a[j], msg_b[j], high), ends], axis=1)


def thrice(value):
    top, low = halves(value)
    return jnp.concatenate([top, low, top], axis=0)


def fold(value, nz):
    rows, tail = value.shape[0], value.shape[1] - nz
    ends = jnp.concatenate(
        [value[k : k + 8, nz:] for k in range(0, rows, 8)]
        + [jnp.zeros((8, nz - rows // 8 * tail), F32)],
        axis=1,
    )
    return jnp.concatenate([value[:, :nz], ends], axis=0)


def unfold(value, tail):
    rows = value.shape[0] - 8
    ends = jnp.concatenate(
        [value[rows:, k * tail : (k + 1) * tail] for k in range(rows // 8)], axis=0
    )
    return jnp.concatenate([value[:rows], ends], axis=1)


def y_modes(plan, spec, ya, yb, basis, i, j, count):
    low = wide_rows(plan, ya, yb, j, count, False)
    top = wide_rows(plan, ya, yb, j, count, True)
    return mxu(basis[...], thrice(jnp.concatenate([low, spec[i], top], axis=0)))


def y_edge_kernel(plan, spec, ya, yb, basis, factors, order, edge, xa, xb):
    nx = plan.nx
    wide = INTERSECTION

    def layer(i, carry):
        k = jnp.where(i < wide, i, nx - 2 * wide + i)
        edge[i] = y_modes(plan, spec, ya, yb, basis, k, i, 2 * wide)
        return carry

    lax.fori_loop(0, 2 * wide, layer, 0, unroll=16)
    low = jnp.zeros(edge.shape[1:], F32)
    top = low
    for k in range(wide):
        low = (edge[wide - 1 - k] + low) * factors[k]
        top = (edge[wide + k] + top) * factors[k]
    for which, out in ((0, xa), (1, xb)):
        out[...] = fold(jnp.where(plan.high("gx", which)[0], top, low), plan.nz)


def y_mid_kernel(plan, spec, ya, yb, basis, factors, edge, zed):
    nx = plan.nx
    wide = INTERSECTION

    def layer(i, carry):
        zed[i] = y_modes(plan, spec, ya, yb, basis, i, i - wide, nx - 2 * wide)
        return carry

    lax.fori_loop(wide, nx - wide, layer, 0, unroll=8)

    def outer(k, carry):
        low, top = carry
        c = factors[wide + k]
        low = (edge[k] + low) * c
        top = (edge[2 * wide - 1 - k] + top) * c
        zed[k] = low
        zed[nx - 1 - k] = top
        return low, top

    def inner(k, carry):
        low, top = carry
        c = factors[wide + k]
        low = (zed[k] + low) * c
        top = (zed[nx - 1 - k] + top) * c
        zed[k] = low
        zed[nx - 1 - k] = top
        return low, top

    zero = jnp.zeros(edge.shape[1:], F32)
    carry = lax.fori_loop(0, wide, outer, (zero, zero), unroll=2)
    lax.fori_loop(wide, nx // 2, inner, carry, unroll=2)


def solve_kernel(
    plan, zed, xa, xb, factors, reach, middle, basis_y, basis_z, total, fa, fb, order, direction, *rest
):
    (dxa, dxb, dya, dyb), z_outs, (work, tile) = rest[:4], rest[4:-2], rest[-2:]
    nx, ny, nz = plan.nx, plan.ny, plan.nz
    wide = INTERSECTION
    half = nx // 2
    low_in = unfold(side(plan, "gx", xa[...], xb[...], False), 2 * wide)
    top_in = unfold(side(plan, "gx", xa[...], xb[...], True), 2 * wide)
    low = zed[half - 1] + reach[half - 1] * low_in
    top = zed[half] + reach[half - 1] * top_in
    c, mid = factors[wide + half - 1], middle[...]
    low, top = (low + c * top) * mid, (top + c * low) * mid

    def put(i, value):
        work[pl.ds(i * ny, ny), :] = mxu(basis_y[...], thrice(value))

    put(half - 1, low)
    put(half, top)

    def outward(k, carry):
        low, top = carry
        i = half - 2 - k
        c = factors[wide + i]
        far = reach[i]
        low = (zed[i] + far * low_in) + c * low
        top = (zed[nx - 1 - i] + far * top_in) + c * top
        put(i, low)
        put(nx - 1 - i, top)
        return low, top

    lax.fori_loop(0, half - 1, outward, (low, top), unroll=15)
    mean = jnp.sum(jnp.sum(total[...], axis=0, keepdims=True), axis=1, keepdims=True) / (
        nx * ny * nz
    )
    inverse = 1.0 / mean
    group = 128 // ny
    base_top, base_low = basis_z[0], basis_z[1]

    def lift(r, carry):
        high, rest_ = halves(work[pl.ds(r * 128, 128), :])
        value = mxu(high, base_top) + (mxu(rest_, base_top) + mxu(high, base_low))
        value = value * inverse
        direction[pl.ds(r * group, group)] = value.reshape(group, ny, nz)
        for q in plan.z_msgs:
            moved = pltpu.roll(value, r + plan.high("gz", q)[0].astype(jnp.int32), 1)
            tile[q] = jnp.where(lanes_of((128, nz)) == r, moved, tile[q])
        return carry

    lax.fori_loop(0, nx // group, lift, 0, unroll=8)
    pack_x(plan, direction, dxa.at[0], dxb.at[0])
    dxa[1] = fa[...]
    dxb[1] = fb[...]
    pack_y(plan, direction, dya, dyb)
    tile_out(plan, tile, z_outs)


def image_kernel(
    plan, n_dev, direction, diag, full, tx, ty_low, ty_top, tz_low, tz_top, xa, xb, ya, yb, *rest
):
    n_msg = len(plan.z_msgs)
    got = rest[:n_msg]
    image, sums, gx, gy_low, gy_top, gz_low, gz_top, hy = rest[n_msg : n_msg + 8]
    hz = rest[n_msg + 8 :]
    nx, ny, nz = plan.nx, plan.ny, plan.nz
    spread(plan, got, hz)
    hy[0] = side(plan, "gy", ya[...], yb[...], False)
    hy[1] = side(plan, "gy", ya[...], yb[...], True)
    lane = lanes_of((ny, nz))

    def layer(i, carry):
        d_last, im_last, rd, da = carry
        d = direction[i]
        flux = tx[i] * (d_last - d)
        gx[i] = flux
        y_last = from_above(d, hy[0, pl.ds(i, 1), :])
        y_next = from_below(d, hy[1, pl.ds(i, 1), :])
        cells = pl.ds(i * ny, ny)
        z_last = jnp.where(lane == 0, hz[0][cells, :], ahead(d, 1))
        z_next = jnp.where(lane == nz - 1, hz[-1][cells, :], back(d, 1))
        im = diag[i] * d - flux
        for ref, g, sign in (
            (gy_low, ty_low[i] * (y_last - d), -1),
            (gy_top, ty_top[i] * (d - y_next), 1),
            (gz_low, tz_low[i] * (z_last - d), -1),
            (gz_top, tz_top[i] * (d - z_next), 1),
        ):
            ref[i] = g
            im = im + g if sign > 0 else im - g
        im_last = im_last + flux
        image[jnp.maximum(i - 1, 0)] = im_last
        rd = rd + full[i] * d
        da = da + jnp.where(i > 0, d_last, 0.0) * im_last
        return d, im, rd, da

    zero = jnp.zeros((ny, nz), F32)
    low = side(plan, "gx", xa[0], xb[0], False)
    top = side(plan, "gx", xa[0], xb[0], True)
    d, im, rd, da = lax.fori_loop(0, nx, layer, (low, zero, zero, zero), unroll=32)
    flux = tx[nx] * (d - top)
    gx[nx] = flux
    im = im + flux
    image[nx - 1] = im
    da = da + d * im
    lane = lanes_of((n_dev, 128))
    sums[...] = jnp.where(lane < 64, jnp.sum(rd), jnp.sum(da))


def upwind(g, low, high):
    return g * jnp.where(g > 0.0, low, high)


def sweep(plan, refs, x_low, x_top, hy, z_at, done, chunk_done=None):
    nx, ny, nz = plan.nx, plan.ny, plan.nz
    (now, frac, coef, rate, anchor, gx, gy_low, gy_top, gz_low, gz_top, outflow) = refs
    lane = lanes_of((ny, nz))

    def layer(i, carry):
        f, flow = carry
        f_next = jnp.where(i == nx - 1, x_top, frac[jnp.minimum(i + 1, nx - 1)])
        s, c = now[i], coef[i]
        flow_next = upwind(gx[i + 1], f, f_next)
        y_last = from_above(f, hy[0, pl.ds(i, 1), :])
        y_next = from_below(f, hy[1, pl.ds(i, 1), :])
        z_low, z_top = z_at(i)
        z_last = jnp.where(lane == 0, z_low, ahead(f, 1))
        z_next = jnp.where(lane == nz - 1, z_top, back(f, 1))
        bal = (
            (flow_next - flow)
            + (upwind(gy_top[i], f, y_next) - upwind(gy_low[i], y_last, f))
            + (upwind(gz_top[i], f, z_next) - upwind(gz_low[i], z_last, f))
            + (rate[i] * s - anchor[i])
        )
        rest = 1.0 - s
        part = c * rest
        den = s * s + part * rest
        square = den * den
        s = s - bal * square / (rate[i] * square + outflow[i] * jnp.abs(part * s))
        done(i, s, c)
        return f_next, flow_next

    f0 = frac[0]
    carry = (f0, upwind(gx[0], x_low, f0))
    if chunk_done is None:
        lax.fori_loop(0, nx, layer, carry, unroll=16)
    else:
        size = nx // CHUNKS
        for c in range(CHUNKS):
            carry = lax.fori_loop(c * size, (c + 1) * size, layer, carry, unroll=size)
            chunk_done(c)


def keep(plan, new, new_frac, tile):
    def done(i, s, c):
        new[i] = s
        water, rest = s * s, 1.0 - s
        f = water / (water + c * rest * rest)
        new_frac[i] = f
        for q in plan.z_msgs:
            tile_put(plan, tile, i, q, f)

    return done


def pack_all(plan, ref, tile, outs):
    xa, xb, ya, yb = outs[:4]
    pack_x(plan, ref, xa, xb)
    pack_y(plan, ref, ya, yb)
    tile_out(plan, tile, outs[4:])


def step_of(sums):
    both = jnp.sum(sums[...], axis=0, keepdims=True)
    return both[:, 0:1] / both[:, 64:65]


def write_part(plan, c, ref, out, sem):
    size = plan.nx // CHUNKS
    cut = pl.ds(c * size, size)
    return pltpu.make_async_copy(ref.at[cut], out.at[cut], sem.at[c])


def output_kernel(plan, sums, press, direction, full, image, p_out, r_out, token, p_new, r_new, p_sem, r_sem):
    step = step_of(sums)

    def layer(i, carry):
        p_new[i] = press[i] + step * direction[i]
        r_new[i] = full[i] - step * image[i]
        return carry

    size = plan.nx // CHUNKS
    pairs_out = ((p_new, p_out, p_sem), (r_new, r_out, r_sem))
    for c in range(CHUNKS):
        lax.fori_loop(c * size, (c + 1) * size, layer, 0, unroll=size)
        for refs in pairs_out:
            write_part(plan, c, *refs).start()
    token[...] = jnp.zeros(token.shape, F32)
    for c in range(CHUNKS):
        for refs in pairs_out:
            write_part(plan, c, *refs).wait()


def step_kernel(plan, *refs):
    n_msg = len(plan.z_msgs)
    sums, still, move = refs[0], refs[1:6], refs[6:11]
    (sat, frac, coef, inject, square, pull, push, xa, xb, hy) = refs[11:21]
    fz = refs[21 : 21 + n_msg]
    outs = refs[21 + n_msg :]
    (s_new, f_new, gx, gy_low, gy_top, gz_low, gz_top, outflow) = outs[:8]
    packs = outs[8 : 12 + n_msg]
    tile = outs[-1]
    nx, ny, nz = plan.nx, plan.ny, plan.nz
    step = step_of(sums)
    lane = lanes_of((ny, nz))
    done = keep(plan, s_new, f_new, tile)
    x_low, x_top = (side(plan, "gx", xa[1], xb[1], high) for high in (False, True))

    def flux(k, i):
        return still[k][i] + step * move[k][i]

    def layer(i, carry):
        f, g, flow = carry
        f_next = jnp.where(i == nx - 1, x_top, frac[jnp.minimum(i + 1, nx - 1)])
        g_next = flux(0, i + 1)
        gx[i + 1] = g_next
        flow_next = upwind(g_next, f, f_next)
        out = jnp.maximum(g_next, 0.0) - jnp.minimum(g, 0.0)
        bal = flow_next - flow - inject[i]
        cells = pl.ds(i * ny, ny)
        y_last = from_above(f, hy[0, 1, pl.ds(i, 1), :])
        y_next = from_below(f, hy[1, 1, pl.ds(i, 1), :])
        z_last = jnp.where(lane == 0, fz[0][cells, :], ahead(f, 1))
        z_next = jnp.where(lane == nz - 1, fz[-1][cells, :], back(f, 1))
        for k, ref, other, low in (
            (1, gy_low, y_last, True),
            (2, gy_top, y_next, False),
            (3, gz_low, z_last, True),
            (4, gz_top, z_next, False),
        ):
            value = flux(k, i)
            ref[i] = value
            if low:
                out = out - jnp.minimum(value, 0.0)
                bal = bal - upwind(value, other, f)
            else:
                out = out + jnp.maximum(value, 0.0)
                bal = bal + upwind(value, f, other)
        outflow[i] = out + out
        done(i, sat[i] - bal * square[i] / (pull[i] + out * push[i]), coef[i])
        return f_next, g_next, flow_next

    f0, g0 = frac[0], flux(0, 0)
    gx[0] = g0
    lax.fori_loop(0, nx, layer, (f0, g0, upwind(g0, x_low, f0)), unroll=16)
    pack_all(plan, f_new, tile, packs)


def later_kernel(plan, last_sweep, *refs):
    n_msg = len(plan.z_msgs)
    fields = refs[:11]
    xa, xb, ya, yb = refs[11:15]
    got = refs[15 : 15 + n_msg]
    rest = refs[16 + n_msg :]
    if last_sweep:
        out, new, sem, fh, *hz = rest

        def done(i, s, c):
            new[i] = s

        def chunk_done(c):
            write_part(plan, c, new, out, sem).start()
    else:
        new, new_frac = rest[:2]
        packs = rest[2 : 6 + n_msg]
        tile, fh, *hz = rest[6 + n_msg :]
        done = keep(plan, new, new_frac, tile)
        chunk_done = None
    spread(plan, got, hz)
    fh[0] = side(plan, "gy", ya[...], yb[...], False)
    fh[1] = side(plan, "gy", ya[...], yb[...], True)

    def z_at(i):
        cells = pl.ds(i * plan.ny, plan.ny)
        return hz[0][cells, :], hz[-1][cells, :]

    sweep(
        plan, fields,
        side(plan, "gx", xa[...], xb[...], False), side(plan, "gx", xa[...], xb[...], True),
        fh, z_at, done, chunk_done,
    )
    if last_sweep:
        for c in range(CHUNKS):
            write_part(plan, c, new, out, sem).wait()
    else:
        pack_all(plan, new_frac, tile, packs)


def per_device(
    counts, pressure, source, saturation, permeability, compress, porosity, rock_type, well_mask, oil_factor
):
    nx, ny, nz = pressure.shape
    wide = INTERSECTION
    plan = Plan(nx, ny, nz, counts)
    n_msg = len(plan.z_msgs)
    n_dev = counts["gx"] * counts["gy"] * counts["gz"]
    cells = nx * ny
    my, mz = ny + 2 * wide, nz + 2 * wide
    table_y, eigen_y = sine_basis(my)
    table_z, eigen_z = sine_basis(mz)
    factors, reach, middle = sweep_factors(wide + nx // 2, wide, eigen_y, eigen_z)
    const = lambda v: jnp.asarray(v, F32)
    factors, reach, middle = const(factors), const(reach), const(middle)
    rim = np.zeros((2, MSG_ROWS, mz))
    rim[0, :wide] = table_z[:wide]
    rim[0, wide] = table_z[wide]
    rim[1, :wide] = table_z[mz - wide :]
    rim[1, wide] = table_z[mz - wide - 1]

    def parts(v):
        v = np.asarray(v, np.float32)
        top = v.astype(jnp.bfloat16)
        return top, (v - top.astype(np.float32)).astype(jnp.bfloat16)

    def left(v):
        top, low = parts(v)
        return jnp.asarray(np.concatenate([top, top, low], axis=1))

    def right(v):
        top, low = parts(v)
        return jnp.asarray(np.concatenate([top, top, low], axis=0))

    rims = [jnp.concatenate([right(v)], axis=0).astype(F32) for v in rim]

    def send(value, axis, which):
        return lax.ppermute(value, axis, plan.perm(axis, which))

    def swap(axis, a, b):
        return send(a, axis, 0), send(b, axis, 1)

    def swap_z(msgs):
        return [send(v, "gz", q) for q, v in zip(plan.z_msgs, msgs)]

    full_shape = (nx, ny, nz)
    x_face, y_face, z_face = (ny, nz), (nx, nz), (cells // 128, 128)
    face_shapes = [x_face, x_face, y_face, y_face] + [z_face] * n_msg
    tile = (2, 128, nz)
    spreads = [(cells, 128)] * n_msg
    dma = pltpu.SemaphoreType.DMA

    def exchange(packs):
        z = swap_z(packs[4:])
        y = swap("gy", packs[2], packs[3])
        x = swap("gx", packs[0], packs[1])
        return [*x, *y, *z]

    press, sat, mob, coef, frac, xa, xb, ya, yb, fa, fb, total = call(
        functools.partial(mobility_kernel, plan),
        [full_shape] * 5 + [(2,) + x_face] * 2 + [(3,) + y_face] * 2 + [x_face] * 3,
        (pressure, saturation, permeability, rock_type, oil_factor),
        hbm=(0, 1, 2, 3, 4),
        scratch=[full_shape, pltpu.VMEM(full_shape, jnp.int32),
                 pltpu.SMEM(oil_factor.shape, F32), dma((CHUNKS, 4)), dma],
    )
    ya, yb = swap("gy", ya, yb)
    xa, xb = swap("gx", xa, xb)
    res, tx, ty, tz, diag, *comps = call(
        functools.partial(inner_kernel, plan),
        [full_shape] * 5 + [(cells, nz)] * n_msg,
        (press, mob, frac, source, compress, well_mask),
    )
    res, *sent = call(
        functools.partial(rim_kernel, plan),
        [full_shape] + [((wide + 3) * cells // 128, 128)] * n_msg,
        (res, press, mob, xa, xb, ya, yb, *comps),
        aliases={0: 0},
    )
    got = swap_z(sent)
    tx, ty_low, ty_top, gx, gy_low, gy_top, hy, rate, inject, anchor, square, pull, push = call(
        functools.partial(faces_xy_kernel, plan),
        [(nx + 1, ny, nz)] + [full_shape] * 2 + [(nx + 1, ny, nz)] + [full_shape] * 2
        + [(2, 2) + y_face] + [full_shape] * 6,
        (mob, press, sat, coef, porosity, well_mask, tx, ty, xa, xb, ya, yb),
        scratch=[(2,) + y_face],
    )
    slabs = [
        (len(v) + len(v) * 2 * wide // 128, wide, nz) for v in y_parts(plan) for _ in (0, 1)
    ]
    spec, *slab = call(
        functools.partial(z_kernel, plan, n_msg),
        [(nx, ny, mz)] + slabs,
        (res, right(table_z[wide : wide + nz]), *rims, hy, *sent, *got),
    )
    edge_slab = swap("gy", *slab[:2])
    mid_slab = swap("gy", *slab[2:])
    full, hz, *fz = call(
        functools.partial(residual_kernel, plan, n_msg),
        [full_shape] + [(cells, 128)] + spreads,
        (res, *sent, *got),
    )
    edge, ma, mb = call(
        functools.partial(y_edge_kernel, plan),
        [(2 * wide, my, mz), (my + 8, nz), (my + 8, nz)],
        (spec, *edge_slab, left(table_y), factors, full),
    )
    ma, mb = swap("gx", ma, mb)
    (zed,) = call(
        functools.partial(y_mid_kernel, plan),
        [(nx, my, mz)],
        (spec, *mid_slab, left(table_y), factors, edge),
    )
    tz_low, tz_top, gz_low, gz_top = call(
        functools.partial(faces_z_kernel, plan, n_msg),
        [full_shape] * 4,
        (press, tz, hz, edge),
    )
    direction, *packs = call(
        functools.partial(solve_kernel, plan),
        [full_shape] + [(2,) + x_face] * 2 + face_shapes[2:],
        (zed, ma, mb, factors, reach, middle, left(table_y[wide : wide + ny]),
         jnp.asarray(np.stack(parts(table_z[:, wide : wide + nz]))), total, fa, fb, gz_low),
        scratch=[(cells, mz), tile],
    )
    dhalo = exchange(packs)
    image, sums, *moves = call(
        functools.partial(image_kernel, plan, n_dev),
        [full_shape, (n_dev, 128), (nx + 1, ny, nz)] + [full_shape] * 4,
        (direction, diag, full, tx, ty_low, ty_top, tz_low, tz_top, *dhalo),
        scratch=[(2,) + y_face] + spreads,
    )
    sums = lax.all_to_all(sums, AXES, 0, 0, tiled=True)
    outs = call(
        functools.partial(step_kernel, plan),
        [full_shape] * 2 + [(nx + 1, ny, nz)] + [full_shape] * 5 + face_shapes,
        (sums, gx, gy_low, gy_top, gz_low, gz_top, *moves,
         sat, frac, coef, inject, square, pull, push, *dhalo[:2], hy, *fz),
        scratch=[tile],
        limit=40,
    )
    current, frac, *flows = outs[:8]
    packs = outs[8:]
    p_new, r_new, token = call(
        functools.partial(output_kernel, plan),
        [full_shape] * 2 + [(8, 128)],
        (sums, press, direction, full, image),
        hbm_out=(0, 1),
        scratch=[full_shape] * 2 + [dma((CHUNKS,))] * 2,
    )
    for sweep_index in range(1, NEWTON):
        halo = exchange(packs)
        last_sweep = sweep_index == NEWTON - 1
        outs = call(
            functools.partial(later_kernel, plan, last_sweep),
            [full_shape] if last_sweep else [full_shape] * 2 + face_shapes,
            (current, frac, coef, rate, anchor, *flows, *halo, token),
            scratch=([full_shape, dma((CHUNKS,))] if last_sweep else [tile])
            + [(2,) + y_face] + spreads,
            hbm_out=(0,) if last_sweep else (),
        )
        current = outs[0]
        if not last_sweep:
            frac, packs = outs[1], outs[2:]
    return p_new, r_new, current


def solution(mesh):
    spec = P(*AXES)

    def body(*args):
        return per_device(dict(mesh.shape), *args)

    return jax.shard_map(
        body,
        mesh=mesh,
        in_specs=(spec,) * 8 + (P(),),
        out_specs=(spec,) * 3,
        check_vma=False,
    )
```
